256 devices in a mesh: ctx: 8 (over y, x_hi), chan: 32 (over x_lo, z, core).
Axes of the slice: x: 4 (x_hi: 2, x_lo: 2; x = x_hi * 2 + x_lo), y: 4, z: 8, core: 2. Of those that a mesh axis runs over, the one named last changes fastest.
Arguments:
- token_ids: int32 [2048], P('ctx'), may hold values from 0 to 511
- embed_table: bfloat16 [512, 8192], P(None, 'chan'), may hold values from -6 to 6
- in_weight: bfloat16 [8192, 3, 8192], P(None, None, 'chan'), may hold values from -0.0625 to 0.0625
- feat_taps: float32 [3, 3, 8192], P(None, None, 'chan'), may hold values from -3.5 to 3.5
- modal_rates: float32 [16, 512], P(None, 'chan'), may hold values from 4.8828126e-05 to 0.03
- modal_residues: float32 [16, 512], P(None, 'chan'), may hold values from -1.5 to 1.5
- out_grad: bfloat16 [2048, 8192], P('ctx', 'chan'), may hold values from -6 to 6
Outputs:
- output: bfloat16 [2048, 8192], P('ctx', 'chan')
- grad_tokens: bfloat16 [2048, 8192], P('ctx', 'chan')
The draws below stay inside these ranges and needn't reach their ends.
All inputs are finite; a program needn't handle non-finite values.
Results may differ from the reference program's by a relative error of at most 0.034.
Values may be sent and summed in bfloat16 or wider, within the bound.
No kernel may reach another device: no remote copies, remote signals or barrier semaphores. Data moves between devices by JAX's collectives and lax.ppermute only.
A program may use at most 128 MiB of HBM per device.

```python
import math
import jax
import jax.numpy as jnp
import numpy as np
from jax import lax

D = 8192
VOCAB = 512
GROUP = 16
ORDER = 16
FEAT = 3
TOKENS = 2048
GROUPS = 512
N_CHAN = 32


def place_ends(values, own_key, least, high):
    dims = values.shape
    place = [jax.random.randint(jax.random.fold_in(own_key, axis), (), 0, dims[axis]) for axis in range(len(dims))]
    values = values.at[tuple(place)].set(least)
    longest = dims.index(max(dims))
    place[longest] = (place[longest] + 1) % dims[longest]
    return values.at[tuple(place)].set(high)


def steps_of(stream_key, extent, shards, least, top_value):
    gain, own = 1.0, jax.random.fold_in(stream_key, 6)
    for position, shards_of in shards:
        heights = jnp.exp(jax.random.uniform(jax.random.fold_in(own, position), (shards_of,), jnp.float32, least / len(shards), top_value / len(shards)))
        gain = gain * jnp.repeat(heights, extent[position] // shards_of).reshape([-1 if axis == position else 1 for axis in range(len(extent))])
    return gain


def cumulative_ranks(count, slope):
    weights = [(1 << 20) // math.isqrt(rank ** slope) + 1 for rank in range(1, count + 1)]
    scale = 1 + sum(weights) // (1 << 30)
    return np.cumsum(np.array([max(1, weight // scale) for weight in weights]))


def ranked_ids(own_key, extent, count, skew):
    table = cumulative_ranks(count, skew)
    pick = jax.random.randint(jax.random.fold_in(own_key, 1), extent, 0, int(table[count - 1]))
    standing = jnp.searchsorted(jnp.asarray(table, jnp.int32), pick, side="right")
    return jax.random.permutation(jax.random.fold_in(own_key, 2), count)[standing].astype(jnp.int32)


def bell_draw(stream_key, dims, spread, bound, split=(), dtype=jnp.bfloat16):
    array = jax.random.normal(stream_key, dims, jnp.float32) * spread
    if len(split) > 0:
        array = steps_of(stream_key, dims, split, -0.22, 0.18) * array
    return jnp.clip(array, min=-bound, max=bound).astype(dtype)


def setup_inputs(seed: int = 0) -> dict:
    key_of = jax.random.split(jax.random.key(seed), 8)
    token_ids = place_ends(ranked_ids(key_of[0], (TOKENS,), VOCAB, 2), jax.random.fold_in(key_of[0], 3), 0, VOCAB - 1).astype(jnp.int32)
    embed_table = bell_draw(key_of[1], (VOCAB, D), 1.0, 6.0, ((1, 32),))
    in_weight = bell_draw(key_of[2], (D, 3, D), D ** -0.5, 0.0625, ((2, 32),))
    feat_taps = bell_draw(key_of[3], (3, FEAT, D), FEAT ** -0.5, 3.5, ((2, 32),), jnp.float32)
    modal_rates = jnp.clip(jnp.exp(math.log(0.03) - 6.420646 * jax.random.uniform(key_of[4], (ORDER, GROUPS), jnp.float32) ** steps_of(key_of[4], (ORDER, GROUPS), ((1, 32),), -0.2, 0.2)), 4.882812572759576e-05, 0.03)
    modal_residues = bell_draw(key_of[5], (ORDER, GROUPS), 0.25, 1.5, ((1, 32),), jnp.float32)
    out_grad = bell_draw(key_of[6], (TOKENS, D), 1.0, 6.0, ((0, 8), (1, 32)))
    return dict(token_ids=token_ids, embed_table=embed_table, in_weight=in_weight, feat_taps=feat_taps, modal_rates=modal_rates, modal_residues=modal_residues, out_grad=out_grad)


def featurize(stream, taps):
    summed = jnp.zeros(stream.shape, jnp.float32)
    for tap_index in range(FEAT):
        shifted = jnp.pad(stream, ((tap_index, 0), (0, 0), (0, 0)))[:stream.shape[0]]
        summed = summed + taps[:, tap_index, :][None] * shifted
    return summed

def featurize_back(stream, taps):
    summed = jnp.zeros(stream.shape, jnp.float32)
    for tap_index in range(FEAT):
        shifted = jnp.pad(stream, ((0, tap_index), (0, 0), (0, 0)))[tap_index:]
        summed = summed + taps[:, tap_index, :][None] * shifted
    return summed

def modal(sequence, modal_rates, modal_residues):
    decays = jnp.exp(-modal_rates)
    gain_terms = modal_residues * jnp.sqrt(-jnp.expm1(-2.0 * modal_rates))
    blocks = sequence.reshape(sequence.shape[0], GROUPS, GROUP)

    def advance(carried, entry_row):
        carried = decays[:, :, None] * carried + entry_row[None]
        return (carried, jnp.einsum('og,ogc->gc', gain_terms, carried, precision=lax.Precision.HIGHEST))
    start_state = jnp.zeros((ORDER, GROUPS, GROUP), jnp.float32)
    _, result = lax.scan(advance, start_state, blocks)
    return result.reshape(sequence.shape)

def reference(token_ids, embed_table, in_weight, feat_taps, modal_rates, modal_residues, out_grad):
    embedded = embed_table[token_ids]
    projected = jnp.stack([jnp.dot(embedded, in_weight[:, stream_index, :], preferred_element_type=jnp.float32) for stream_index in range(3)], axis=1).astype(jnp.bfloat16)
    projected = lax.optimization_barrier(projected)
    featured = featurize(projected.astype(jnp.float32), feat_taps)
    query_rows = featured[:, 0]
    key_rows = featured[:, 1]
    value_rows = featured[:, 2]
    mixed_rows = key_rows * value_rows
    long_conv = modal(mixed_rows, modal_rates, modal_residues)
    output = (query_rows * long_conv).astype(jnp.bfloat16)
    grad_rows = out_grad.astype(jnp.float32)
    grad_query = grad_rows * long_conv
    grad_long = grad_rows * query_rows
    grad_mixed = jnp.flip(modal(jnp.flip(grad_long, 0), modal_rates, modal_residues), 0)
    grad_feat = jnp.stack([grad_query, grad_mixed * value_rows, grad_mixed * key_rows], axis=1).astype(jnp.bfloat16)
    grad_feat = lax.optimization_barrier(grad_feat)
    grad_proj = featurize_back(grad_feat.astype(jnp.float32), feat_taps).astype(jnp.bfloat16)
    block_width = D // N_CHAN
    grad_tokens = jnp.zeros(embedded.shape, jnp.float32)
    for block_index in range(N_CHAN):
        first = block_index * block_width
        partial_sum = jnp.zeros(embedded.shape, jnp.float32)
        for stream_index in range(3):
            grad_piece = grad_proj[:, stream_index, first:first + block_width]
            weight_piece = in_weight[:, stream_index, first:first + block_width]
            partial_sum = partial_sum + jnp.dot(grad_piece, weight_piece.T, preferred_element_type=jnp.float32)
        rounded = lax.optimization_barrier(partial_sum.astype(jnp.bfloat16))
        grad_tokens = grad_tokens + rounded.astype(jnp.float32)
    return (output, grad_tokens.astype(jnp.bfloat16))
```

```python
import jax
import jax.numpy as jnp
from jax import lax
from jax.experimental import pallas as pl
from jax.experimental.pallas import tpu as pltpu
from jax.sharding import PartitionSpec as P

F32 = jnp.float32
BF16 = jnp.bfloat16
EXACT = lax.Precision.HIGHEST
N_CTX = 8
N_CHAN = 32
N_Z = 8
BLOCK = 256
GROUP = 16
ORDER = 16
GROUPS = BLOCK // GROUP
VOCAB = 512
SHARE = VOCAB // N_CTX
HALO = 128
EXTRA = 16
WINDOW = N_CTX * BLOCK

CORE_SWAP = [(i, i ^ 1) for i in range(N_CHAN)]
X_SWAP = [(i, i ^ 16) for i in range(N_CHAN)]
Z_GROUPS = [[x * 16 + z * 2 + c for z in range(N_Z)] for x in range(2) for c in range(2)]


def z_shift(by):
    return [(i, (i & 16) | ((i + 2 * by) & 15)) for i in range(N_CHAN)]


def nn(a, b):
    return lax.dot_general(a, b, (((1,), (0,)), ((), ())), preferred_element_type=F32)


def nt(a, b):
    return lax.dot_general(a, b, (((1,), (1,)), ((), ())), preferred_element_type=F32)


def lanes_of(shape):
    return lax.broadcasted_iota(jnp.int32, shape, 1)


def table_kernel(rate_ref, gain_ref, fwd_ref, bwd_ref, end_ref, begin_ref, enter_ref, leave_ref):
    rates = rate_ref[...]
    gains = gain_ref[...]
    position = lanes_of((BLOCK, BLOCK)).astype(F32)
    decay = jnp.exp(-position * rates)
    growth = jnp.exp(position * rates)
    weighted = decay * gains
    end_ref[...] = jnp.exp((position - (BLOCK - 1.0)) * rates).astype(BF16)
    begin_ref[...] = decay.astype(BF16)
    enter_ref[...] = (gains * jnp.exp(-(position + 1.0) * rates)).astype(BF16)
    wide = jnp.minimum(lanes_of((BLOCK, BLOCK + HALO)), BLOCK + 1).astype(F32)
    leave_ref[...] = (gains * jnp.exp((wide - float(BLOCK)) * rates)).astype(BF16)
    row = lax.broadcasted_iota(jnp.int32, (BLOCK, BLOCK), 0)
    col = lanes_of((BLOCK, BLOCK))
    for g in range(GROUPS):
        rows = slice(g * ORDER, (g + 1) * ORDER)
        grown, scaled = growth[rows], weighted[rows]
        dims = (((0,), (0,)), ((), ()))
        later = lax.dot_general(grown, scaled, dims, precision=EXACT, preferred_element_type=F32)
        fwd_ref[g] = jnp.where(col >= row, later, 0.0).astype(BF16)
        earlier = lax.dot_general(scaled, grown, dims, precision=EXACT, preferred_element_type=F32)
        bwd_ref[g] = jnp.where(row >= col, earlier, 0.0).astype(BF16)


def make_tables(rate_col, gain_col):
    square = jax.ShapeDtypeStruct((BLOCK, BLOCK), BF16)
    stack = jax.ShapeDtypeStruct((GROUPS, BLOCK, BLOCK), BF16)
    wide = jax.ShapeDtypeStruct((BLOCK, BLOCK + HALO), BF16)
    vmem = pl.BlockSpec(memory_space=pltpu.VMEM)
    return pl.pallas_call(
        table_kernel,
        out_shape=(stack, stack, square, square, square, wide),
        in_specs=[vmem] * 2,
        out_specs=(vmem,) * 6,
        compiler_params=pltpu.CompilerParams(vmem_limit_bytes=32 << 20),
        cost_estimate=pl.CostEstimate(flops=6 * 64 * 2**20, bytes_accessed=5 << 20, transcendentals=1 << 19),
        name="filter_tables",
    )(rate_col, gain_col)


def project_kernel(place_ref, rows_ref, weight_ref, out_ref, acc_ref):
    step = pl.program_id(0)

    @pl.when(step == 0)
    def _():
        acc_ref[...] = jnp.zeros_like(acc_ref)

    for z in range(4):
        rows = rows_ref[z]
        for s in range(3):
            cols = slice(s * BLOCK, (s + 1) * BLOCK)
            acc_ref[:, cols] += nn(rows, weight_ref[s, 0, z, 0])

    @pl.when(step == pl.num_programs(0) - 1)
    def _():
        out_ref[...] = acc_ref[...].astype(BF16)


def project(place, rows, weight):
    def weight_map(step, place):
        return (0, place[1] ^ ((step // 2) % 2), step % 2, place[3] ^ (step // 4), 0, 0)

    return pl.pallas_call(
        project_kernel,
        out_shape=jax.ShapeDtypeStruct((SHARE, 3 * BLOCK), BF16),
        grid_spec=pltpu.PrefetchScalarGridSpec(
            num_scalar_prefetch=1,
            grid=(8,),
            in_specs=[
                pl.BlockSpec((4, SHARE, BLOCK), lambda step, place: (step, 0, 0)),
                pl.BlockSpec((3, 1, 4, 1, BLOCK, BLOCK), weight_map),
            ],
            out_specs=pl.BlockSpec((SHARE, 3 * BLOCK), lambda step, place: (0, 0)),
            scratch_shapes=[pltpu.VMEM((SHARE, 3 * BLOCK), F32)],
        ),
        compiler_params=pltpu.CompilerParams(vmem_limit_bytes=32 << 20),
        cost_estimate=pl.CostEstimate(flops=2 * 64 * 768 * 8192, bytes_accessed=14 << 20, transcendentals=0),
        name="project",
    )(place, rows, weight)


def mixer_kernel(
    place_ref, table_ref, token_ref, grad_ref, tap_ref, rate_ref, gain_ref,
    fwd_ref, bwd_ref, end_ref, begin_ref, enter_ref, leave_ref,
    out_ref, grad_proj_ref, raw_ref,
):
    own = place_ref[0]
    table = table_ref[...].astype(F32).T.astype(BF16)
    vocab = lax.broadcasted_iota(jnp.int32, (VOCAB, BLOCK), 0)
    for tile in range((WINDOW + 2 * HALO) // BLOCK):
        lanes = slice(tile * BLOCK, (tile + 1) * BLOCK)
        one_hot = jnp.where(token_ref[:, lanes] == vocab, 1.0, 0.0).astype(BF16)
        raw_ref[:, lanes] = nn(table, one_hot)

    def featured(stream, block, width):
        rows = pl.ds(stream * BLOCK, BLOCK)
        begin = pl.multiple_of(block * BLOCK, BLOCK)
        raw = raw_ref[rows, pl.ds(begin, HALO + width)]
        total = tap_ref[rows, 0:1] * raw[:, HALO:]
        for tap in (1, 2):
            total += tap_ref[rows, tap : tap + 1] * raw[:, HALO - tap : HALO - tap + width]
        return total

    rate_row = rate_ref[...]
    gain_row = gain_ref[...]
    block_decay = jnp.exp(rate_row * -float(BLOCK))
    same_group = (
        lax.broadcasted_iota(jnp.int32, (BLOCK, BLOCK), 0) // GROUP == lanes_of((BLOCK, BLOCK)) // ORDER
    )

    def earlier(block, state):
        mixed = featured(1, block, BLOCK) * featured(2, block, BLOCK)
        return block_decay * state + nt(mixed.astype(BF16), end_ref[...])

    def later(step, state):
        block = N_CTX - 1 - step
        grad = grad_ref[block, 0:BLOCK, :].astype(F32) * featured(0, block, BLOCK)
        return block_decay * state + nt(grad.astype(BF16), begin_ref[...])

    zero = jnp.zeros((BLOCK, BLOCK), F32)
    before = lax.fori_loop(0, own, earlier, zero)
    after = lax.fori_loop(0, N_CTX - 1 - own, later, zero)

    wide = BLOCK + HALO
    query = featured(0, own, wide)
    key = featured(1, own, wide)
    value = featured(2, own, wide)
    mixed = key * value
    following = jnp.minimum(own + 1, N_CTX - 1)
    grad_rows = jnp.concatenate(
        [grad_ref[own, 0:BLOCK, :], grad_ref[following, 0:BLOCK, 0:HALO]], axis=1
    ).astype(F32)
    grad_long = grad_rows * query
    mixed_own = mixed[:, :BLOCK].astype(BF16)
    long_own = grad_long[:, :BLOCK].astype(BF16)

    through = block_decay * before + nt(mixed_own, end_ref[...])
    before = jnp.where(same_group, before, 0.0).astype(BF16)
    through = jnp.where(same_group, through, 0.0).astype(BF16)
    after = jnp.where(same_group, after, 0.0).astype(BF16)

    conv_rows, mixed_grads = [], []
    for g in range(GROUPS):
        rows = slice(g * GROUP, (g + 1) * GROUP)
        conv_rows.append(nn(mixed_own[rows], fwd_ref[g]))
        mixed_grads.append(nn(long_own[rows], bwd_ref[g]))
    conv = jnp.concatenate(conv_rows, axis=0) + nn(before, enter_ref[...])
    mixed_grad = jnp.concatenate(mixed_grads, axis=0) + nn(after, leave_ref[:, :BLOCK])

    def filter_at(lag):
        terms = jnp.where(same_group, gain_row * jnp.exp(rate_row * -float(lag)), 0.0)
        return jnp.sum(terms, axis=1, keepdims=True)

    second = lanes_of((BLOCK, HALO)) == 1
    conv_next = nn(through, enter_ref[:, :HALO]) + filter_at(0) * mixed[:, BLOCK:]
    conv_next += jnp.where(second, filter_at(1) * mixed[:, BLOCK - 1 : wide - 1], 0.0)
    grad_next = nn(after, leave_ref[:, BLOCK:])
    grad_next -= jnp.where(second, filter_at(-1) * grad_long[:, BLOCK - 1 : wide - 1], 0.0)

    out_ref[...] = (query[:, :BLOCK] * conv).T.astype(BF16)

    conv = jnp.concatenate([conv, conv_next], axis=1)
    mixed_grad = jnp.concatenate([mixed_grad, grad_next], axis=1)
    lane = lanes_of((BLOCK, wide))
    inside = (lane < BLOCK) | ((lane < BLOCK + 2) & (own < N_CTX - 1))
    streams = (grad_rows * conv, mixed_grad * value, mixed_grad * key)
    for s in range(3):
        rows = slice(s * BLOCK, (s + 1) * BLOCK)
        grads = jnp.where(inside, streams[s], 0.0).astype(BF16).astype(F32)
        total = tap_ref[rows, 0:1] * grads[:, :BLOCK]
        for tap in (1, 2):
            total += tap_ref[rows, tap : tap + 1] * grads[:, tap : tap + BLOCK]
        grad_proj_ref[rows, :] = total.astype(BF16)


def mix(place, table, tokens, grads, taps, rate_row, gain_row, tables):
    vmem = pl.BlockSpec(memory_space=pltpu.VMEM)
    return pl.pallas_call(
        mixer_kernel,
        out_shape=(
            jax.ShapeDtypeStruct((BLOCK, BLOCK), BF16),
            jax.ShapeDtypeStruct((3 * BLOCK, BLOCK), BF16),
        ),
        in_specs=[pl.BlockSpec(memory_space=pltpu.SMEM)] + [vmem] * 12,
        out_specs=(vmem, vmem),
        scratch_shapes=[pltpu.VMEM((3 * BLOCK, WINDOW + 2 * HALO), F32)],
        compiler_params=pltpu.CompilerParams(vmem_limit_bytes=48 << 20),
        cost_estimate=pl.CostEstimate(flops=3 << 30, bytes_accessed=8 << 20, transcendentals=1 << 16),
        name="mixer",
    )(place, table, tokens, grads, taps, rate_row, gain_row, *tables)


def back_kernel(place_ref, grad_ref, weight_ref, own_ref, other_ref):
    for core in range(2):
        target = own_ref if core == 0 else other_ref
        c = place_ref[3] ^ core
        for shift in range(2):
            x = place_ref[1] ^ shift
            total = nn(weight_ref[0, x, 0, c], grad_ref[0:BLOCK])
            total += nn(weight_ref[1, x, 0, c], grad_ref[BLOCK : 2 * BLOCK])
            total += nn(weight_ref[2, x, 0, c], grad_ref[2 * BLOCK :])
            target[0, shift] = total.astype(BF16)


def back_project(place, grad_proj, weight):
    part = jax.ShapeDtypeStruct((N_Z, 2, BLOCK, BLOCK), BF16)
    part_spec = pl.BlockSpec((1, 2, BLOCK, BLOCK), lambda step, place: (step, 0, 0, 0))
    return pl.pallas_call(
        back_kernel,
        out_shape=(part, part),
        grid_spec=pltpu.PrefetchScalarGridSpec(
            num_scalar_prefetch=1,
            grid=(N_Z,),
            in_specs=[
                pl.BlockSpec((3 * BLOCK, BLOCK), lambda step, place: (0, 0)),
                pl.BlockSpec(
                    (3, 2, 1, 2, BLOCK, BLOCK),
                    lambda step, place: (0, 0, (place[2] + step) % N_Z, 0, 0, 0),
                ),
            ],
            out_specs=(part_spec, part_spec),
        ),
        compiler_params=pltpu.CompilerParams(vmem_limit_bytes=32 << 20),
        cost_estimate=pl.CostEstimate(flops=2 * 256 * 768 * 8192, bytes_accessed=17 << 20, transcendentals=0),
        name="back_project",
    )(place, grad_proj, weight)


def added(a, *rest):
    total = a.astype(F32)
    for b in rest:
        total = total + b.astype(F32)
    return total.astype(BF16)


def gather_features(rows):
    held = lax.all_to_all(
        jnp.broadcast_to(rows[None], (N_Z,) + rows.shape), "chan", 0, 0, axis_index_groups=Z_GROUPS
    )
    held = jnp.concatenate([held, lax.ppermute(held, "chan", X_SWAP)], axis=0)
    return jnp.concatenate([held, lax.ppermute(held, "chan", CORE_SWAP)], axis=0)


def gather_ctx(value):
    return lax.all_to_all(jnp.broadcast_to(value[None], (N_CTX,) + value.shape), "ctx", 0, 0)


def reduce_chan(own, other):
    parts = added(own, lax.ppermute(other, "chan", CORE_SWAP))
    up, down = z_shift(1), z_shift(-1)
    ahead = added(lax.ppermute(parts[4], "chan", up), parts[3])
    ahead = added(lax.ppermute(ahead, "chan", up), parts[2])
    behind = added(lax.ppermute(parts[5], "chan", down), parts[6])
    ahead = added(lax.ppermute(ahead, "chan", up), parts[1])
    behind = added(lax.ppermute(behind, "chan", down), parts[7])
    total = added(parts[0], lax.ppermute(ahead, "chan", up), lax.ppermute(behind, "chan", down))
    return added(total[0], lax.ppermute(total[1], "chan", X_SWAP))


def body(token_ids, embed_table, in_weight, feat_taps, modal_rates, modal_residues, out_grad):
    ctx = lax.axis_index("ctx")
    chan = lax.axis_index("chan")
    place = jnp.stack([ctx, chan // 16, (chan // 2) % N_Z, chan % 2]).astype(jnp.int32)
    weight = in_weight.transpose(1, 0, 2).reshape(3, 2, N_Z, 2, BLOCK, BLOCK)

    own_vocab = lax.dynamic_slice_in_dim(embed_table, ctx * SHARE, SHARE, 0)
    features = gather_features(own_vocab)

    id_rows = jnp.stack([token_ids // 256, token_ids % 256]).astype(BF16)
    payload = jnp.concatenate(
        [out_grad.T, id_rows, jnp.zeros((EXTRA - 2, BLOCK), BF16)], axis=0
    )
    grads = gather_ctx(payload)
    ids = grads[:, BLOCK : BLOCK + 2, :].astype(jnp.int32)
    ids = (ids[:, 0] * 256 + ids[:, 1]).reshape(1, WINDOW)
    edge = jnp.full((1, HALO), -1, jnp.int32)
    tokens = jnp.concatenate([edge, ids, edge], axis=1)

    gains = modal_residues * jnp.sqrt(-jnp.expm1(-2.0 * modal_rates))
    rate_row = modal_rates.T.reshape(1, BLOCK)
    gain_row = gains.T.reshape(1, BLOCK)
    tables = make_tables(rate_row.reshape(BLOCK, 1), gain_row.reshape(BLOCK, 1))
    taps = feat_taps.transpose(0, 2, 1).reshape(3 * BLOCK, 3)

    table = gather_ctx(project(place, features, weight)).reshape(VOCAB, 3 * BLOCK)
    output, grad_proj = mix(place, table, tokens, grads, taps, rate_row, gain_row, tables)
    own, other = back_project(place, grad_proj, weight)
    return (output, reduce_chan(own, other).T)


def solution(mesh):
    in_specs = (
        P("ctx"),
        P(None, "chan"),
        P(None, None, "chan"),
        P(None, None, "chan"),
        P(None, "chan"),
        P(None, "chan"),
        P("ctx", "chan"),
    )
    out_specs = (P("ctx", "chan"), P("ctx", "chan"))
    return jax.shard_map(body, mesh=mesh, in_specs=in_specs, out_specs=out_specs, check_vma=False)
```

```python
import functools

import jax
import jax.numpy as jnp
from jax import lax
from jax.experimental import pallas as pl
from jax.experimental.pallas import tpu as pltpu
from jax.sharding import PartitionSpec as P

F32 = jnp.float32
BF16 = jnp.bfloat16
EXACT = lax.Precision.HIGHEST
N_CTX = 8
N_CHAN = 32
N_Z = 8
BLOCK = 256
GROUP = 16
ORDER = 16
GROUPS = BLOCK // GROUP
VOCAB = 512
SHARE = VOCAB // N_CTX
HALO = 128
EXTRA = 16
WINDOW = N_CTX * BLOCK

END = slice(0, BLOCK)
BEGIN = slice(BLOCK, 2 * BLOCK)
ENTER = slice(2 * BLOCK, 3 * BLOCK)
LEAVE = slice(3 * BLOCK, 4 * BLOCK + HALO)
SIDE = 4 * BLOCK + HALO

CORE_SWAP = [(i, i ^ 1) for i in range(N_CHAN)]
X_SWAP = [(i, i ^ 16) for i in range(N_CHAN)]
X_HALF_SWAP = [(i, i ^ 1) for i in range(N_CTX)]
Y_STEPS = (1, -1, 2)
Z_GROUPS = [[x * 16 + z * 2 + c for z in range(N_Z)] for x in range(2) for c in range(2)]


def z_shift(by):
    return [(i, (i & 16) | ((i + 2 * by) & 15)) for i in range(N_CHAN)]


def y_shift(by):
    return [(i, (i & 1) | ((i + 2 * by) & 7)) for i in range(N_CTX)]


def nn(a, b):
    return lax.dot_general(a, b, (((1,), (0,)), ((), ())), preferred_element_type=F32)


def nt(a, b):
    return lax.dot_general(a, b, (((1,), (1,)), ((), ())), preferred_element_type=F32)


def lanes_of(shape):
    return lax.broadcasted_iota(jnp.int32, shape, 1)


def place_of(axis):
    chan = lax.axis_index("chan")
    return {"x": chan // 16, "z": (chan // 2) & (N_Z - 1), "core": chan & 1}[axis]


def payload_kernel(grad_ref, token_ref, out_ref):
    out_ref[:BLOCK] = grad_ref[...].astype(F32).T.astype(BF16)
    tokens = token_ref[...]
    row = lax.broadcasted_iota(jnp.int32, (EXTRA, BLOCK), 0)
    ids = jnp.where(row == 0, tokens >> 8, jnp.where(row == 1, tokens & 255, 0))
    out_ref[BLOCK:] = ids.astype(F32).astype(BF16)


def make_payload(out_grad, token_ids):
    vmem = pl.BlockSpec(memory_space=pltpu.VMEM)
    return pl.pallas_call(
        payload_kernel,
        out_shape=jax.ShapeDtypeStruct((BLOCK + EXTRA, BLOCK), BF16),
        in_specs=[vmem] * 2,
        out_specs=vmem,
        compiler_params=pltpu.CompilerParams(vmem_limit_bytes=4 << 20),
        cost_estimate=pl.CostEstimate(flops=1 << 16, bytes_accessed=1 << 19, transcendentals=0),
        name="payload",
    )(out_grad, token_ids.reshape(1, BLOCK))


def table_kernel(
    rate_ref, gain_ref, tap_ref,
    fwd_ref, bwd_ref, side_ref, row_ref, tap_out_ref,
):
    shape = (BLOCK, ORDER)
    mode = lax.broadcasted_iota(jnp.int32, shape, 0)
    group_pick = jnp.where(mode // ORDER == lanes_of(shape), 1.0, 0.0)
    order_pick = mode % ORDER == lanes_of(shape)
    shape = (ORDER, BLOCK)
    group_row = jnp.where(lanes_of(shape) // ORDER == lax.broadcasted_iota(jnp.int32, shape, 0), 1.0, 0.0)
    order_row = lanes_of(shape) % ORDER == lax.broadcasted_iota(jnp.int32, shape, 0)

    def column(values):
        spread = lax.dot_general(
            group_pick, values, (((1,), (1,)), ((), ())), precision=EXACT, preferred_element_type=F32
        )
        return jnp.sum(jnp.where(order_pick, spread, 0.0), axis=1, keepdims=True)

    def as_row(values):
        spread = lax.dot_general(
            values, group_row, (((1,), (0,)), ((), ())), precision=EXACT, preferred_element_type=F32
        )
        return jnp.sum(jnp.where(order_row, spread, 0.0), axis=0, keepdims=True)

    row_ref[0:1] = as_row(rate_ref[...])
    row_ref[1:2] = as_row(gain_ref[...])
    for s in range(3):
        tap_out_ref[s * BLOCK : (s + 1) * BLOCK, :] = tap_ref[s].T
    rates = column(rate_ref[...])
    gains = column(gain_ref[...])
    position = lanes_of((BLOCK, BLOCK)).astype(F32)
    decay = jnp.exp(-position * rates)
    growth = jnp.exp(position * rates)
    weighted = decay * gains
    side_ref[:, END] = jnp.exp((position - (BLOCK - 1.0)) * rates).astype(BF16)
    side_ref[:, BEGIN] = decay.astype(BF16)
    side_ref[:, ENTER] = (gains * jnp.exp(-(position + 1.0) * rates)).astype(BF16)
    wide = jnp.minimum(lanes_of((BLOCK, BLOCK + HALO)), BLOCK + 1).astype(F32)
    side_ref[:, LEAVE] = (gains * jnp.exp((wide - float(BLOCK)) * rates)).astype(BF16)
    row = lax.broadcasted_iota(jnp.int32, (BLOCK, BLOCK), 0)
    col = lanes_of((BLOCK, BLOCK))
    for g in range(GROUPS):
        rows = slice(g * ORDER, (g + 1) * ORDER)
        grown, scaled = growth[rows], weighted[rows]
        dims = (((0,), (0,)), ((), ()))
        later = lax.dot_general(grown, scaled, dims, precision=EXACT, preferred_element_type=F32)
        fwd_ref[g] = jnp.where(col >= row, later, 0.0).astype(BF16)
        earlier = lax.dot_general(scaled, grown, dims, precision=EXACT, preferred_element_type=F32)
        bwd_ref[g] = jnp.where(row >= col, earlier, 0.0).astype(BF16)


def make_tables(rates, gains, taps):
    stack = jax.ShapeDtypeStruct((GROUPS, BLOCK, BLOCK), BF16)
    side = jax.ShapeDtypeStruct((BLOCK, SIDE), BF16)
    rows = jax.ShapeDtypeStruct((2, BLOCK), F32)
    columns = jax.ShapeDtypeStruct((3 * BLOCK, 3), F32)
    vmem = pl.BlockSpec(memory_space=pltpu.VMEM)
    return pl.pallas_call(
        table_kernel,
        out_shape=(stack, stack, side, rows, columns),
        in_specs=[vmem] * 3,
        out_specs=(vmem,) * 5,
        compiler_params=pltpu.CompilerParams(vmem_limit_bytes=8 << 20),
        cost_estimate=pl.CostEstimate(flops=6 * 64 * 2**20, bytes_accessed=5 << 20, transcendentals=1 << 19),
        name="filter_tables",
    )(rates, gains, taps)


def project_kernel(parts, first, last, *refs):
    row_refs, refs = refs[: len(parts)], refs[len(parts) :]
    weight_ref, refs = refs[0], refs[1:]
    out_ref, held_ref, sems = refs[-3:]
    copies = []
    for n, part in enumerate(parts):
        c, x = place_of("core") ^ (part // 2), place_of("x") ^ (part % 2)
        copies.append(pltpu.make_async_copy(weight_ref.at[:, x, :, c], held_ref.at[n], sems.at[n]))
        copies[n].start()
    total = tuple(
        jnp.zeros((SHARE, BLOCK), F32) if first else refs[0][:, s * BLOCK : (s + 1) * BLOCK] for s in range(3)
    )
    for n, row_ref in enumerate(row_refs):
        copies[n].wait()

        def add_block(z, total):
            rows = row_ref[z]
            return tuple(total[s] + nn(rows, held_ref[n, s, z]) for s in range(3))

        total = lax.fori_loop(0, N_Z, add_block, total, unroll=2)
    for s in range(3):
        out_ref[:, s * BLOCK : (s + 1) * BLOCK] = total[s].astype(BF16 if last else F32)


def project(parts, rows, weight, sums, last):
    vmem = pl.BlockSpec(memory_space=pltpu.VMEM)
    first = sums is None
    return pl.pallas_call(
        functools.partial(project_kernel, parts, first, last),
        out_shape=jax.ShapeDtypeStruct((SHARE, 3 * BLOCK), BF16 if last else F32),
        in_specs=[vmem] * len(parts) + [pl.BlockSpec(memory_space=pltpu.HBM)] + [vmem] * (not first),
        out_specs=vmem,
        scratch_shapes=[
            pltpu.VMEM((len(parts), 3, N_Z, BLOCK, BLOCK), BF16),
            pltpu.SemaphoreType.DMA((len(parts),)),
        ],
        compiler_params=pltpu.CompilerParams(vmem_limit_bytes=50 << 20),
        cost_estimate=pl.CostEstimate(
            flops=2 * 64 * 768 * 2048 * len(parts), bytes_accessed=len(parts) * (3 << 20), transcendentals=0
        ),
        name="project",
    )(*rows, weight, *([] if first else [sums]))


def mixer_kernel(*refs):
    table_refs, refs = refs[:N_CTX], refs[N_CTX:]
    sources, refs = refs[:4], refs[4:]
    row_ref, tap_ref, out_ref, grad_proj_ref, raw_ref = refs[:5]
    grad_ref, side_ref, fwd_ref, bwd_ref, sems = refs[5:]
    copies = [
        pltpu.make_async_copy(source, target, sems.at[n])
        for n, (source, target) in enumerate(zip(sources, (grad_ref, side_ref, fwd_ref, bwd_ref)))
    ]
    for copy in copies:
        copy.start()
    own = lax.axis_index("ctx")
    table = jnp.concatenate([ref[...].astype(F32) for ref in table_refs], axis=0).T.astype(BF16)
    share_row = lax.broadcasted_iota(jnp.int32, (SHARE, BLOCK), 0)
    vocab = []
    for step in (0,) + Y_STEPS:
        for half in range(2):
            source = ((own - 2 * step) & 6) | ((own & 1) ^ half)
            vocab.append(share_row + source * SHARE)
    vocab = jnp.concatenate(vocab, axis=0)

    edge = jnp.zeros((3 * BLOCK, HALO), F32)
    raw_ref[:, :HALO] = edge
    raw_ref[:, HALO + WINDOW :] = edge

    def look_up(block, carried):
        ids = grad_ref[block, BLOCK : BLOCK + EXTRA, :].astype(F32)
        ids = (ids[0:1] * 256.0 + ids[1:2]).astype(jnp.int32)
        one_hot = jnp.where(ids == vocab, 1.0, 0.0).astype(BF16)
        raw_ref[:, pl.ds(pl.multiple_of(HALO + block * BLOCK, HALO), BLOCK)] = nn(table, one_hot)
        return carried

    copies[0].wait()
    lax.fori_loop(0, N_CTX, look_up, 0)
    copies[1].wait()

    def featured(stream, block, width):
        rows = pl.ds(stream * BLOCK, BLOCK)
        begin = pl.multiple_of(block * BLOCK, BLOCK)
        raw = raw_ref[rows, pl.ds(begin, HALO + width)]
        total = tap_ref[rows, 0:1] * raw[:, HALO:]
        for tap in (1, 2):
            total += tap_ref[rows, tap : tap + 1] * raw[:, HALO - tap : HALO - tap + width]
        return total

    rate_row = row_ref[0:1]
    gain_row = row_ref[1:2]
    block_decay = jnp.exp(rate_row * -float(BLOCK))
    same_group = (
        lax.broadcasted_iota(jnp.int32, (BLOCK, BLOCK), 0) // GROUP == lanes_of((BLOCK, BLOCK)) // ORDER
    )

    def earlier(block, state):
        mixed = featured(1, block, BLOCK) * featured(2, block, BLOCK)
        return block_decay * state + nt(mixed.astype(BF16), side_ref[:, END])

    def later(step, state):
        block = N_CTX - 1 - step
        grad = grad_ref[block, 0:BLOCK, :].astype(F32) * featured(0, block, BLOCK)
        return block_decay * state + nt(grad.astype(BF16), side_ref[:, BEGIN])

    zero = jnp.zeros((BLOCK, BLOCK), F32)
    before = lax.fori_loop(0, own, earlier, zero)
    after = lax.fori_loop(0, N_CTX - 1 - own, later, zero)

    wide = BLOCK + HALO
    query = featured(0, own, wide)
    key = featured(1, own, wide)
    value = featured(2, own, wide)
    mixed = key * value
    following = jnp.minimum(own + 1, N_CTX - 1)
    grad_rows = jnp.concatenate(
        [grad_ref[own, 0:BLOCK, :], grad_ref[following, 0:BLOCK, 0:HALO]], axis=1
    ).astype(F32)
    grad_long = grad_rows * query
    mixed_own = mixed[:, :BLOCK].astype(BF16)
    long_own = grad_long[:, :BLOCK].astype(BF16)

    through = block_decay * before + nt(mixed_own, side_ref[:, END])
    before = jnp.where(same_group, before, 0.0).astype(BF16)
    through = jnp.where(same_group, through, 0.0).astype(BF16)
    after = jnp.where(same_group, after, 0.0).astype(BF16)

    copies[2].wait()
    copies[3].wait()
    conv_rows, mixed_grads = [], []
    for g in range(GROUPS):
        rows = slice(g * GROUP, (g + 1) * GROUP)
        conv_rows.append(nn(mixed_own[rows], fwd_ref[g]))
        mixed_grads.append(nn(long_own[rows], bwd_ref[g]))
    conv = jnp.concatenate(conv_rows, axis=0) + nn(before, side_ref[:, ENTER])
    mixed_grad = jnp.concatenate(mixed_grads, axis=0) + nn(after, side_ref[:, LEAVE.start : LEAVE.start + BLOCK])

    def filter_at(lag):
        terms = jnp.where(same_group, gain_row * jnp.exp(rate_row * -float(lag)), 0.0)
        return jnp.sum(terms, axis=1, keepdims=True)

    second = lanes_of((BLOCK, HALO)) == 1
    conv_next = nn(through, side_ref[:, ENTER.start : ENTER.start + HALO]) + filter_at(0) * mixed[:, BLOCK:]
    conv_next += jnp.where(second, filter_at(1) * mixed[:, BLOCK - 1 : wide - 1], 0.0)
    grad_next = nn(after, side_ref[:, LEAVE.start + BLOCK :])
    grad_next -= jnp.where(second, filter_at(-1) * grad_long[:, BLOCK - 1 : wide - 1], 0.0)

    out_ref[...] = (query[:, :BLOCK] * conv).T.astype(BF16)

    conv = jnp.concatenate([conv, conv_next], axis=1)
    mixed_grad = jnp.concatenate([mixed_grad, grad_next], axis=1)
    lane = lanes_of((BLOCK, wide))
    inside = (lane < BLOCK) | ((lane < BLOCK + 2) & (own < N_CTX - 1))
    streams = (grad_rows * conv, mixed_grad * value, mixed_grad * key)
    for s in range(3):
        rows = slice(s * BLOCK, (s + 1) * BLOCK)
        grads = jnp.where(inside, streams[s], 0.0).astype(BF16).astype(F32)
        total = tap_ref[rows, 0:1] * grads[:, :BLOCK]
        for tap in (1, 2):
            total += tap_ref[rows, tap : tap + 1] * grads[:, tap : tap + BLOCK]
        grad_proj_ref[rows, :] = total.astype(BF16)


def mix(pieces, grads, tables):
    fwd, bwd, side, row, taps = tables
    vmem = pl.BlockSpec(memory_space=pltpu.VMEM)
    return pl.pallas_call(
        mixer_kernel,
        out_shape=(
            jax.ShapeDtypeStruct((BLOCK, BLOCK), BF16),
            jax.ShapeDtypeStruct((3 * BLOCK, BLOCK), BF16),
        ),
        in_specs=[vmem] * N_CTX + [pl.BlockSpec(memory_space=pl.ANY)] * 4 + [vmem] * 2,
        out_specs=(vmem, vmem),
        scratch_shapes=[
            pltpu.VMEM((3 * BLOCK, WINDOW + 2 * HALO), F32),
            pltpu.VMEM((N_CTX, BLOCK + EXTRA, BLOCK), BF16),
            pltpu.VMEM((BLOCK, SIDE), BF16),
            pltpu.VMEM((GROUPS, BLOCK, BLOCK), BF16),
            pltpu.VMEM((GROUPS, BLOCK, BLOCK), BF16),
            pltpu.SemaphoreType.DMA((4,)),
        ],
        compiler_params=pltpu.CompilerParams(vmem_limit_bytes=50 << 20),
        cost_estimate=pl.CostEstimate(flops=3 << 30, bytes_accessed=8 << 20, transcendentals=1 << 16),
        name="mixer",
    )(*pieces, grads, side, fwd, bwd, row, taps)


def back_kernel(step_ref, grad_ref, weight_ref, own_ref, other_ref, held_ref, sems):
    count = own_ref.shape[0]

    def copy(n):
        z = (place_of("z") + step_ref[n]) & (N_Z - 1)
        return pltpu.make_async_copy(weight_ref.at[:, :, z], held_ref.at[n], sems.at[n])

    for n in range(count):
        copy(n).start()

    def one_step(n, carried):
        copy(n).wait()
        for core in (1, 0):
            target = other_ref if core else own_ref
            c = place_of("core") ^ core
            for shift in range(2):
                x = place_of("x") ^ shift
                total = nn(held_ref[n, 0, x, c], grad_ref[0:BLOCK])
                total += nn(held_ref[n, 1, x, c], grad_ref[BLOCK : 2 * BLOCK])
                total += nn(held_ref[n, 2, x, c], grad_ref[2 * BLOCK :])
                target[n, shift] = total.astype(BF16)
        return carried

    lax.fori_loop(0, count, one_step, 0)


def back_project(grad_proj, weight, steps):
    vmem = pl.BlockSpec(memory_space=pltpu.VMEM)
    count = len(steps)
    part = jax.ShapeDtypeStruct((count, 2, BLOCK, BLOCK), BF16)
    return pl.pallas_call(
        back_kernel,
        out_shape=(part, part),
        in_specs=[pl.BlockSpec(memory_space=pltpu.SMEM), vmem, pl.BlockSpec(memory_space=pltpu.HBM)],
        out_specs=(vmem, vmem),
        scratch_shapes=[
            pltpu.VMEM((count, 3, 2, 2, BLOCK, BLOCK), BF16),
            pltpu.SemaphoreType.DMA((count,)),
        ],
        compiler_params=pltpu.CompilerParams(vmem_limit_bytes=50 << 20),
        cost_estimate=pl.CostEstimate(
            flops=2 * 256 * 768 * 1024 * count, bytes_accessed=count << 21, transcendentals=0
        ),
        name="back_project",
    )(jnp.asarray(steps, jnp.int32), grad_proj, weight)


def project_features(rows, weight):
    held = lax.all_to_all(
        jnp.broadcast_to(rows[None], (N_Z,) + rows.shape), "chan", 0, 0, axis_index_groups=Z_GROUPS
    )
    beside = lax.ppermute(held, "chan", X_SWAP)
    across = lax.ppermute(held, "chan", CORE_SWAP)
    both = lax.ppermute(beside, "chan", CORE_SWAP)
    sums = project((0,), (held,), weight, None, False)
    sums = project((2, 1), (across, beside), weight, sums, False)
    return project((3,), (both,), weight, sums, True)


def gather_ctx(value):
    across = lax.ppermute(value, "ctx", X_HALF_SWAP)
    found = [value, across]
    for piece in (value, across):
        found += [lax.ppermute(piece, "ctx", y_shift(by)) for by in Y_STEPS]
    return [found[n] for n in (0, 1, 2, 5, 3, 6, 4, 7)]


def reduce_chan(grad_proj, weight):
    up, down = z_shift(1), z_shift(-1)
    terms = {}
    for steps in ((4,), (3, 5), (2, 6, 1, 7, 0)):
        own, other = back_project(grad_proj, weight, steps)
        swapped = lax.ppermute(other, "chan", CORE_SWAP)
        for n, step in enumerate(steps):
            terms[step] = own[n].astype(F32) + swapped[n].astype(F32)
    far = terms[4].astype(BF16)
    ahead = lax.ppermute(far[0], "chan", up).astype(F32)
    behind = lax.ppermute(far[1], "chan", down).astype(F32)
    ahead = jnp.stack([terms[3][0] + ahead, terms[3][1]])
    behind = jnp.stack([terms[5][0], terms[5][1] + behind])
    for near, other in ((2, 6), (1, 7)):
        ahead = terms[near] + lax.ppermute(ahead.astype(BF16), "chan", up).astype(F32)
        behind = terms[other] + lax.ppermute(behind.astype(BF16), "chan", down).astype(F32)
    total = terms[0] + lax.ppermute(ahead.astype(BF16), "chan", up).astype(F32)
    total = total + lax.ppermute(behind.astype(BF16), "chan", down).astype(F32)
    total = total[0] + lax.ppermute(total[1].astype(BF16), "chan", X_SWAP).astype(F32)
    return total.astype(BF16)


def body(token_ids, embed_table, in_weight, feat_taps, modal_rates, modal_residues, out_grad):
    weight = in_weight.transpose(1, 0, 2).reshape(3, 2, N_Z, 2, BLOCK, BLOCK)
    own_vocab = lax.dynamic_slice_in_dim(embed_table, lax.axis_index("ctx") * SHARE, SHARE, 0)
    payload = make_payload(out_grad, token_ids)
    grads = lax.all_gather(payload, "ctx", axis=0)

    part = project_features(own_vocab, weight)
    modal_rates, part = lax.optimization_barrier((modal_rates, part))
    pieces = gather_ctx(part)

    gains = modal_residues * jnp.sqrt(-jnp.expm1(-2.0 * modal_rates))
    tables = make_tables(modal_rates, gains, feat_taps)

    output, grad_proj = mix(pieces, grads, tables)
    return (output, reduce_chan(grad_proj, weight).T)


def solution(mesh):
    in_specs = (
        P("ctx"),
        P(None, "chan"),
        P(None, None, "chan"),
        P(None, None, "chan"),
        P(None, "chan"),
        P(None, "chan"),
        P("ctx", "chan"),
    )
    out_specs = (P("ctx", "chan"), P("ctx", "chan"))
    return jax.shard_map(body, mesh=mesh, in_specs=in_specs, out_specs=out_specs, check_vma=False)
```

```python
import functools

import jax
import jax.numpy as jnp
from jax import lax
from jax.experimental import pallas as pl
from jax.experimental.pallas import tpu as pltpu
from jax.sharding import PartitionSpec as P

F32 = jnp.float32
BF16 = jnp.bfloat16
EXACT = lax.Precision.HIGHEST
N_CTX = 8
N_CHAN = 32
N_Z = 8
BLOCK = 256
GROUP = 16
ORDER = 16
GROUPS = BLOCK // GROUP
VOCAB = 512
SHARE = VOCAB // N_CTX
HALO = 128
EXTRA = 16
WINDOW = N_CTX * BLOCK

END = slice(0, BLOCK)
BEGIN = slice(BLOCK, 2 * BLOCK)
ENTER = slice(2 * BLOCK, 3 * BLOCK)
LEAVE = slice(3 * BLOCK, 4 * BLOCK + HALO)
SIDE = 4 * BLOCK + HALO

CORE_SWAP = [(i, i ^ 1) for i in range(N_CHAN)]
X_SWAP = [(i, i ^ 16) for i in range(N_CHAN)]
X_HALF_SWAP = [(i, i ^ 1) for i in range(N_CTX)]
Y_STEPS = (1, -1, 2)
Z_GROUPS = [[x * 16 + z * 2 + c for z in range(N_Z)] for x in range(2) for c in range(2)]


def z_shift(by):
    return [(i, (i & 16) | ((i + 2 * by) & 15)) for i in range(N_CHAN)]


def y_shift(by):
    return [(i, (i & 1) | ((i + 2 * by) & 7)) for i in range(N_CTX)]


def nn(a, b):
    return lax.dot_general(a, b, (((1,), (0,)), ((), ())), preferred_element_type=F32)


def nt(a, b):
    return lax.dot_general(a, b, (((1,), (1,)), ((), ())), preferred_element_type=F32)


def lanes_of(shape):
    return lax.broadcasted_iota(jnp.int32, shape, 1)


def place_of(axis):
    chan = lax.axis_index("chan")
    return {"x": chan // 16, "z": (chan // 2) & (N_Z - 1), "core": chan & 1}[axis]


def payload_kernel(grad_ref, token_ref, out_ref):
    out_ref[:BLOCK] = grad_ref[...].astype(F32).T.astype(BF16)
    tokens = token_ref[...]
    row = lax.broadcasted_iota(jnp.int32, (EXTRA, BLOCK), 0)
    ids = jnp.where(row == 0, tokens >> 8, jnp.where(row == 1, tokens & 255, 0))
    out_ref[BLOCK:] = ids.astype(F32).astype(BF16)


def make_payload(out_grad, token_ids):
    vmem = pl.BlockSpec(memory_space=pltpu.VMEM)
    return pl.pallas_call(
        payload_kernel,
        out_shape=jax.ShapeDtypeStruct((BLOCK + EXTRA, BLOCK), BF16),
        in_specs=[vmem] * 2,
        out_specs=vmem,
        compiler_params=pltpu.CompilerParams(vmem_limit_bytes=4 << 20),
        cost_estimate=pl.CostEstimate(flops=1 << 16, bytes_accessed=1 << 19, transcendentals=0),
        name="payload",
    )(out_grad, token_ids.reshape(1, BLOCK))


def table_kernel(
    rate_ref, gain_ref, tap_ref,
    fwd_ref, side_ref, row_ref, tap_out_ref,
):
    shape = (BLOCK, ORDER)
    mode = lax.broadcasted_iota(jnp.int32, shape, 0)
    group_pick = jnp.where(mode // ORDER == lanes_of(shape), 1.0, 0.0)
    order_pick = mode % ORDER == lanes_of(shape)
    shape = (ORDER, BLOCK)
    group_row = jnp.where(lanes_of(shape) // ORDER == lax.broadcasted_iota(jnp.int32, shape, 0), 1.0, 0.0)
    order_row = lanes_of(shape) % ORDER == lax.broadcasted_iota(jnp.int32, shape, 0)

    def column(values):
        spread = lax.dot_general(
            group_pick, values, (((1,), (1,)), ((), ())), precision=EXACT, preferred_element_type=F32
        )
        return jnp.sum(jnp.where(order_pick, spread, 0.0), axis=1, keepdims=True)

    def as_row(values):
        spread = lax.dot_general(
            values, group_row, (((1,), (0,)), ((), ())), precision=EXACT, preferred_element_type=F32
        )
        return jnp.sum(jnp.where(order_row, spread, 0.0), axis=0, keepdims=True)

    row_ref[0:1] = as_row(rate_ref[...])
    row_ref[1:2] = as_row(gain_ref[...])
    for s in range(3):
        tap_out_ref[s * BLOCK : (s + 1) * BLOCK, :] = tap_ref[s].T
    rates = column(rate_ref[...])
    gains = column(gain_ref[...])
    position = lanes_of((BLOCK, BLOCK)).astype(F32)
    decay = jnp.exp(-position * rates)
    growth = jnp.exp(position * rates)
    weighted = decay * gains
    side_ref[:, END] = jnp.exp((position - (BLOCK - 1.0)) * rates).astype(BF16)
    side_ref[:, BEGIN] = decay.astype(BF16)
    side_ref[:, ENTER] = (gains * jnp.exp(-(position + 1.0) * rates)).astype(BF16)
    wide = jnp.minimum(lanes_of((BLOCK, BLOCK + HALO)), BLOCK + 1).astype(F32)
    side_ref[:, LEAVE] = (gains * jnp.exp((wide - float(BLOCK)) * rates)).astype(BF16)
    row = lax.broadcasted_iota(jnp.int32, (BLOCK, BLOCK), 0)
    col = lanes_of((BLOCK, BLOCK))
    for g in range(GROUPS):
        rows = slice(g * ORDER, (g + 1) * ORDER)
        grown, scaled = growth[rows], weighted[rows]
        dims = (((0,), (0,)), ((), ()))
        later = lax.dot_general(grown, scaled, dims, precision=EXACT, preferred_element_type=F32)
        fwd_ref[g] = jnp.where(col >= row, later, 0.0).astype(BF16)


def make_tables(rates, gains, taps):
    stack = jax.ShapeDtypeStruct((GROUPS, BLOCK, BLOCK), BF16)
    side = jax.ShapeDtypeStruct((BLOCK, SIDE), BF16)
    rows = jax.ShapeDtypeStruct((2, BLOCK), F32)
    columns = jax.ShapeDtypeStruct((3 * BLOCK, 3), F32)
    vmem = pl.BlockSpec(memory_space=pltpu.VMEM)
    return pl.pallas_call(
        table_kernel,
        out_shape=(stack, side, rows, columns),
        in_specs=[vmem] * 3,
        out_specs=(vmem,) * 4,
        compiler_params=pltpu.CompilerParams(vmem_limit_bytes=8 << 20),
        cost_estimate=pl.CostEstimate(flops=6 * 64 * 2**20, bytes_accessed=5 << 20, transcendentals=1 << 19),
        name="filter_tables",
    )(rates, gains, taps)


def project_kernel(parts, first, last, *refs):
    row_refs, refs = refs[: len(parts)], refs[len(parts) :]
    weight_ref, refs = refs[0], refs[1:]
    out_ref, held_ref, sems = refs[-3:]
    copies = []
    for n, part in enumerate(parts):
        c, x = place_of("core") ^ (part // 2), place_of("x") ^ (part % 2)
        copies.append(pltpu.make_async_copy(weight_ref.at[:, x, :, c], held_ref.at[n], sems.at[n]))
        copies[n].start()
    total = tuple(
        jnp.zeros((SHARE, BLOCK), F32) if first else refs[0][:, s * BLOCK : (s + 1) * BLOCK] for s in range(3)
    )
    for n, row_ref in enumerate(row_refs):
        copies[n].wait()

        def add_block(z, total):
            rows = row_ref[z]
            return tuple(total[s] + nn(rows, held_ref[n, s, z]) for s in range(3))

        total = lax.fori_loop(0, N_Z, add_block, total, unroll=2)
    for s in range(3):
        out_ref[:, s * BLOCK : (s + 1) * BLOCK] = total[s].astype(BF16 if last else F32)


def project(parts, rows, weight, sums, last):
    vmem = pl.BlockSpec(memory_space=pltpu.VMEM)
    first = sums is None
    return pl.pallas_call(
        functools.partial(project_kernel, parts, first, last),
        out_shape=jax.ShapeDtypeStruct((SHARE, 3 * BLOCK), BF16 if last else F32),
        in_specs=[vmem] * len(parts) + [pl.BlockSpec(memory_space=pltpu.HBM)] + [vmem] * (not first),
        out_specs=vmem,
        scratch_shapes=[
            pltpu.VMEM((len(parts), 3, N_Z, BLOCK, BLOCK), BF16),
            pltpu.SemaphoreType.DMA((len(parts),)),
        ],
        compiler_params=pltpu.CompilerParams(vmem_limit_bytes=50 << 20),
        cost_estimate=pl.CostEstimate(
            flops=2 * 64 * 768 * 2048 * len(parts), bytes_accessed=len(parts) * (3 << 20), transcendentals=0
        ),
        name="project",
    )(*rows, weight, *([] if first else [sums]))


def source_of(own, n):
    return ((own - 2 * ((0,) + Y_STEPS)[n // 2]) & 6) | ((own & 1) ^ (n % 2))


def mixer_kernel(*refs):
    own = lax.axis_index("ctx")
    table_refs, refs = refs[:N_CTX], refs[N_CTX:]
    sources, refs = refs[:6], refs[6:]
    row_ref, tap_ref, out_ref, grad_proj_ref, raw_ref = refs[:5]
    grad_ref, side_ref, fwd_ref, sems = refs[5:]
    copies = []
    for n in range(N_CTX):
        target = grad_ref.at[source_of(own, n)]
        copies.append(pltpu.make_async_copy(sources[n // 2].at[n % 2], target, sems.at[n]))
    copies.append(pltpu.make_async_copy(sources[4], side_ref, sems.at[N_CTX]))
    copies.append(pltpu.make_async_copy(sources[5], fwd_ref, sems.at[N_CTX + 1]))
    for copy in copies:
        copy.start()
    table = jnp.concatenate([ref[...].astype(F32) for ref in table_refs], axis=0).T.astype(BF16)
    share_row = lax.broadcasted_iota(jnp.int32, (SHARE, BLOCK), 0)
    vocab = jnp.concatenate([share_row + source_of(own, n) * SHARE for n in range(N_CTX)], axis=0)

    edge = jnp.zeros((3 * BLOCK, HALO), F32)
    raw_ref[:, :HALO] = edge
    raw_ref[:, HALO + WINDOW :] = edge

    def look_up(block, carried):
        ids = grad_ref[block, BLOCK : BLOCK + EXTRA, :].astype(F32)
        ids = (ids[0:1] * 256.0 + ids[1:2]).astype(jnp.int32)
        one_hot = jnp.where(ids == vocab, 1.0, 0.0).astype(BF16)
        raw_ref[:, pl.ds(pl.multiple_of(HALO + block * BLOCK, HALO), BLOCK)] = nn(table, one_hot)
        return carried

    for copy in copies[:N_CTX]:
        copy.wait()
    lax.fori_loop(0, N_CTX, look_up, 0)
    copies[N_CTX].wait()

    def featured(stream, block, width):
        rows = pl.ds(stream * BLOCK, BLOCK)
        begin = pl.multiple_of(block * BLOCK, BLOCK)
        raw = raw_ref[rows, pl.ds(begin, HALO + width)]
        total = tap_ref[rows, 0:1] * raw[:, HALO:]
        for tap in (1, 2):
            total += tap_ref[rows, tap : tap + 1] * raw[:, HALO - tap : HALO - tap + width]
        return total

    rate_row = row_ref[0:1]
    gain_row = row_ref[1:2]
    block_decay = jnp.exp(rate_row * -float(BLOCK))
    same_group = (
        lax.broadcasted_iota(jnp.int32, (BLOCK, BLOCK), 0) // GROUP == lanes_of((BLOCK, BLOCK)) // ORDER
    )

    def earlier(block, state):
        mixed = featured(1, block, BLOCK) * featured(2, block, BLOCK)
        return block_decay * state + nt(mixed.astype(BF16), side_ref[:, END])

    def later(step, state):
        block = N_CTX - 1 - step
        grad = grad_ref[block, 0:BLOCK, :].astype(F32) * featured(0, block, BLOCK)
        return block_decay * state + nt(grad.astype(BF16), side_ref[:, BEGIN])

    zero = jnp.zeros((BLOCK, BLOCK), F32)
    before = lax.fori_loop(0, own, earlier, zero)
    after = lax.fori_loop(0, N_CTX - 1 - own, later, zero)

    wide = BLOCK + HALO
    query = featured(0, own, wide)
    key = featured(1, own, wide)
    value = featured(2, own, wide)
    mixed = key * value
    following = jnp.minimum(own + 1, N_CTX - 1)
    grad_rows = jnp.concatenate(
        [grad_ref[own, 0:BLOCK, :], grad_ref[following, 0:BLOCK, 0:HALO]], axis=1
    ).astype(F32)
    grad_long = grad_rows * query
    mixed_own = mixed[:, :BLOCK].astype(BF16)
    long_own = grad_long[:, :BLOCK].astype(BF16)

    through = block_decay * before + nt(mixed_own, side_ref[:, END])
    before = jnp.where(same_group, before, 0.0).astype(BF16)
    through = jnp.where(same_group, through, 0.0).astype(BF16)
    after = jnp.where(same_group, after, 0.0).astype(BF16)

    copies[N_CTX + 1].wait()
    conv_rows, mixed_grads = [], []
    for g in range(GROUPS):
        rows = slice(g * GROUP, (g + 1) * GROUP)
        conv_rows.append(nn(mixed_own[rows], fwd_ref[g]))
        mixed_grads.append(nt(long_own[rows], fwd_ref[g]))
    conv = jnp.concatenate(conv_rows, axis=0) + nn(before, side_ref[:, ENTER])
    mixed_grad = jnp.concatenate(mixed_grads, axis=0) + nn(after, side_ref[:, LEAVE.start : LEAVE.start + BLOCK])

    def filter_at(lag):
        terms = jnp.where(same_group, gain_row * jnp.exp(rate_row * -float(lag)), 0.0)
        return jnp.sum(terms, axis=1, keepdims=True)

    second = lanes_of((BLOCK, HALO)) == 1
    conv_next = nn(through, side_ref[:, ENTER.start : ENTER.start + HALO]) + filter_at(0) * mixed[:, BLOCK:]
    conv_next += jnp.where(second, filter_at(1) * mixed[:, BLOCK - 1 : wide - 1], 0.0)
    grad_next = nn(after, side_ref[:, LEAVE.start + BLOCK :])
    grad_next -= jnp.where(second, filter_at(-1) * grad_long[:, BLOCK - 1 : wide - 1], 0.0)

    out_ref[...] = (query[:, :BLOCK] * conv).T.astype(BF16)

    conv = jnp.concatenate([conv, conv_next], axis=1)
    mixed_grad = jnp.concatenate([mixed_grad, grad_next], axis=1)
    lane = lanes_of((BLOCK, wide))
    inside = (lane < BLOCK) | ((lane < BLOCK + 2) & (own < N_CTX - 1))
    streams = (grad_rows * conv, mixed_grad * value, mixed_grad * key)
    for s in range(3):
        rows = slice(s * BLOCK, (s + 1) * BLOCK)
        grads = jnp.where(inside, streams[s], 0.0).astype(BF16).astype(F32)
        total = tap_ref[rows, 0:1] * grads[:, :BLOCK]
        for tap in (1, 2):
            total += tap_ref[rows, tap : tap + 1] * grads[:, tap : tap + BLOCK]
        grad_proj_ref[rows, :] = total.astype(BF16)


def mix(pieces, grads, tables):
    fwd, side, row, taps = tables
    vmem = pl.BlockSpec(memory_space=pltpu.VMEM)
    return pl.pallas_call(
        mixer_kernel,
        out_shape=(
            jax.ShapeDtypeStruct((BLOCK, BLOCK), BF16),
            jax.ShapeDtypeStruct((3 * BLOCK, BLOCK), BF16),
        ),
        in_specs=[vmem] * N_CTX + [pl.BlockSpec(memory_space=pl.ANY)] * 6 + [vmem] * 2,
        out_specs=(vmem, vmem),
        scratch_shapes=[
            pltpu.VMEM((3 * BLOCK, WINDOW + 2 * HALO), F32),
            pltpu.VMEM((N_CTX, BLOCK + EXTRA, BLOCK), BF16),
            pltpu.VMEM((BLOCK, SIDE), BF16),
            pltpu.VMEM((GROUPS, BLOCK, BLOCK), BF16),
            pltpu.SemaphoreType.DMA((N_CTX + 2,)),
        ],
        compiler_params=pltpu.CompilerParams(vmem_limit_bytes=50 << 20),
        cost_estimate=pl.CostEstimate(flops=3 << 30, bytes_accessed=8 << 20, transcendentals=1 << 16),
        name="mixer",
    )(*pieces, *grads, side, fwd, row, taps)


def back_kernel(step_ref, grad_ref, weight_ref, own_ref, other_ref, held_ref, sems):
    count = own_ref.shape[0]

    def copy(n):
        z = (place_of("z") + step_ref[n]) & (N_Z - 1)
        return pltpu.make_async_copy(weight_ref.at[:, :, z], held_ref.at[n], sems.at[n])

    for n in range(count):
        copy(n).start()

    def one_step(n, carried):
        copy(n).wait()
        for core in (1, 0):
            target = other_ref if core else own_ref
            c = place_of("core") ^ core
            for shift in range(2):
                x = place_of("x") ^ shift
                total = nn(held_ref[n, 0, x, c], grad_ref[0:BLOCK])
                total += nn(held_ref[n, 1, x, c], grad_ref[BLOCK : 2 * BLOCK])
                total += nn(held_ref[n, 2, x, c], grad_ref[2 * BLOCK :])
                target[n, shift] = total.astype(BF16)
        return carried

    lax.fori_loop(0, count, one_step, 0)


def back_project(grad_proj, weight, steps):
    vmem = pl.BlockSpec(memory_space=pltpu.VMEM)
    count = len(steps)
    part = jax.ShapeDtypeStruct((count, 2, BLOCK, BLOCK), BF16)
    return pl.pallas_call(
        back_kernel,
        out_shape=(part, part),
        in_specs=[pl.BlockSpec(memory_space=pltpu.SMEM), vmem, pl.BlockSpec(memory_space=pltpu.HBM)],
        out_specs=(vmem, vmem),
        scratch_shapes=[
            pltpu.VMEM((count, 3, 2, 2, BLOCK, BLOCK), BF16),
            pltpu.SemaphoreType.DMA((count,)),
        ],
        compiler_params=pltpu.CompilerParams(vmem_limit_bytes=50 << 20),
        cost_estimate=pl.CostEstimate(
            flops=2 * 256 * 768 * 1024 * count, bytes_accessed=count << 21, transcendentals=0
        ),
        name="back_project",
    )(jnp.asarray(steps, jnp.int32), grad_proj, weight)


def project_features(rows, weight, tables):
    held = lax.all_to_all(
        jnp.broadcast_to(rows[None], (N_Z,) + rows.shape), "chan", 0, 0, axis_index_groups=Z_GROUPS
    )
    held, tables = lax.optimization_barrier((held, tables))
    beside = lax.ppermute(held, "chan", X_SWAP)
    across = lax.ppermute(held, "chan", CORE_SWAP)
    sums = project((0,), (held,), weight, None, False)
    beside, sums = lax.optimization_barrier((beside, sums))
    both = lax.ppermute(beside, "chan", CORE_SWAP)
    sums = project((2, 1), (across, beside), weight, sums, False)
    return project((3,), (both,), weight, sums, True), tables


def gather_ctx(value):
    across = lax.ppermute(value, "ctx", X_HALF_SWAP)
    found = [value, across]
    for piece in (value, across):
        found += [lax.ppermute(piece, "ctx", y_shift(by)) for by in Y_STEPS]
    return [found[n] for n in (0, 1, 2, 5, 3, 6, 4, 7)]


def gather_ctx_staged(value):
    pair = jnp.stack([value, lax.ppermute(value, "ctx", X_HALF_SWAP)])
    return [pair] + [lax.ppermute(pair, "ctx", y_shift(by)) for by in Y_STEPS]


def moved(value, by):
    return lax.ppermute(value.astype(BF16), "chan", z_shift(by)).astype(F32)


def reduce_chan(grad_proj, weight):
    terms = {}

    def add_terms(grad_proj, steps):
        own, other = back_project(grad_proj, weight, steps)
        swapped = lax.ppermute(other, "chan", CORE_SWAP)
        for n, step in enumerate(steps):
            for half in range(2):
                terms[step, half] = own[n, half].astype(F32) + swapped[n, half].astype(F32)

    add_terms(grad_proj, (4,))
    add_terms(grad_proj, (3, 5))
    far = [terms[4, half].astype(BF16) for half in range(2)]
    far, grad_proj = lax.optimization_barrier((far, grad_proj))
    add_terms(grad_proj, (2, 6, 1, 7, 0))
    totals = []
    for half, long, short in ((1, 1, -1), (0, -1, 1)):
        chain = {long: moved(far[half], long) + terms[(4 - long) % 8, half], short: terms[(4 - short) % 8, half]}
        for hop in (2, 1):
            for by in (long, short):
                chain[by] = moved(chain[by], by) + terms[(by * hop) % 8, half]
        totals.append(terms[0, half] + moved(chain[long], long) + moved(chain[short], short))
    far_half, near_half = totals
    total = near_half + lax.ppermute(far_half.astype(BF16), "chan", X_SWAP).astype(F32)
    return total.astype(BF16)


def body(token_ids, embed_table, in_weight, feat_taps, modal_rates, modal_residues, out_grad):
    weight = in_weight.transpose(1, 0, 2).reshape(3, 2, N_Z, 2, BLOCK, BLOCK)
    own_vocab = lax.dynamic_slice_in_dim(embed_table, lax.axis_index("ctx") * SHARE, SHARE, 0)
    grads = gather_ctx_staged(make_payload(out_grad, token_ids))
    gains = modal_residues * jnp.sqrt(-jnp.expm1(-2.0 * modal_rates))
    tables = make_tables(modal_rates, gains, feat_taps)
    part, tables = project_features(own_vocab, weight, tables)
    output, grad_proj = mix(gather_ctx(part), grads, tables)
    return (output, reduce_chan(grad_proj, weight).T)


def solution(mesh):
    in_specs = (
        P("ctx"),
        P(None, "chan"),
        P(None, None, "chan"),
        P(None, None, "chan"),
        P(None, "chan"),
        P(None, "chan"),
        P("ctx", "chan"),
    )
    out_specs = (P("ctx", "chan"), P("ctx", "chan"))
    return jax.shard_map(body, mesh=mesh, in_specs=in_specs, out_specs=out_specs, check_vma=False)
```

```python
import functools

import jax
import jax.numpy as jnp
from jax import lax
from jax.experimental import pallas as pl
from jax.experimental.pallas import tpu as pltpu
from jax.sharding import PartitionSpec as P

F32 = jnp.float32
BF16 = jnp.bfloat16
EXACT = lax.Precision.HIGHEST
N_CTX = 8
N_CHAN = 32
N_Z = 8
BLOCK = 256
GROUP = 16
ORDER = 16
GROUPS = BLOCK // GROUP
VOCAB = 512
SHARE = VOCAB // N_CTX
HALO = 128
EXTRA = 16
WINDOW = N_CTX * BLOCK

END = slice(0, BLOCK)
BEGIN = slice(BLOCK, 2 * BLOCK)
ENTER = slice(2 * BLOCK, 3 * BLOCK)
LEAVE = slice(3 * BLOCK, 4 * BLOCK + HALO)
SIDE = 4 * BLOCK + HALO

CORE_SWAP = [(i, i ^ 1) for i in range(N_CHAN)]
X_SWAP = [(i, i ^ 16) for i in range(N_CHAN)]
X_HALF_SWAP = [(i, i ^ 1) for i in range(N_CTX)]
Y_STEPS = (1, -1, 2)
Z_GROUPS = [[x * 16 + z * 2 + c for z in range(N_Z)] for x in range(2) for c in range(2)]


def z_shift(by):
    return [(i, (i & 16) | ((i + 2 * by) & 15)) for i in range(N_CHAN)]


def y_shift(by):
    return [(i, (i & 1) | ((i + 2 * by) & 7)) for i in range(N_CTX)]


def nn(a, b):
    return lax.dot_general(a, b, (((1,), (0,)), ((), ())), preferred_element_type=F32)


def nt(a, b):
    return lax.dot_general(a, b, (((1,), (1,)), ((), ())), preferred_element_type=F32)


def lanes_of(shape):
    return lax.broadcasted_iota(jnp.int32, shape, 1)


def place_of(axis):
    chan = lax.axis_index("chan")
    return {"x": chan // 16, "z": (chan // 2) & (N_Z - 1), "core": chan & 1}[axis]


def payload_kernel(grad_ref, token_ref, out_ref):
    out_ref[:BLOCK] = grad_ref[...].astype(F32).T.astype(BF16)
    tokens = token_ref[...]
    row = lax.broadcasted_iota(jnp.int32, (EXTRA, BLOCK), 0)
    ids = jnp.where(row == 0, tokens >> 8, jnp.where(row == 1, tokens & 255, 0))
    out_ref[BLOCK:] = ids.astype(F32).astype(BF16)


def make_payload(out_grad, token_ids):
    vmem = pl.BlockSpec(memory_space=pltpu.VMEM)
    return pl.pallas_call(
        payload_kernel,
        out_shape=jax.ShapeDtypeStruct((BLOCK + EXTRA, BLOCK), BF16),
        in_specs=[vmem] * 2,
        out_specs=vmem,
        compiler_params=pltpu.CompilerParams(vmem_limit_bytes=4 << 20),
        cost_estimate=pl.CostEstimate(flops=1 << 16, bytes_accessed=1 << 19, transcendentals=0),
        name="payload",
    )(out_grad, token_ids.reshape(1, BLOCK))


def table_kernel(
    rate_ref, gain_ref, tap_ref,
    fwd_ref, side_ref, row_ref, tap_out_ref,
):
    shape = (BLOCK, ORDER)
    mode = lax.broadcasted_iota(jnp.int32, shape, 0)
    group_pick = jnp.where(mode // ORDER == lanes_of(shape), 1.0, 0.0)
    order_pick = mode % ORDER == lanes_of(shape)
    shape = (ORDER, BLOCK)
    group_row = jnp.where(lanes_of(shape) // ORDER == lax.broadcasted_iota(jnp.int32, shape, 0), 1.0, 0.0)
    order_row = lanes_of(shape) % ORDER == lax.broadcasted_iota(jnp.int32, shape, 0)

    def column(values):
        spread = lax.dot_general(
            group_pick, values, (((1,), (1,)), ((), ())), precision=EXACT, preferred_element_type=F32
        )
        return jnp.sum(jnp.where(order_pick, spread, 0.0), axis=1, keepdims=True)

    def as_row(values):
        spread = lax.dot_general(
            values, group_row, (((1,), (0,)), ((), ())), precision=EXACT, preferred_element_type=F32
        )
        return jnp.sum(jnp.where(order_row, spread, 0.0), axis=0, keepdims=True)

    row_ref[0:1] = as_row(rate_ref[...])
    row_ref[1:2] = as_row(gain_ref[...])
    for s in range(3):
        tap_out_ref[s * BLOCK : (s + 1) * BLOCK, :] = tap_ref[s].T
    rates = column(rate_ref[...])
    gains = column(gain_ref[...])
    position = lanes_of((BLOCK, BLOCK)).astype(F32)
    decay = jnp.exp(-position * rates)
    growth = jnp.exp(position * rates)
    weighted = decay * gains
    side_ref[:, END] = jnp.exp((position - (BLOCK - 1.0)) * rates).astype(BF16)
    side_ref[:, BEGIN] = decay.astype(BF16)
    side_ref[:, ENTER] = (gains * jnp.exp(-(position + 1.0) * rates)).astype(BF16)
    wide = jnp.minimum(lanes_of((BLOCK, BLOCK + HALO)), BLOCK + 1).astype(F32)
    side_ref[:, LEAVE] = (gains * jnp.exp((wide - float(BLOCK)) * rates)).astype(BF16)
    row = lax.broadcasted_iota(jnp.int32, (BLOCK, BLOCK), 0)
    col = lanes_of((BLOCK, BLOCK))
    for g in range(GROUPS):
        rows = slice(g * ORDER, (g + 1) * ORDER)
        grown, scaled = growth[rows], weighted[rows]
        dims = (((0,), (0,)), ((), ()))
        later = lax.dot_general(grown, scaled, dims, precision=EXACT, preferred_element_type=F32)
        fwd_ref[g] = jnp.where(col >= row, later, 0.0).astype(BF16)


def make_tables(rates, gains, taps):
    stack = jax.ShapeDtypeStruct((GROUPS, BLOCK, BLOCK), BF16)
    side = jax.ShapeDtypeStruct((BLOCK, SIDE), BF16)
    rows = jax.ShapeDtypeStruct((2, BLOCK), F32)
    columns = jax.ShapeDtypeStruct((3 * BLOCK, 3), F32)
    vmem = pl.BlockSpec(memory_space=pltpu.VMEM)
    return pl.pallas_call(
        table_kernel,
        out_shape=(stack, side, rows, columns),
        in_specs=[vmem] * 3,
        out_specs=(vmem,) * 4,
        compiler_params=pltpu.CompilerParams(vmem_limit_bytes=8 << 20),
        cost_estimate=pl.CostEstimate(flops=6 * 64 * 2**20, bytes_accessed=5 << 20, transcendentals=1 << 19),
        name="filter_tables",
    )(rates, gains, taps)


def project_kernel(part, first, ready, ahead, *refs):
    row_ref, weight_ref, refs = refs[0], refs[1], refs[2:]
    sum_ref, refs = (None, refs) if first else (refs[0], refs[1:])
    out_ref, refs = refs[0], refs[1:]

    def fetch(part, target, sem):
        c, x = place_of("core") ^ (part // 2), place_of("x") ^ (part % 2)
        copy = pltpu.make_async_copy(weight_ref.at[:, x, :, c], target, sem)
        copy.start()
        return copy

    copies = []
    held = weight_ref
    if not ready:
        held, sems = refs[-2:]
        copies = [fetch(part, held, sems.at[0])]
        copies += [fetch(later, refs[n], sems.at[n + 1]) for n, later in enumerate(ahead)]
        copies[0].wait()
    total = tuple(
        jnp.zeros((SHARE, BLOCK), F32) if first else sum_ref[:, s * BLOCK : (s + 1) * BLOCK] for s in range(3)
    )

    def add_block(z, total):
        rows = row_ref[z]
        return tuple(total[s] + nn(rows, held[s, z]) for s in range(3))

    total = lax.fori_loop(0, N_Z, add_block, total, unroll=2)
    for s in range(3):
        out_ref[:, s * BLOCK : (s + 1) * BLOCK] = total[s].astype(out_ref.dtype)
    for copy in copies[1:]:
        copy.wait()


def project(part, rows, weight, sums=None, ready=False, ahead=(), last=False):
    vmem = pl.BlockSpec(memory_space=pltpu.VMEM)
    result = jax.ShapeDtypeStruct((SHARE, 3 * BLOCK), BF16 if last else F32)
    block = (3, N_Z, BLOCK, BLOCK)
    scratch = [pltpu.VMEM(block, BF16), pltpu.SemaphoreType.DMA((1 + len(ahead),))]
    earlier = [] if sums is None else [sums]
    return pl.pallas_call(
        functools.partial(project_kernel, part, sums is None, ready, ahead),
        out_shape=(result,) + (jax.ShapeDtypeStruct(block, BF16),) * len(ahead),
        in_specs=[vmem, vmem if ready else pl.BlockSpec(memory_space=pltpu.HBM)] + [vmem] * len(earlier),
        out_specs=(vmem,) * (1 + len(ahead)),
        scratch_shapes=[] if ready else scratch,
        compiler_params=pltpu.CompilerParams(vmem_limit_bytes=(4 if ready else 46) << 20),
        cost_estimate=pl.CostEstimate(
            flops=2 * 64 * 768 * 2048, bytes_accessed=(1 + len(ahead)) * (3 << 20), transcendentals=0
        ),
        name="project",
    )(rows, weight, *earlier)


def back_step(n, held_ref, grad_ref, own_ref, other_ref):
    for core in (1, 0):
        target = other_ref if core else own_ref
        c = place_of("core") ^ core
        for shift in range(2):
            x = place_of("x") ^ shift
            total = nn(held_ref[n, 0, x, c], grad_ref[0:BLOCK])
            total += nn(held_ref[n, 1, x, c], grad_ref[BLOCK : 2 * BLOCK])
            total += nn(held_ref[n, 2, x, c], grad_ref[2 * BLOCK :])
            target[n, shift] = total.astype(BF16)


def source_of(own, n):
    return ((own - 2 * ((0,) + Y_STEPS)[n // 2]) & 6) | ((own & 1) ^ (n % 2))


def mixer_kernel(*refs):
    own = lax.axis_index("ctx")
    table_refs, refs = refs[:N_CTX], refs[N_CTX:]
    sources, refs = refs[:7], refs[7:]
    row_ref, tap_ref, out_ref, grad_proj_ref, own_ref, other_ref = refs[:6]
    raw_ref, tapped_ref, id_ref, grad_ref, side_ref, fwd_ref, weight_ref, sems = refs[6:]
    copies = []
    for n in range(N_CTX):
        target = grad_ref.at[source_of(own, n)]
        copies.append(pltpu.make_async_copy(sources[n // 2].at[n % 2], target, sems.at[n]))
    copies.append(pltpu.make_async_copy(sources[4], side_ref, sems.at[N_CTX]))
    copies.append(pltpu.make_async_copy(sources[5], fwd_ref, sems.at[N_CTX + 1]))
    far_z = (place_of("z") + N_Z // 2) & (N_Z - 1)
    copies.append(pltpu.make_async_copy(sources[6].at[:, :, far_z], weight_ref.at[0], sems.at[N_CTX + 2]))
    for copy in copies:
        copy.start()
    table = jnp.concatenate([ref[...].astype(F32) for ref in table_refs], axis=0).T.astype(BF16)
    share_row = lax.broadcasted_iota(jnp.int32, (SHARE, BLOCK), 0)
    vocab = jnp.concatenate([share_row + source_of(own, n) * SHARE for n in range(N_CTX)], axis=0)
    table = jnp.concatenate([ref[...].astype(F32) for ref in table_refs], axis=0).T
    for tap in range(3):
        tapped_ref[:, tap * VOCAB : (tap + 1) * VOCAB] = (tap_ref[:, tap : tap + 1] * table).astype(BF16)
    table = table.astype(BF16)

    for copy in copies[:N_CTX]:
        copy.wait()
    edge = jnp.full((1, HALO), -1, jnp.int32)
    id_ref[:, :HALO] = edge
    id_ref[:, HALO + WINDOW :] = edge
    for block in range(N_CTX):
        ids = grad_ref[block, BLOCK : BLOCK + EXTRA, :].astype(F32)
        ids = (ids[0:1] * 256.0 + ids[1:2]).astype(jnp.int32)
        id_ref[:, HALO + block * BLOCK : HALO + (block + 1) * BLOCK] = ids
    copies[N_CTX].wait()

    def one_hot(ids):
        return jnp.where(ids == vocab, 1.0, 0.0).astype(BF16)

    def far_lookup(block):
        ids = id_ref[:, pl.ds(pl.multiple_of(block * BLOCK, BLOCK), HALO + BLOCK)]
        return jnp.concatenate([one_hot(ids[:, HALO - tap : HALO - tap + BLOCK]) for tap in range(3)], axis=0)

    def far_features(stream, picks):
        return nn(tapped_ref[stream * BLOCK : (stream + 1) * BLOCK, :], picks)

    for half in range(2):
        begin = pl.multiple_of(own * BLOCK + half * BLOCK, BLOCK)
        raw_ref[:, half * BLOCK : (half + 1) * BLOCK] = nn(table, one_hot(id_ref[:, pl.ds(begin, BLOCK)]))

    def featured(stream):
        rows = slice(stream * BLOCK, (stream + 1) * BLOCK)
        raw = raw_ref[rows, :]
        total = tap_ref[rows, 0:1] * raw[:, HALO:]
        for tap in (1, 2):
            total += tap_ref[rows, tap : tap + 1] * raw[:, HALO - tap : 2 * BLOCK - tap]
        return total

    rate_row = row_ref[0:1]
    gain_row = row_ref[1:2]
    block_decay = jnp.exp(rate_row * -float(BLOCK))
    same_group = (
        lax.broadcasted_iota(jnp.int32, (BLOCK, BLOCK), 0) // GROUP == lanes_of((BLOCK, BLOCK)) // ORDER
    )

    def earlier(block, state):
        picks = far_lookup(block)
        mixed = far_features(1, picks) * far_features(2, picks)
        return block_decay * state + nt(mixed.astype(BF16), side_ref[:, END])

    def later(step, state):
        block = N_CTX - 1 - step
        grad = grad_ref[block, 0:BLOCK, :].astype(F32) * far_features(0, far_lookup(block))
        return block_decay * state + nt(grad.astype(BF16), side_ref[:, BEGIN])

    zero = jnp.zeros((BLOCK, BLOCK), F32)
    before = lax.fori_loop(0, own, earlier, zero)
    after = lax.fori_loop(0, N_CTX - 1 - own, later, zero)

    wide = BLOCK + HALO
    query, key, value = featured(0), featured(1), featured(2)
    mixed = key * value
    following = jnp.minimum(own + 1, N_CTX - 1)
    grad_rows = jnp.concatenate(
        [grad_ref[own, 0:BLOCK, :], grad_ref[following, 0:BLOCK, 0:HALO]], axis=1
    ).astype(F32)
    grad_long = grad_rows * query
    mixed_own = mixed[:, :BLOCK].astype(BF16)
    long_own = grad_long[:, :BLOCK].astype(BF16)

    through = block_decay * before + nt(mixed_own, side_ref[:, END])
    before = jnp.where(same_group, before, 0.0).astype(BF16)
    through = jnp.where(same_group, through, 0.0).astype(BF16)
    after = jnp.where(same_group, after, 0.0).astype(BF16)

    copies[N_CTX + 1].wait()
    conv_rows, mixed_grads = [], []
    for g in range(GROUPS):
        rows = slice(g * GROUP, (g + 1) * GROUP)
        conv_rows.append(nn(mixed_own[rows], fwd_ref[g]))
        mixed_grads.append(nt(long_own[rows], fwd_ref[g]))
    conv = jnp.concatenate(conv_rows, axis=0) + nn(before, side_ref[:, ENTER])
    mixed_grad = jnp.concatenate(mixed_grads, axis=0) + nn(after, side_ref[:, LEAVE.start : LEAVE.start + BLOCK])

    def filter_at(lag):
        terms = jnp.where(same_group, gain_row * jnp.exp(rate_row * -float(lag)), 0.0)
        return jnp.sum(terms, axis=1, keepdims=True)

    second = lanes_of((BLOCK, HALO)) == 1
    conv_next = nn(through, side_ref[:, ENTER.start : ENTER.start + HALO]) + filter_at(0) * mixed[:, BLOCK:]
    conv_next += jnp.where(second, filter_at(1) * mixed[:, BLOCK - 1 : wide - 1], 0.0)
    grad_next = nn(after, side_ref[:, LEAVE.start + BLOCK :])
    grad_next -= jnp.where(second, filter_at(-1) * grad_long[:, BLOCK - 1 : wide - 1], 0.0)

    out_ref[...] = (query[:, :BLOCK] * conv).T.astype(BF16)

    conv = jnp.concatenate([conv, conv_next], axis=1)
    mixed_grad = jnp.concatenate([mixed_grad, grad_next], axis=1)
    lane = lanes_of((BLOCK, wide))
    inside = (lane < BLOCK) | ((lane < BLOCK + 2) & (own < N_CTX - 1))
    streams = (grad_rows * conv, mixed_grad * value, mixed_grad * key)
    for s in range(3):
        rows = slice(s * BLOCK, (s + 1) * BLOCK)
        grads = jnp.where(inside, streams[s], 0.0).astype(BF16).astype(F32)
        total = tap_ref[rows, 0:1] * grads[:, :BLOCK]
        for tap in (1, 2):
            total += tap_ref[rows, tap : tap + 1] * grads[:, tap : tap + BLOCK]
        grad_proj_ref[rows, :] = total.astype(BF16)
    copies[N_CTX + 2].wait()
    back_step(0, weight_ref, grad_proj_ref, own_ref, other_ref)


def mix(pieces, grads, tables, weight):
    fwd, side, row, taps = tables
    vmem = pl.BlockSpec(memory_space=pltpu.VMEM)
    return pl.pallas_call(
        mixer_kernel,
        out_shape=(
            jax.ShapeDtypeStruct((BLOCK, BLOCK), BF16),
            jax.ShapeDtypeStruct((3 * BLOCK, BLOCK), BF16),
            jax.ShapeDtypeStruct((1, 2, BLOCK, BLOCK), BF16),
            jax.ShapeDtypeStruct((1, 2, BLOCK, BLOCK), BF16),
        ),
        in_specs=[vmem] * N_CTX + [pl.BlockSpec(memory_space=pl.ANY)] * 7 + [vmem] * 2,
        out_specs=(vmem,) * 4,
        scratch_shapes=[
            pltpu.VMEM((3 * BLOCK, 2 * BLOCK), F32),
            pltpu.VMEM((3 * BLOCK, 3 * VOCAB), BF16),
            pltpu.VMEM((1, WINDOW + 2 * HALO), jnp.int32),
            pltpu.VMEM((N_CTX, BLOCK + EXTRA, BLOCK), BF16),
            pltpu.VMEM((BLOCK, SIDE), BF16),
            pltpu.VMEM((GROUPS, BLOCK, BLOCK), BF16),
            pltpu.VMEM((1, 3, 2, 2, BLOCK, BLOCK), BF16),
            pltpu.SemaphoreType.DMA((N_CTX + 3,)),
        ],
        compiler_params=pltpu.CompilerParams(vmem_limit_bytes=47 << 20),
        cost_estimate=pl.CostEstimate(flops=3 << 30, bytes_accessed=8 << 20, transcendentals=1 << 16),
        name="mixer",
    )(*pieces, *grads, side, fwd, weight, row, taps)


def back_kernel(step_ref, grad_ref, weight_ref, own_ref, other_ref, held_ref, sems):
    count = own_ref.shape[0]

    def copy(n):
        z = (place_of("z") + step_ref[n]) & (N_Z - 1)
        return pltpu.make_async_copy(weight_ref.at[:, :, z], held_ref.at[n], sems.at[n])

    for n in range(count):
        copy(n).start()

    def one_step(n, carried):
        copy(n).wait()
        back_step(n, held_ref, grad_ref, own_ref, other_ref)
        return carried

    lax.fori_loop(0, count, one_step, 0)


def back_project(grad_proj, weight, steps):
    vmem = pl.BlockSpec(memory_space=pltpu.VMEM)
    count = len(steps)
    part = jax.ShapeDtypeStruct((count, 2, BLOCK, BLOCK), BF16)
    return pl.pallas_call(
        back_kernel,
        out_shape=(part, part),
        in_specs=[pl.BlockSpec(memory_space=pltpu.SMEM), vmem, pl.BlockSpec(memory_space=pltpu.HBM)],
        out_specs=(vmem, vmem),
        scratch_shapes=[
            pltpu.VMEM((count, 3, 2, 2, BLOCK, BLOCK), BF16),
            pltpu.SemaphoreType.DMA((count,)),
        ],
        compiler_params=pltpu.CompilerParams(vmem_limit_bytes=50 << 20),
        cost_estimate=pl.CostEstimate(
            flops=2 * 256 * 768 * 1024 * count, bytes_accessed=count << 21, transcendentals=0
        ),
        name="back_project",
    )(jnp.asarray(steps, jnp.int32), grad_proj, weight)


def project_features(rows, weight, pair):
    held = lax.all_to_all(
        jnp.broadcast_to(rows[None], (N_Z,) + rows.shape), "chan", 0, 0, axis_index_groups=Z_GROUPS
    )
    held, pair = lax.optimization_barrier((held, pair))
    beside = lax.ppermute(held, "chan", X_SWAP)
    across = lax.ppermute(held, "chan", CORE_SWAP)
    sums, weight_beside, weight_both = project(0, held, weight, ahead=(1, 3))
    (sums,) = project(2, across, weight, sums)
    beside, sums = lax.optimization_barrier((beside, sums))
    both = lax.ppermute(beside, "chan", CORE_SWAP)
    (sums,) = project(1, beside, weight_beside, sums, ready=True)
    both, sums = lax.optimization_barrier((both, sums))
    (part,) = project(3, both, weight_both, sums, ready=True, last=True)
    return part, pair


def gather_ctx(value):
    across = lax.ppermute(value, "ctx", X_HALF_SWAP)
    found = [value, across]
    for piece in (value, across):
        found += [lax.ppermute(piece, "ctx", y_shift(by)) for by in Y_STEPS]
    return [found[n] for n in (0, 1, 2, 5, 3, 6, 4, 7)]


def pair_ctx(value):
    return jnp.stack([value, lax.ppermute(value, "ctx", X_HALF_SWAP)])


def gather_pairs(pair):
    return [pair] + [lax.ppermute(pair, "ctx", y_shift(by)) for by in Y_STEPS]


def moved(value, by):
    return lax.ppermute(value.astype(BF16), "chan", z_shift(by))


def reduce_chan(far_parts, grad_proj, weight):
    terms = {}

    def swap(parts):
        return parts[0], lax.ppermute(parts[1], "chan", CORE_SWAP)

    def add_terms(steps, own, swapped):
        for n, step in enumerate(steps):
            for half in range(2):
                terms[step, half] = own[n, half].astype(F32) + swapped[n, half].astype(F32)

    def arrive(values, tied):
        values, tied = lax.optimization_barrier((values, tied))
        return values, tied

    def send(values):
        return {(half, by): moved(value, by) for (half, by), value in values.items()}

    own, swapped = swap(far_parts)
    near = back_project(grad_proj, weight, (3, 5))
    (swapped, near) = lax.optimization_barrier((swapped, near))
    add_terms((4,), own, swapped)
    ways = {1: (1, -1), 0: (-1, 1)}
    chain = send({(half, ways[half][0]): terms[4, half] for half in (1, 0)})
    grad_proj, near = lax.optimization_barrier((grad_proj, near))
    near_own, near_swapped = swap(near)
    middle = back_project(grad_proj, weight, (2, 6))
    arrived, middle = arrive(chain, middle)
    add_terms((3, 5), near_own, near_swapped)
    middle_own, middle_swapped = swap(middle)
    chain = {}
    for half in (1, 0):
        long, short = ways[half]
        chain[half, long] = terms[(3 * long) % 8, half] + arrived[half, long].astype(F32)
        chain[half, short] = terms[(3 * short) % 8, half]
    chain = send(chain)
    grad_proj, middle_own = lax.optimization_barrier((grad_proj, middle_own))
    last = back_project(grad_proj, weight, (1, 7, 0))
    arrived, last = arrive(chain, last)
    add_terms((2, 6), middle_own, middle_swapped)
    last_own, last_swapped = swap(last)
    chain = send({(half, by): value.astype(F32) + terms[(2 * by) % 8, half] for (half, by), value in arrived.items()})
    add_terms((1, 7, 0), last_own, last_swapped)
    chain = send({(half, by): value.astype(F32) + terms[by % 8, half] for (half, by), value in chain.items()})
    far_half, near_half = (
        terms[0, half] + chain[half, 1].astype(F32) + chain[half, -1].astype(F32) for half in (1, 0)
    )
    total = near_half + lax.ppermute(far_half.astype(BF16), "chan", X_SWAP).astype(F32)
    return total.astype(BF16)


def body(token_ids, embed_table, in_weight, feat_taps, modal_rates, modal_residues, out_grad):
    weight = in_weight.transpose(1, 0, 2).reshape(3, 2, N_Z, 2, BLOCK, BLOCK)
    own_vocab = lax.dynamic_slice_in_dim(embed_table, lax.axis_index("ctx") * SHARE, SHARE, 0)
    pair = pair_ctx(make_payload(out_grad, token_ids))
    part, pair = project_features(own_vocab, weight, pair)
    grads = gather_pairs(pair)
    modal_rates, part = lax.optimization_barrier((modal_rates, part))
    pieces = gather_ctx(part)
    gains = modal_residues * jnp.sqrt(-jnp.expm1(-2.0 * modal_rates))
    tables = make_tables(modal_rates, gains, feat_taps)
    output, grad_proj, *far_parts = mix(pieces, grads, tables, weight)
    return (output, reduce_chan(far_parts, grad_proj, weight).T)


def solution(mesh):
    in_specs = (
        P("ctx"),
        P(None, "chan"),
        P(None, None, "chan"),
        P(None, None, "chan"),
        P(None, "chan"),
        P(None, "chan"),
        P("ctx", "chan"),
    )
    out_specs = (P("ctx", "chan"), P("ctx", "chan"))
    return jax.shard_map(body, mesh=mesh, in_specs=in_specs, out_specs=out_specs, check_vma=False)
```

```python
import functools

import jax
import jax.numpy as jnp
from jax import lax
from jax.experimental import pallas as pl
from jax.experimental.pallas import tpu as pltpu
from jax.sharding import PartitionSpec as P

F32 = jnp.float32
BF16 = jnp.bfloat16
EXACT = lax.Precision.HIGHEST
N_CTX = 8
N_CHAN = 32
N_Z = 8
BLOCK = 256
GROUP = 16
ORDER = 16
GROUPS = BLOCK // GROUP
VOCAB = 512
SHARE = VOCAB // N_CTX
HALO = 128
EXTRA = 16
WINDOW = N_CTX * BLOCK

END = slice(0, BLOCK)
BEGIN = slice(BLOCK, 2 * BLOCK)
ENTER = slice(2 * BLOCK, 3 * BLOCK)
LEAVE = slice(3 * BLOCK, 4 * BLOCK + HALO)
SIDE = 4 * BLOCK + HALO

CORE_SWAP = [(i, i ^ 1) for i in range(N_CHAN)]
X_SWAP = [(i, i ^ 16) for i in range(N_CHAN)]
X_HALF_SWAP = [(i, i ^ 1) for i in range(N_CTX)]
Y_STEPS = (1, -1, 2)
Z_GROUPS = [[x * 16 + z * 2 + c for z in range(N_Z)] for x in range(2) for c in range(2)]


def z_shift(by):
    return [(i, (i & 16) | ((i + 2 * by) & 15)) for i in range(N_CHAN)]


def y_shift(by):
    return [(i, (i & 1) | ((i + 2 * by) & 7)) for i in range(N_CTX)]


def nn(a, b):
    return lax.dot_general(a, b, (((1,), (0,)), ((), ())), preferred_element_type=F32)


def nt(a, b):
    return lax.dot_general(a, b, (((1,), (1,)), ((), ())), preferred_element_type=F32)


def lanes_of(shape):
    return lax.broadcasted_iota(jnp.int32, shape, 1)


def place_of(axis):
    chan = lax.axis_index("chan")
    return {"x": chan // 16, "z": (chan // 2) & (N_Z - 1), "core": chan & 1}[axis]


def payload_kernel(grad_ref, token_ref, out_ref):
    out_ref[:BLOCK] = grad_ref[...].astype(F32).T.astype(BF16)
    tokens = token_ref[...]
    row = lax.broadcasted_iota(jnp.int32, (EXTRA, BLOCK), 0)
    ids = jnp.where(row == 0, tokens >> 8, jnp.where(row == 1, tokens & 255, 0))
    out_ref[BLOCK:] = ids.astype(F32).astype(BF16)


def make_payload(out_grad, token_ids):
    vmem = pl.BlockSpec(memory_space=pltpu.VMEM)
    return pl.pallas_call(
        payload_kernel,
        out_shape=jax.ShapeDtypeStruct((BLOCK + EXTRA, BLOCK), BF16),
        in_specs=[vmem] * 2,
        out_specs=vmem,
        compiler_params=pltpu.CompilerParams(vmem_limit_bytes=4 << 20),
        cost_estimate=pl.CostEstimate(flops=1 << 16, bytes_accessed=1 << 19, transcendentals=0),
        name="payload",
    )(out_grad, token_ids.reshape(1, BLOCK))


def table_kernel(
    rate_ref, gain_ref, tap_ref,
    fwd_ref, side_ref, row_ref, tap_out_ref,
):
    shape = (BLOCK, ORDER)
    mode = lax.broadcasted_iota(jnp.int32, shape, 0)
    group_pick = jnp.where(mode // ORDER == lanes_of(shape), 1.0, 0.0)
    order_pick = mode % ORDER == lanes_of(shape)
    shape = (ORDER, BLOCK)
    group_row = jnp.where(lanes_of(shape) // ORDER == lax.broadcasted_iota(jnp.int32, shape, 0), 1.0, 0.0)
    order_row = lanes_of(shape) % ORDER == lax.broadcasted_iota(jnp.int32, shape, 0)

    def column(values):
        spread = lax.dot_general(
            group_pick, values, (((1,), (1,)), ((), ())), precision=EXACT, preferred_element_type=F32
        )
        return jnp.sum(jnp.where(order_pick, spread, 0.0), axis=1, keepdims=True)

    def as_row(values):
        spread = lax.dot_general(
            values, group_row, (((1,), (0,)), ((), ())), precision=EXACT, preferred_element_type=F32
        )
        return jnp.sum(jnp.where(order_row, spread, 0.0), axis=0, keepdims=True)

    row_ref[0:1] = as_row(rate_ref[...])
    row_ref[1:2] = as_row(gain_ref[...])
    for s in range(3):
        tap_out_ref[s * BLOCK : (s + 1) * BLOCK, :] = tap_ref[s].T
    rates = column(rate_ref[...])
    gains = column(gain_ref[...])
    position = lanes_of((BLOCK, BLOCK)).astype(F32)
    decay = jnp.exp(-position * rates)
    growth = jnp.exp(position * rates)
    weighted = decay * gains
    side_ref[:, END] = jnp.exp((position - (BLOCK - 1.0)) * rates).astype(BF16)
    side_ref[:, BEGIN] = decay.astype(BF16)
    side_ref[:, ENTER] = (gains * jnp.exp(-(position + 1.0) * rates)).astype(BF16)
    wide = jnp.minimum(lanes_of((BLOCK, BLOCK + HALO)), BLOCK + 1).astype(F32)
    side_ref[:, LEAVE] = (gains * jnp.exp((wide - float(BLOCK)) * rates)).astype(BF16)
    row = lax.broadcasted_iota(jnp.int32, (BLOCK, BLOCK), 0)
    col = lanes_of((BLOCK, BLOCK))
    for g in range(GROUPS):
        rows = slice(g * ORDER, (g + 1) * ORDER)
        grown, scaled = growth[rows], weighted[rows]
        dims = (((0,), (0,)), ((), ()))
        later = lax.dot_general(grown, scaled, dims, precision=EXACT, preferred_element_type=F32)
        fwd_ref[g] = jnp.where(col >= row, later, 0.0).astype(BF16)


def make_tables(rates, gains, taps):
    stack = jax.ShapeDtypeStruct((GROUPS, BLOCK, BLOCK), BF16)
    side = jax.ShapeDtypeStruct((BLOCK, SIDE), BF16)
    rows = jax.ShapeDtypeStruct((2, BLOCK), F32)
    columns = jax.ShapeDtypeStruct((3 * BLOCK, 3), F32)
    vmem = pl.BlockSpec(memory_space=pltpu.VMEM)
    return pl.pallas_call(
        table_kernel,
        out_shape=(stack, side, rows, columns),
        in_specs=[vmem] * 3,
        out_specs=(vmem,) * 4,
        compiler_params=pltpu.CompilerParams(vmem_limit_bytes=8 << 20),
        cost_estimate=pl.CostEstimate(flops=6 * 64 * 2**20, bytes_accessed=5 << 20, transcendentals=1 << 19),
        name="filter_tables",
    )(rates, gains, taps)


def project_kernel(part, first, ready, ahead, *refs):
    row_ref, weight_ref, refs = refs[0], refs[1], refs[2:]
    sum_ref, refs = (None, refs) if first else (refs[0], refs[1:])
    out_ref, refs = refs[0], refs[1:]

    def fetch(part, target, sem):
        c, x = place_of("core") ^ (part // 2), place_of("x") ^ (part % 2)
        copy = pltpu.make_async_copy(weight_ref.at[:, x, :, c], target, sem)
        copy.start()
        return copy

    copies = []
    held = weight_ref
    if not ready:
        held, sems = refs[-2:]
        copies = [fetch(part, held, sems.at[0])]
        copies += [fetch(later, refs[n], sems.at[n + 1]) for n, later in enumerate(ahead)]
        copies[0].wait()
    total = tuple(
        jnp.zeros((SHARE, BLOCK), F32) if first else sum_ref[:, s * BLOCK : (s + 1) * BLOCK] for s in range(3)
    )

    def add_block(z, total):
        rows = row_ref[z]
        return tuple(total[s] + nn(rows, held[s, z]) for s in range(3))

    total = lax.fori_loop(0, N_Z, add_block, total, unroll=2)
    for s in range(3):
        out_ref[:, s * BLOCK : (s + 1) * BLOCK] = total[s].astype(out_ref.dtype)
    for copy in copies[1:]:
        copy.wait()


def project(part, rows, weight, sums=None, ready=False, ahead=(), last=False):
    vmem = pl.BlockSpec(memory_space=pltpu.VMEM)
    result = jax.ShapeDtypeStruct((SHARE, 3 * BLOCK), BF16 if last else F32)
    block = (3, N_Z, BLOCK, BLOCK)
    scratch = [pltpu.VMEM(block, BF16), pltpu.SemaphoreType.DMA((1 + len(ahead),))]
    earlier = [] if sums is None else [sums]
    return pl.pallas_call(
        functools.partial(project_kernel, part, sums is None, ready, ahead),
        out_shape=(result,) + (jax.ShapeDtypeStruct(block, BF16),) * len(ahead),
        in_specs=[vmem, vmem if ready else pl.BlockSpec(memory_space=pltpu.HBM)] + [vmem] * len(earlier),
        out_specs=(vmem,) * (1 + len(ahead)),
        scratch_shapes=[] if ready else scratch,
        compiler_params=pltpu.CompilerParams(vmem_limit_bytes=(4 if ready else 46) << 20),
        cost_estimate=pl.CostEstimate(
            flops=2 * 64 * 768 * 2048, bytes_accessed=(1 + len(ahead)) * (3 << 20), transcendentals=0
        ),
        name="project",
    )(rows, weight, *earlier)


def back_step(n, held_ref, grad_ref, own_ref, other_ref):
    for core in (1, 0):
        target = other_ref if core else own_ref
        c = place_of("core") ^ core
        for shift in range(2):
            x = place_of("x") ^ shift
            total = nn(held_ref[n, 0, x, c], grad_ref[0:BLOCK])
            total += nn(held_ref[n, 1, x, c], grad_ref[BLOCK : 2 * BLOCK])
            total += nn(held_ref[n, 2, x, c], grad_ref[2 * BLOCK :])
            target[n, shift] = total.astype(BF16)


def source_of(own, n):
    return ((own - 2 * ((0,) + Y_STEPS)[n // 2]) & 6) | ((own & 1) ^ (n % 2))


def mixer_kernel(*refs):
    own = lax.axis_index("ctx")
    table_refs, refs = refs[:N_CTX], refs[N_CTX:]
    sources, refs = refs[:7], refs[7:]
    row_ref, tap_ref, out_ref, grad_proj_ref, own_ref, other_ref = refs[:6]
    raw_ref, tapped_ref, id_ref, grad_ref, side_ref, fwd_ref, weight_ref, sems = refs[6:]
    copies = []
    for n in range(N_CTX):
        target = grad_ref.at[source_of(own, n)]
        copies.append(pltpu.make_async_copy(sources[n // 2].at[n % 2], target, sems.at[n]))
    copies.append(pltpu.make_async_copy(sources[4], side_ref, sems.at[N_CTX]))
    copies.append(pltpu.make_async_copy(sources[5], fwd_ref, sems.at[N_CTX + 1]))
    far_z = (place_of("z") + N_Z // 2) & (N_Z - 1)
    copies.append(pltpu.make_async_copy(sources[6].at[:, :, far_z], weight_ref.at[0], sems.at[N_CTX + 2]))
    for copy in copies:
        copy.start()
    table = jnp.concatenate([ref[...].astype(F32) for ref in table_refs], axis=0).T.astype(BF16)
    table = jnp.concatenate([ref[...].astype(F32) for ref in table_refs], axis=0).T
    for tap in range(3):
        tapped_ref[:, tap * VOCAB : (tap + 1) * VOCAB] = (tap_ref[:, tap : tap + 1] * table).astype(BF16)
    table = table.astype(BF16)

    for copy in copies[:N_CTX]:
        copy.wait()
    edge = jnp.full((1, HALO), -1, jnp.int32)
    id_ref[:, :HALO] = edge
    id_ref[:, HALO + WINDOW :] = edge
    for block in range(N_CTX):
        ids = grad_ref[block, BLOCK : BLOCK + EXTRA, :].astype(F32)
        ids = (ids[0:1] * 256.0 + ids[1:2]).astype(jnp.int32)
        id_ref[:, HALO + block * BLOCK : HALO + (block + 1) * BLOCK] = ids
    copies[N_CTX].wait()

    tile_rows = [(lax.broadcasted_iota(jnp.int32, (16, BLOCK), 0) + 16 * n).astype(F32).astype(BF16) for n in range(SHARE // 16)]
    one, none = jnp.ones((16, BLOCK), BF16), jnp.zeros((16, BLOCK), BF16)

    def one_hot(ids):
        share, row = ids >> 6, (ids & (SHARE - 1)).astype(F32)
        tiles = []
        for n in range(N_CTX):
            rows = jnp.where(share == source_of(own, n), row, -1.0)
            rows = jnp.broadcast_to(rows, (16, BLOCK)).astype(BF16)
            tiles += [jnp.where(rows == tile, one, none) for tile in tile_rows]
        return jnp.concatenate(tiles, axis=0)

    def far_lookup(block):
        ids = id_ref[:, pl.ds(pl.multiple_of(block * BLOCK, BLOCK), HALO + BLOCK)]
        return jnp.concatenate([one_hot(ids[:, HALO - tap : HALO - tap + BLOCK]) for tap in range(3)], axis=0)

    def far_features(stream, picks):
        return nn(tapped_ref[stream * BLOCK : (stream + 1) * BLOCK, :], picks)

    for half in range(2):
        begin = pl.multiple_of(own * BLOCK + half * BLOCK, BLOCK)
        raw_ref[:, half * BLOCK : (half + 1) * BLOCK] = nn(table, one_hot(id_ref[:, pl.ds(begin, BLOCK)]))

    def featured(stream):
        rows = slice(stream * BLOCK, (stream + 1) * BLOCK)
        raw = raw_ref[rows, :]
        total = tap_ref[rows, 0:1] * raw[:, HALO:]
        for tap in (1, 2):
            total += tap_ref[rows, tap : tap + 1] * raw[:, HALO - tap : 2 * BLOCK - tap]
        return total

    rate_row = row_ref[0:1]
    gain_row = row_ref[1:2]
    block_decay = jnp.exp(rate_row * -float(BLOCK))
    same_group = (
        lax.broadcasted_iota(jnp.int32, (BLOCK, BLOCK), 0) // GROUP == lanes_of((BLOCK, BLOCK)) // ORDER
    )

    def earlier(block, state):
        picks = far_lookup(block)
        mixed = far_features(1, picks) * far_features(2, picks)
        return block_decay * state + nt(mixed.astype(BF16), side_ref[:, END])

    def later(step, state):
        block = N_CTX - 1 - step
        grad = grad_ref[block, 0:BLOCK, :].astype(F32) * far_features(0, far_lookup(block))
        return block_decay * state + nt(grad.astype(BF16), side_ref[:, BEGIN])

    zero = jnp.zeros((BLOCK, BLOCK), F32)
    before = lax.fori_loop(0, own, earlier, zero)
    after = lax.fori_loop(0, N_CTX - 1 - own, later, zero)

    wide = BLOCK + HALO
    query, key, value = featured(0), featured(1), featured(2)
    mixed = key * value
    following = jnp.minimum(own + 1, N_CTX - 1)
    grad_rows = jnp.concatenate(
        [grad_ref[own, 0:BLOCK, :], grad_ref[following, 0:BLOCK, 0:HALO]], axis=1
    ).astype(F32)
    grad_long = grad_rows * query
    mixed_own = mixed[:, :BLOCK].astype(BF16)
    long_own = grad_long[:, :BLOCK].astype(BF16)

    through = block_decay * before + nt(mixed_own, side_ref[:, END])
    before = jnp.where(same_group, before, 0.0).astype(BF16)
    through = jnp.where(same_group, through, 0.0).astype(BF16)
    after = jnp.where(same_group, after, 0.0).astype(BF16)

    copies[N_CTX + 1].wait()
    conv_rows, mixed_grads = [], []
    for g in range(GROUPS):
        rows = slice(g * GROUP, (g + 1) * GROUP)
        conv_rows.append(nn(mixed_own[rows], fwd_ref[g]))
        mixed_grads.append(nt(long_own[rows], fwd_ref[g]))
    conv = jnp.concatenate(conv_rows, axis=0) + nn(before, side_ref[:, ENTER])
    mixed_grad = jnp.concatenate(mixed_grads, axis=0) + nn(after, side_ref[:, LEAVE.start : LEAVE.start + BLOCK])

    def filter_at(lag):
        terms = jnp.where(same_group, gain_row * jnp.exp(rate_row * -float(lag)), 0.0)
        return jnp.sum(terms, axis=1, keepdims=True)

    second = lanes_of((BLOCK, HALO)) == 1
    conv_next = nn(through, side_ref[:, ENTER.start : ENTER.start + HALO]) + filter_at(0) * mixed[:, BLOCK:]
    conv_next += jnp.where(second, filter_at(1) * mixed[:, BLOCK - 1 : wide - 1], 0.0)
    grad_next = nn(after, side_ref[:, LEAVE.start + BLOCK :])
    grad_next -= jnp.where(second, filter_at(-1) * grad_long[:, BLOCK - 1 : wide - 1], 0.0)

    out_ref[...] = (query[:, :BLOCK] * conv).T.astype(BF16)

    conv = jnp.concatenate([conv, conv_next], axis=1)
    mixed_grad = jnp.concatenate([mixed_grad, grad_next], axis=1)
    lane = lanes_of((BLOCK, wide))
    inside = (lane < BLOCK) | ((lane < BLOCK + 2) & (own < N_CTX - 1))
    streams = (grad_rows * conv, mixed_grad * value, mixed_grad * key)
    for s in range(3):
        rows = slice(s * BLOCK, (s + 1) * BLOCK)
        grads = jnp.where(inside, streams[s], 0.0).astype(BF16).astype(F32)
        total = tap_ref[rows, 0:1] * grads[:, :BLOCK]
        for tap in (1, 2):
            total += tap_ref[rows, tap : tap + 1] * grads[:, tap : tap + BLOCK]
        grad_proj_ref[rows, :] = total.astype(BF16)
    copies[N_CTX + 2].wait()
    back_step(0, weight_ref, grad_proj_ref, own_ref, other_ref)


def mix(pieces, grads, tables, weight):
    fwd, side, row, taps = tables
    vmem = pl.BlockSpec(memory_space=pltpu.VMEM)
    return pl.pallas_call(
        mixer_kernel,
        out_shape=(
            jax.ShapeDtypeStruct((BLOCK, BLOCK), BF16),
            jax.ShapeDtypeStruct((3 * BLOCK, BLOCK), BF16),
            jax.ShapeDtypeStruct((1, 2, BLOCK, BLOCK), BF16),
            jax.ShapeDtypeStruct((1, 2, BLOCK, BLOCK), BF16),
        ),
        in_specs=[vmem] * N_CTX + [pl.BlockSpec(memory_space=pl.ANY)] * 7 + [vmem] * 2,
        out_specs=(vmem,) * 4,
        scratch_shapes=[
            pltpu.VMEM((3 * BLOCK, 2 * BLOCK), F32),
            pltpu.VMEM((3 * BLOCK, 3 * VOCAB), BF16),
            pltpu.VMEM((1, WINDOW + 2 * HALO), jnp.int32),
            pltpu.VMEM((N_CTX, BLOCK + EXTRA, BLOCK), BF16),
            pltpu.VMEM((BLOCK, SIDE), BF16),
            pltpu.VMEM((GROUPS, BLOCK, BLOCK), BF16),
            pltpu.VMEM((1, 3, 2, 2, BLOCK, BLOCK), BF16),
            pltpu.SemaphoreType.DMA((N_CTX + 3,)),
        ],
        compiler_params=pltpu.CompilerParams(vmem_limit_bytes=47 << 20),
        cost_estimate=pl.CostEstimate(flops=3 << 30, bytes_accessed=8 << 20, transcendentals=1 << 16),
        name="mixer",
    )(*pieces, *grads, side, fwd, weight, row, taps)


def back_kernel(step_ref, grad_ref, weight_ref, own_ref, other_ref, held_ref, sems):
    count = own_ref.shape[0]

    def copy(n):
        z = (place_of("z") + step_ref[n]) & (N_Z - 1)
        return pltpu.make_async_copy(weight_ref.at[:, :, z], held_ref.at[n], sems.at[n])

    for n in range(count):
        copy(n).start()

    def one_step(n, carried):
        copy(n).wait()
        back_step(n, held_ref, grad_ref, own_ref, other_ref)
        return carried

    lax.fori_loop(0, count, one_step, 0)


def back_project(grad_proj, weight, steps):
    vmem = pl.BlockSpec(memory_space=pltpu.VMEM)
    count = len(steps)
    part = jax.ShapeDtypeStruct((count, 2, BLOCK, BLOCK), BF16)
    return pl.pallas_call(
        back_kernel,
        out_shape=(part, part),
        in_specs=[pl.BlockSpec(memory_space=pltpu.SMEM), vmem, pl.BlockSpec(memory_space=pltpu.HBM)],
        out_specs=(vmem, vmem),
        scratch_shapes=[
            pltpu.VMEM((count, 3, 2, 2, BLOCK, BLOCK), BF16),
            pltpu.SemaphoreType.DMA((count,)),
        ],
        compiler_params=pltpu.CompilerParams(vmem_limit_bytes=50 << 20),
        cost_estimate=pl.CostEstimate(
            flops=2 * 256 * 768 * 1024 * count, bytes_accessed=count << 21, transcendentals=0
        ),
        name="back_project",
    )(jnp.asarray(steps, jnp.int32), grad_proj, weight)


def project_features(rows, weight, pair):
    held = lax.all_to_all(
        jnp.broadcast_to(rows[None], (N_Z,) + rows.shape), "chan", 0, 0, axis_index_groups=Z_GROUPS
    )
    beside = lax.ppermute(held, "chan", X_SWAP)
    across = lax.ppermute(held, "chan", CORE_SWAP)
    held, pair = lax.optimization_barrier((held, pair))
    grads = gather_pairs(pair)
    sums, weight_beside, weight_both = project(0, held, weight, ahead=(1, 3))
    (sums,) = project(2, across, weight, sums)
    beside, sums = lax.optimization_barrier((beside, sums))
    both = lax.ppermute(beside, "chan", CORE_SWAP)
    (sums,) = project(1, beside, weight_beside, sums, ready=True)
    both, sums, grads = lax.optimization_barrier((both, sums, grads))
    (part,) = project(3, both, weight_both, sums, ready=True, last=True)
    return part, grads


def gather_ctx(value):
    across = lax.ppermute(value, "ctx", X_HALF_SWAP)
    found = [value, across]
    for piece in (value, across):
        found += [lax.ppermute(piece, "ctx", y_shift(by)) for by in Y_STEPS]
    return [found[n] for n in (0, 1, 2, 5, 3, 6, 4, 7)]


def pair_ctx(value):
    return jnp.stack([value, lax.ppermute(value, "ctx", X_HALF_SWAP)])


def gather_pairs(pair):
    return [pair] + [lax.ppermute(pair, "ctx", y_shift(by)) for by in Y_STEPS]


def moved(value, by):
    return lax.ppermute(value.astype(BF16), "chan", z_shift(by))


def reduce_chan(far_parts, grad_proj, weight):
    terms = {}

    def swap(parts):
        return parts[0], lax.ppermute(parts[1], "chan", CORE_SWAP)

    def add_terms(steps, own, swapped):
        for n, step in enumerate(steps):
            for half in range(2):
                terms[step, half] = own[n, half].astype(F32) + swapped[n, half].astype(F32)

    def arrive(values, tied):
        values, tied = lax.optimization_barrier((values, tied))
        return values, tied

    def send(values):
        return {(half, by): moved(value, by) for (half, by), value in values.items()}

    own, swapped = swap(far_parts)
    near = back_project(grad_proj, weight, (3, 5))
    (swapped, near) = lax.optimization_barrier((swapped, near))
    add_terms((4,), own, swapped)
    ways = {1: (1, -1), 0: (-1, 1)}
    chain = send({(half, ways[half][0]): terms[4, half] for half in (1, 0)})
    grad_proj, near = lax.optimization_barrier((grad_proj, near))
    near_own, near_swapped = swap(near)
    middle = back_project(grad_proj, weight, (2, 6))
    arrived, middle = arrive(chain, middle)
    add_terms((3, 5), near_own, near_swapped)
    middle_own, middle_swapped = swap(middle)
    chain = {}
    for half in (1, 0):
        long, short = ways[half]
        chain[half, long] = terms[(3 * long) % 8, half] + arrived[half, long].astype(F32)
        chain[half, short] = terms[(3 * short) % 8, half]
    chain = send(chain)
    grad_proj, middle_own = lax.optimization_barrier((grad_proj, middle_own))
    last = back_project(grad_proj, weight, (1, 7, 0))
    arrived, last = arrive(chain, last)
    add_terms((2, 6), middle_own, middle_swapped)
    last_own, last_swapped = swap(last)
    chain = send({(half, by): value.astype(F32) + terms[(2 * by) % 8, half] for (half, by), value in arrived.items()})
    add_terms((1, 7, 0), last_own, last_swapped)
    chain = send({(half, by): value.astype(F32) + terms[by % 8, half] for (half, by), value in chain.items()})
    far_half, near_half = (
        terms[0, half] + chain[half, 1].astype(F32) + chain[half, -1].astype(F32) for half in (1, 0)
    )
    total = near_half + lax.ppermute(far_half.astype(BF16), "chan", X_SWAP).astype(F32)
    return total.astype(BF16)


def body(token_ids, embed_table, in_weight, feat_taps, modal_rates, modal_residues, out_grad):
    weight = in_weight.transpose(1, 0, 2).reshape(3, 2, N_Z, 2, BLOCK, BLOCK)
    own_vocab = lax.dynamic_slice_in_dim(embed_table, lax.axis_index("ctx") * SHARE, SHARE, 0)
    pair = pair_ctx(make_payload(out_grad, token_ids))
    part, grads = project_features(own_vocab, weight, pair)
    modal_rates, part = lax.optimization_barrier((modal_rates, part))
    pieces = gather_ctx(part)
    gains = modal_residues * jnp.sqrt(-jnp.expm1(-2.0 * modal_rates))
    tables = make_tables(modal_rates, gains, feat_taps)
    output, grad_proj, *far_parts = mix(pieces, grads, tables, weight)
    return (output, reduce_chan(far_parts, grad_proj, weight).T)


def solution(mesh):
    in_specs = (
        P("ctx"),
        P(None, "chan"),
        P(None, None, "chan"),
        P(None, None, "chan"),
        P(None, "chan"),
        P(None, "chan"),
        P("ctx", "chan"),
    )
    out_specs = (P("ctx", "chan"), P("ctx", "chan"))
    return jax.shard_map(body, mesh=mesh, in_specs=in_specs, out_specs=out_specs, check_vma=False)
```

```python
import functools

import jax
import jax.numpy as jnp
from jax import lax
from jax.experimental import pallas as pl
from jax.experimental.pallas import tpu as pltpu
from jax.sharding import PartitionSpec as P

F32 = jnp.float32
BF16 = jnp.bfloat16
EXACT = lax.Precision.HIGHEST
N_CTX = 8
N_CHAN = 32
N_Z = 8
BLOCK = 256
GROUP = 16
ORDER = 16
GROUPS = BLOCK // GROUP
VOCAB = 512
SHARE = VOCAB // N_CTX
HALO = 128
EXTRA = 16
WINDOW = N_CTX * BLOCK

END = slice(0, BLOCK)
BEGIN = slice(BLOCK, 2 * BLOCK)
ENTER = slice(2 * BLOCK, 3 * BLOCK)
LEAVE = slice(3 * BLOCK, 4 * BLOCK + HALO)
SIDE = 4 * BLOCK + HALO

CORE_SWAP = [(i, i ^ 1) for i in range(N_CHAN)]
X_SWAP = [(i, i ^ 16) for i in range(N_CHAN)]
FAR_STEPS = (4, 3, 5)
NEAR_STEPS = (2, 6, 1, 7, 0)
X_HALF_SWAP = [(i, i ^ 1) for i in range(N_CTX)]
Y_STEPS = (1, -1, 2)
Z_GROUPS = [[x * 16 + z * 2 + c for z in range(N_Z)] for x in range(2) for c in range(2)]


def z_shift(by):
    return [(i, (i & 16) | ((i + 2 * by) & 15)) for i in range(N_CHAN)]


def y_shift(by):
    return [(i, (i & 1) | ((i + 2 * by) & 7)) for i in range(N_CTX)]


def nn(a, b):
    return lax.dot_general(a, b, (((1,), (0,)), ((), ())), preferred_element_type=F32)


def nt(a, b):
    return lax.dot_general(a, b, (((1,), (1,)), ((), ())), preferred_element_type=F32)


def lanes_of(shape):
    return lax.broadcasted_iota(jnp.int32, shape, 1)


def place_of(axis):
    chan = lax.axis_index("chan")
    return {"x": chan // 16, "z": (chan // 2) & (N_Z - 1), "core": chan & 1}[axis]


def payload_kernel(grad_ref, token_ref, out_ref):
    out_ref[:BLOCK] = grad_ref[...].astype(F32).T.astype(BF16)
    tokens = token_ref[...]
    row = lax.broadcasted_iota(jnp.int32, (EXTRA, BLOCK), 0)
    ids = jnp.where(row == 0, tokens >> 8, jnp.where(row == 1, tokens & 255, 0))
    out_ref[BLOCK:] = ids.astype(F32).astype(BF16)


def make_payload(out_grad, token_ids):
    vmem = pl.BlockSpec(memory_space=pltpu.VMEM)
    return pl.pallas_call(
        payload_kernel,
        out_shape=jax.ShapeDtypeStruct((BLOCK + EXTRA, BLOCK), BF16),
        in_specs=[vmem] * 2,
        out_specs=vmem,
        compiler_params=pltpu.CompilerParams(vmem_limit_bytes=4 << 20),
        cost_estimate=pl.CostEstimate(flops=1 << 16, bytes_accessed=1 << 19, transcendentals=0),
        name="payload",
    )(out_grad, token_ids.reshape(1, BLOCK))


def table_kernel(
    rate_ref, gain_ref, tap_ref,
    fwd_ref, side_ref, row_ref, tap_out_ref,
):
    shape = (BLOCK, ORDER)
    mode = lax.broadcasted_iota(jnp.int32, shape, 0)
    group_pick = jnp.where(mode // ORDER == lanes_of(shape), 1.0, 0.0)
    order_pick = mode % ORDER == lanes_of(shape)
    shape = (ORDER, BLOCK)
    group_row = jnp.where(lanes_of(shape) // ORDER == lax.broadcasted_iota(jnp.int32, shape, 0), 1.0, 0.0)
    order_row = lanes_of(shape) % ORDER == lax.broadcasted_iota(jnp.int32, shape, 0)

    def column(values):
        spread = lax.dot_general(
            group_pick, values, (((1,), (1,)), ((), ())), precision=EXACT, preferred_element_type=F32
        )
        return jnp.sum(jnp.where(order_pick, spread, 0.0), axis=1, keepdims=True)

    def as_row(values):
        spread = lax.dot_general(
            values, group_row, (((1,), (0,)), ((), ())), precision=EXACT, preferred_element_type=F32
        )
        return jnp.sum(jnp.where(order_row, spread, 0.0), axis=0, keepdims=True)

    row_ref[0:1] = as_row(rate_ref[...])
    row_ref[1:2] = as_row(gain_ref[...])
    for s in range(3):
        tap_out_ref[s * BLOCK : (s + 1) * BLOCK, :] = tap_ref[s].T
    rates = column(rate_ref[...])
    gains = column(gain_ref[...])
    position = lanes_of((BLOCK, BLOCK)).astype(F32)
    decay = jnp.exp(-position * rates)
    growth = jnp.exp(position * rates)
    weighted = decay * gains
    side_ref[:, END] = jnp.exp((position - (BLOCK - 1.0)) * rates).astype(BF16)
    side_ref[:, BEGIN] = decay.astype(BF16)
    side_ref[:, ENTER] = (gains * jnp.exp(-(position + 1.0) * rates)).astype(BF16)
    wide = jnp.minimum(lanes_of((BLOCK, BLOCK + HALO)), BLOCK + 1).astype(F32)
    side_ref[:, LEAVE] = (gains * jnp.exp((wide - float(BLOCK)) * rates)).astype(BF16)
    row = lax.broadcasted_iota(jnp.int32, (BLOCK, BLOCK), 0)
    col = lanes_of((BLOCK, BLOCK))
    for g in range(GROUPS):
        rows = slice(g * ORDER, (g + 1) * ORDER)
        grown, scaled = growth[rows], weighted[rows]
        dims = (((0,), (0,)), ((), ()))
        later = lax.dot_general(grown, scaled, dims, precision=EXACT, preferred_element_type=F32)
        fwd_ref[g] = jnp.where(col >= row, later, 0.0).astype(BF16)


def make_tables(rates, gains, taps):
    stack = jax.ShapeDtypeStruct((GROUPS, BLOCK, BLOCK), BF16)
    side = jax.ShapeDtypeStruct((BLOCK, SIDE), BF16)
    rows = jax.ShapeDtypeStruct((2, BLOCK), F32)
    columns = jax.ShapeDtypeStruct((3 * BLOCK, 3), F32)
    vmem = pl.BlockSpec(memory_space=pltpu.VMEM)
    return pl.pallas_call(
        table_kernel,
        out_shape=(stack, side, rows, columns),
        in_specs=[vmem] * 3,
        out_specs=(vmem,) * 4,
        compiler_params=pltpu.CompilerParams(vmem_limit_bytes=8 << 20),
        cost_estimate=pl.CostEstimate(flops=6 * 64 * 2**20, bytes_accessed=5 << 20, transcendentals=1 << 19),
        name="filter_tables",
    )(rates, gains, taps)


def project_kernel(part, first, ready, ahead, *refs):
    row_ref, weight_ref, refs = refs[0], refs[1], refs[2:]
    sum_ref, refs = (None, refs) if first else (refs[0], refs[1:])
    out_ref, refs = refs[0], refs[1:]

    def fetch(part, target, sem):
        c, x = place_of("core") ^ (part // 2), place_of("x") ^ (part % 2)
        copy = pltpu.make_async_copy(weight_ref.at[:, x, :, c], target, sem)
        copy.start()
        return copy

    copies = []
    held = weight_ref
    if not ready:
        held, sems = refs[-2:]
        copies = [fetch(part, held, sems.at[0])]
        copies += [fetch(later, refs[n], sems.at[n + 1]) for n, later in enumerate(ahead)]
        copies[0].wait()
    total = tuple(
        jnp.zeros((SHARE, BLOCK), F32) if first else sum_ref[:, s * BLOCK : (s + 1) * BLOCK] for s in range(3)
    )

    def add_block(z, total):
        rows = row_ref[z]
        return tuple(total[s] + nn(rows, held[s, z]) for s in range(3))

    total = lax.fori_loop(0, N_Z, add_block, total, unroll=2)
    for s in range(3):
        out_ref[:, s * BLOCK : (s + 1) * BLOCK] = total[s].astype(out_ref.dtype)
    for copy in copies[1:]:
        copy.wait()


def project(part, rows, weight, sums=None, ready=False, ahead=(), last=False):
    vmem = pl.BlockSpec(memory_space=pltpu.VMEM)
    result = jax.ShapeDtypeStruct((SHARE, 3 * BLOCK), BF16 if last else F32)
    block = (3, N_Z, BLOCK, BLOCK)
    scratch = [pltpu.VMEM(block, BF16), pltpu.SemaphoreType.DMA((1 + len(ahead),))]
    earlier = [] if sums is None else [sums]
    return pl.pallas_call(
        functools.partial(project_kernel, part, sums is None, ready, ahead),
        out_shape=(result,) + (jax.ShapeDtypeStruct(block, BF16),) * len(ahead),
        in_specs=[vmem, vmem if ready else pl.BlockSpec(memory_space=pltpu.HBM)] + [vmem] * len(earlier),
        out_specs=(vmem,) * (1 + len(ahead)),
        scratch_shapes=[] if ready else scratch,
        compiler_params=pltpu.CompilerParams(vmem_limit_bytes=(4 if ready else 46) << 20),
        cost_estimate=pl.CostEstimate(
            flops=2 * 64 * 768 * 2048, bytes_accessed=(1 + len(ahead)) * (3 << 20), transcendentals=0
        ),
        name="project",
    )(rows, weight, *earlier)


def back_step(n, held_ref, grad_ref, own_ref, other_ref):
    for core in (1, 0):
        target = other_ref if core else own_ref
        c = place_of("core") ^ core
        for shift in range(2):
            x = place_of("x") ^ shift
            total = nn(held_ref[n, 0, x, c], grad_ref[0:BLOCK])
            total += nn(held_ref[n, 1, x, c], grad_ref[BLOCK : 2 * BLOCK])
            total += nn(held_ref[n, 2, x, c], grad_ref[2 * BLOCK :])
            target[n, shift] = total.astype(BF16)


def source_of(own, n):
    return ((own - 2 * ((0,) + Y_STEPS)[n // 2]) & 6) | ((own & 1) ^ (n % 2))


def mixer_kernel(*refs):
    own = lax.axis_index("ctx")
    table_refs, refs = refs[:N_CTX], refs[N_CTX:]
    sources, refs = refs[:7], refs[7:]
    row_ref, tap_ref, out_ref, grad_proj_ref, own_ref, other_ref, ahead_ref = refs[:7]
    raw_ref, tapped_ref, id_ref, grad_ref, side_ref, fwd_ref, weight_ref, sems = refs[7:]
    copies = []
    for n in range(N_CTX):
        target = grad_ref.at[source_of(own, n)]
        copies.append(pltpu.make_async_copy(sources[n // 2].at[n % 2], target, sems.at[n]))
    copies.append(pltpu.make_async_copy(sources[4], side_ref, sems.at[N_CTX]))
    copies.append(pltpu.make_async_copy(sources[5], fwd_ref, sems.at[N_CTX + 1]))
    for n, step in enumerate(FAR_STEPS + NEAR_STEPS):
        z = (place_of("z") + step) & (N_Z - 1)
        far = n < len(FAR_STEPS)
        target = weight_ref.at[n] if far else ahead_ref.at[n - len(FAR_STEPS)]
        copies.append(pltpu.make_async_copy(sources[6].at[:, :, z], target, sems.at[N_CTX + 2 + n]))
    for copy in copies:
        copy.start()
    table = jnp.concatenate([ref[...].astype(F32) for ref in table_refs], axis=0).T.astype(BF16)
    table = jnp.concatenate([ref[...].astype(F32) for ref in table_refs], axis=0).T
    for tap in range(3):
        tapped_ref[:, tap * VOCAB : (tap + 1) * VOCAB] = (tap_ref[:, tap : tap + 1] * table).astype(BF16)
    table = table.astype(BF16)

    for copy in copies[:N_CTX]:
        copy.wait()
    edge = jnp.full((1, HALO), -1, jnp.int32)
    id_ref[:, :HALO] = edge
    id_ref[:, HALO + WINDOW :] = edge
    for block in range(N_CTX):
        ids = grad_ref[block, BLOCK : BLOCK + EXTRA, :].astype(F32)
        ids = (ids[0:1] * 256.0 + ids[1:2]).astype(jnp.int32)
        id_ref[:, HALO + block * BLOCK : HALO + (block + 1) * BLOCK] = ids
    copies[N_CTX].wait()

    tile_rows = [(lax.broadcasted_iota(jnp.int32, (16, BLOCK), 0) + 16 * n).astype(F32).astype(BF16) for n in range(SHARE // 16)]
    one, none = jnp.ones((16, BLOCK), BF16), jnp.zeros((16, BLOCK), BF16)

    def one_hot(ids):
        share, row = ids >> 6, (ids & (SHARE - 1)).astype(F32)
        tiles = []
        for n in range(N_CTX):
            rows = jnp.where(share == source_of(own, n), row, -1.0)
            rows = jnp.broadcast_to(rows, (16, BLOCK)).astype(BF16)
            tiles += [jnp.where(rows == tile, one, none) for tile in tile_rows]
        return jnp.concatenate(tiles, axis=0)

    def far_lookup(block):
        ids = id_ref[:, pl.ds(pl.multiple_of(block * BLOCK, BLOCK), HALO + BLOCK)]
        return jnp.concatenate([one_hot(ids[:, HALO - tap : HALO - tap + BLOCK]) for tap in range(3)], axis=0)

    def far_features(stream, picks):
        return nn(tapped_ref[stream * BLOCK : (stream + 1) * BLOCK, :], picks)

    for half in range(2):
        begin = pl.multiple_of(own * BLOCK + half * BLOCK, BLOCK)
        raw_ref[:, half * BLOCK : (half + 1) * BLOCK] = nn(table, one_hot(id_ref[:, pl.ds(begin, BLOCK)]))

    def featured(stream):
        rows = slice(stream * BLOCK, (stream + 1) * BLOCK)
        raw = raw_ref[rows, :]
        total = tap_ref[rows, 0:1] * raw[:, HALO:]
        for tap in (1, 2):
            total += tap_ref[rows, tap : tap + 1] * raw[:, HALO - tap : 2 * BLOCK - tap]
        return total

    rate_row = row_ref[0:1]
    gain_row = row_ref[1:2]
    block_decay = jnp.exp(rate_row * -float(BLOCK))
    same_group = (
        lax.broadcasted_iota(jnp.int32, (BLOCK, BLOCK), 0) // GROUP == lanes_of((BLOCK, BLOCK)) // ORDER
    )

    def earlier(block, state):
        picks = far_lookup(block)
        mixed = far_features(1, picks) * far_features(2, picks)
        return block_decay * state + nt(mixed.astype(BF16), side_ref[:, END])

    def later(step, state):
        block = N_CTX - 1 - step
        grad = grad_ref[block, 0:BLOCK, :].astype(F32) * far_features(0, far_lookup(block))
        return block_decay * state + nt(grad.astype(BF16), side_ref[:, BEGIN])

    zero = jnp.zeros((BLOCK, BLOCK), F32)
    before = lax.fori_loop(0, own, earlier, zero)
    after = lax.fori_loop(0, N_CTX - 1 - own, later, zero)

    wide = BLOCK + HALO
    query, key, value = featured(0), featured(1), featured(2)
    mixed = key * value
    following = jnp.minimum(own + 1, N_CTX - 1)
    grad_rows = jnp.concatenate(
        [grad_ref[own, 0:BLOCK, :], grad_ref[following, 0:BLOCK, 0:HALO]], axis=1
    ).astype(F32)
    grad_long = grad_rows * query
    mixed_own = mixed[:, :BLOCK].astype(BF16)
    long_own = grad_long[:, :BLOCK].astype(BF16)

    through = block_decay * before + nt(mixed_own, side_ref[:, END])
    before = jnp.where(same_group, before, 0.0).astype(BF16)
    through = jnp.where(same_group, through, 0.0).astype(BF16)
    after = jnp.where(same_group, after, 0.0).astype(BF16)

    copies[N_CTX + 1].wait()
    conv_rows, mixed_grads = [], []
    for g in range(GROUPS):
        rows = slice(g * GROUP, (g + 1) * GROUP)
        conv_rows.append(nn(mixed_own[rows], fwd_ref[g]))
        mixed_grads.append(nt(long_own[rows], fwd_ref[g]))
    conv = jnp.concatenate(conv_rows, axis=0) + nn(before, side_ref[:, ENTER])
    mixed_grad = jnp.concatenate(mixed_grads, axis=0) + nn(after, side_ref[:, LEAVE.start : LEAVE.start + BLOCK])

    def filter_at(lag):
        terms = jnp.where(same_group, gain_row * jnp.exp(rate_row * -float(lag)), 0.0)
        return jnp.sum(terms, axis=1, keepdims=True)

    second = lanes_of((BLOCK, HALO)) == 1
    conv_next = nn(through, side_ref[:, ENTER.start : ENTER.start + HALO]) + filter_at(0) * mixed[:, BLOCK:]
    conv_next += jnp.where(second, filter_at(1) * mixed[:, BLOCK - 1 : wide - 1], 0.0)
    grad_next = nn(after, side_ref[:, LEAVE.start + BLOCK :])
    grad_next -= jnp.where(second, filter_at(-1) * grad_long[:, BLOCK - 1 : wide - 1], 0.0)

    out_ref[...] = (query[:, :BLOCK] * conv).T.astype(BF16)

    conv = jnp.concatenate([conv, conv_next], axis=1)
    mixed_grad = jnp.concatenate([mixed_grad, grad_next], axis=1)
    lane = lanes_of((BLOCK, wide))
    inside = (lane < BLOCK) | ((lane < BLOCK + 2) & (own < N_CTX - 1))
    streams = (grad_rows * conv, mixed_grad * value, mixed_grad * key)
    for s in range(3):
        rows = slice(s * BLOCK, (s + 1) * BLOCK)
        grads = jnp.where(inside, streams[s], 0.0).astype(BF16).astype(F32)
        total = tap_ref[rows, 0:1] * grads[:, :BLOCK]
        for tap in (1, 2):
            total += tap_ref[rows, tap : tap + 1] * grads[:, tap : tap + BLOCK]
        grad_proj_ref[rows, :] = total.astype(BF16)
    for copy in copies[N_CTX + 2 :]:
        copy.wait()

    def far_step(n, carried):
        back_step(n, weight_ref, grad_proj_ref, own_ref, other_ref)
        return carried

    lax.fori_loop(0, len(FAR_STEPS), far_step, 0)


def mix(pieces, grads, tables, weight):
    fwd, side, row, taps = tables
    vmem = pl.BlockSpec(memory_space=pltpu.VMEM)
    return pl.pallas_call(
        mixer_kernel,
        out_shape=(
            jax.ShapeDtypeStruct((BLOCK, BLOCK), BF16),
            jax.ShapeDtypeStruct((3 * BLOCK, BLOCK), BF16),
            jax.ShapeDtypeStruct((len(FAR_STEPS), 2, BLOCK, BLOCK), BF16),
            jax.ShapeDtypeStruct((len(FAR_STEPS), 2, BLOCK, BLOCK), BF16),
            jax.ShapeDtypeStruct((len(NEAR_STEPS), 3, 2, 2, BLOCK, BLOCK), BF16),
        ),
        in_specs=[vmem] * N_CTX + [pl.BlockSpec(memory_space=pl.ANY)] * 7 + [vmem] * 2,
        out_specs=(vmem,) * 5,
        scratch_shapes=[
            pltpu.VMEM((3 * BLOCK, 2 * BLOCK), F32),
            pltpu.VMEM((3 * BLOCK, 3 * VOCAB), BF16),
            pltpu.VMEM((1, WINDOW + 2 * HALO), jnp.int32),
            pltpu.VMEM((N_CTX, BLOCK + EXTRA, BLOCK), BF16),
            pltpu.VMEM((BLOCK, SIDE), BF16),
            pltpu.VMEM((GROUPS, BLOCK, BLOCK), BF16),
            pltpu.VMEM((len(FAR_STEPS), 3, 2, 2, BLOCK, BLOCK), BF16),
            pltpu.SemaphoreType.DMA((N_CTX + 2 + N_Z,)),
        ],
        compiler_params=pltpu.CompilerParams(vmem_limit_bytes=36 << 20),
        cost_estimate=pl.CostEstimate(flops=3 << 30, bytes_accessed=8 << 20, transcendentals=1 << 16),
        name="mixer",
    )(*pieces, *grads, side, fwd, weight, row, taps)


def back_kernel(grad_ref, held_ref, own_ref, other_ref):
    def one_step(n, carried):
        back_step(n, held_ref, grad_ref, own_ref, other_ref)
        return carried

    lax.fori_loop(0, own_ref.shape[0], one_step, 0)


def back_project(grad_proj, held):
    vmem = pl.BlockSpec(memory_space=pltpu.VMEM)
    count = held.shape[0]
    part = jax.ShapeDtypeStruct((count, 2, BLOCK, BLOCK), BF16)
    return pl.pallas_call(
        back_kernel,
        out_shape=(part, part),
        in_specs=[vmem] * 2,
        out_specs=(vmem,) * 2,
        compiler_params=pltpu.CompilerParams(vmem_limit_bytes=4 << 20),
        cost_estimate=pl.CostEstimate(
            flops=2 * 256 * 768 * 1024 * count, bytes_accessed=count << 21, transcendentals=0
        ),
        name="back_project",
    )(grad_proj, held)


def project_features(rows, weight, pair):
    held = lax.all_to_all(
        jnp.broadcast_to(rows[None], (N_Z,) + rows.shape), "chan", 0, 0, axis_index_groups=Z_GROUPS
    )
    beside = lax.ppermute(held, "chan", X_SWAP)
    across = lax.ppermute(held, "chan", CORE_SWAP)
    held, pair = lax.optimization_barrier((held, pair))
    grads = gather_pairs(pair)
    sums, weight_beside, weight_both = project(0, held, weight, ahead=(1, 3))
    (sums,) = project(2, across, weight, sums)
    beside, sums = lax.optimization_barrier((beside, sums))
    both = lax.ppermute(beside, "chan", CORE_SWAP)
    (sums,) = project(1, beside, weight_beside, sums, ready=True)
    both, sums, grads = lax.optimization_barrier((both, sums, grads))
    (part,) = project(3, both, weight_both, sums, ready=True, last=True)
    return part, grads


def gather_ctx(value):
    across = lax.ppermute(value, "ctx", X_HALF_SWAP)
    found = [value, across]
    for piece in (value, across):
        found += [lax.ppermute(piece, "ctx", y_shift(by)) for by in Y_STEPS]
    return [found[n] for n in (0, 1, 2, 5, 3, 6, 4, 7)]


def pair_ctx(value):
    return jnp.stack([value, lax.ppermute(value, "ctx", X_HALF_SWAP)])


def gather_pairs(pair):
    return [pair] + [lax.ppermute(pair, "ctx", y_shift(by)) for by in Y_STEPS]


def moved(value, by):
    return lax.ppermute(value.astype(BF16), "chan", z_shift(by))


def reduce_chan(own, other, grad_proj, held):
    terms = {}

    def add_terms(steps, own, swapped):
        for n, step in enumerate(steps):
            terms[step] = own[n].astype(F32) + swapped[n].astype(F32)

    swapped = lax.ppermute(other, "chan", CORE_SWAP)
    near_own, near_other = back_project(grad_proj, held)
    swapped, near_own, near_other = lax.optimization_barrier((swapped, near_own, near_other))
    add_terms(FAR_STEPS, own, swapped)
    add_terms(NEAR_STEPS, near_own, lax.ppermute(near_other, "chan", CORE_SWAP))
    ahead, behind = moved(terms[4][0], 1).astype(F32), moved(terms[4][1], -1).astype(F32)
    ahead = jnp.stack([terms[3][0] + ahead, terms[3][1]])
    behind = jnp.stack([terms[5][0], terms[5][1] + behind])
    for near, other in ((2, 6), (1, 7)):
        ahead = terms[near] + moved(ahead, 1).astype(F32)
        behind = terms[other] + moved(behind, -1).astype(F32)
    total = terms[0] + moved(ahead, 1).astype(F32) + moved(behind, -1).astype(F32)
    total = total[0] + lax.ppermute(total[1].astype(BF16), "chan", X_SWAP).astype(F32)
    return total.astype(BF16)


def body(token_ids, embed_table, in_weight, feat_taps, modal_rates, modal_residues, out_grad):
    weight = in_weight.transpose(1, 0, 2).reshape(3, 2, N_Z, 2, BLOCK, BLOCK)
    own_vocab = lax.dynamic_slice_in_dim(embed_table, lax.axis_index("ctx") * SHARE, SHARE, 0)
    pair = pair_ctx(make_payload(out_grad, token_ids))
    part, grads = project_features(own_vocab, weight, pair)
    modal_rates, part = lax.optimization_barrier((modal_rates, part))
    pieces = gather_ctx(part)
    gains = modal_residues * jnp.sqrt(-jnp.expm1(-2.0 * modal_rates))
    tables = make_tables(modal_rates, gains, feat_taps)
    output, grad_proj, own, other, held = mix(pieces, grads, tables, weight)
    return (output, reduce_chan(own, other, grad_proj, held).T)


def solution(mesh):
    in_specs = (
        P("ctx"),
        P(None, "chan"),
        P(None, None, "chan"),
        P(None, None, "chan"),
        P(None, "chan"),
        P(None, "chan"),
        P("ctx", "chan"),
    )
    out_specs = (P("ctx", "chan"), P("ctx", "chan"))
    return jax.shard_map(body, mesh=mesh, in_specs=in_specs, out_specs=out_specs, check_vma=False)
```

```python
import functools

import jax
import jax.numpy as jnp
from jax import lax
from jax.experimental import pallas as pl
from jax.experimental.pallas import tpu as pltpu
from jax.sharding import PartitionSpec as P

F32 = jnp.float32
BF16 = jnp.bfloat16
EXACT = lax.Precision.HIGHEST
N_CTX = 8
N_CHAN = 32
N_Z = 8
BLOCK = 256
GROUP = 16
ORDER = 16
GROUPS = BLOCK // GROUP
VOCAB = 512
SHARE = VOCAB // N_CTX
HALO = 128
EXTRA = 16
WINDOW = N_CTX * BLOCK

END = slice(0, BLOCK)
BEGIN = slice(BLOCK, 2 * BLOCK)
ENTER = slice(2 * BLOCK, 3 * BLOCK)
LEAVE = slice(3 * BLOCK, 4 * BLOCK + HALO)
SIDE = 4 * BLOCK + HALO

CORE_SWAP = [(i, i ^ 1) for i in range(N_CHAN)]
X_SWAP = [(i, i ^ 16) for i in range(N_CHAN)]
FAR_STEPS = (4, 3, 5)
NEAR_STEPS = (2, 6, 1, 7, 0)
X_HALF_SWAP = [(i, i ^ 1) for i in range(N_CTX)]
Y_STEPS = (1, -1, 2)
Z_GROUPS = [[x * 16 + z * 2 + c for z in range(N_Z)] for x in range(2) for c in range(2)]


def z_shift(by):
    return [(i, (i & 16) | ((i + 2 * by) & 15)) for i in range(N_CHAN)]


def y_shift(by):
    return [(i, (i & 1) | ((i + 2 * by) & 7)) for i in range(N_CTX)]


def nn(a, b):
    return lax.dot_general(a, b, (((1,), (0,)), ((), ())), preferred_element_type=F32)


def nt(a, b):
    return lax.dot_general(a, b, (((1,), (1,)), ((), ())), preferred_element_type=F32)


def lanes_of(shape):
    return lax.broadcasted_iota(jnp.int32, shape, 1)


def place_of(axis):
    chan = lax.axis_index("chan")
    return {"x": chan // 16, "z": (chan // 2) & (N_Z - 1), "core": chan & 1}[axis]


def payload_kernel(grad_ref, token_ref, out_ref):
    out_ref[:BLOCK] = grad_ref[...].astype(F32).T.astype(BF16)
    tokens = token_ref[...]
    row = lax.broadcasted_iota(jnp.int32, (EXTRA, BLOCK), 0)
    ids = jnp.where(row == 0, tokens >> 8, jnp.where(row == 1, tokens & 255, 0))
    out_ref[BLOCK:] = ids.astype(F32).astype(BF16)


def make_payload(out_grad, token_ids):
    vmem = pl.BlockSpec(memory_space=pltpu.VMEM)
    return pl.pallas_call(
        payload_kernel,
        out_shape=jax.ShapeDtypeStruct((BLOCK + EXTRA, BLOCK), BF16),
        in_specs=[vmem] * 2,
        out_specs=vmem,
        compiler_params=pltpu.CompilerParams(vmem_limit_bytes=4 << 20),
        cost_estimate=pl.CostEstimate(flops=1 << 16, bytes_accessed=1 << 19, transcendentals=0),
        name="payload",
    )(out_grad, token_ids.reshape(1, BLOCK))


def table_kernel(
    rate_ref, gain_ref, tap_ref,
    fwd_ref, side_ref, row_ref, tap_out_ref,
):
    shape = (BLOCK, ORDER)
    mode = lax.broadcasted_iota(jnp.int32, shape, 0)
    group_pick = jnp.where(mode // ORDER == lanes_of(shape), 1.0, 0.0)
    order_pick = mode % ORDER == lanes_of(shape)
    shape = (ORDER, BLOCK)
    group_row = jnp.where(lanes_of(shape) // ORDER == lax.broadcasted_iota(jnp.int32, shape, 0), 1.0, 0.0)
    order_row = lanes_of(shape) % ORDER == lax.broadcasted_iota(jnp.int32, shape, 0)

    def column(values):
        spread = lax.dot_general(
            group_pick, values, (((1,), (1,)), ((), ())), precision=EXACT, preferred_element_type=F32
        )
        return jnp.sum(jnp.where(order_pick, spread, 0.0), axis=1, keepdims=True)

    def as_row(values):
        spread = lax.dot_general(
            values, group_row, (((1,), (0,)), ((), ())), precision=EXACT, preferred_element_type=F32
        )
        return jnp.sum(jnp.where(order_row, spread, 0.0), axis=0, keepdims=True)

    row_ref[0:1] = as_row(rate_ref[...])
    row_ref[1:2] = as_row(gain_ref[...])
    for s in range(3):
        tap_out_ref[s * BLOCK : (s + 1) * BLOCK, :] = tap_ref[s].T
    rates = column(rate_ref[...])
    gains = column(gain_ref[...])
    position = lanes_of((BLOCK, BLOCK)).astype(F32)
    decay = jnp.exp(-position * rates)
    growth = jnp.exp(position * rates)
    weighted = decay * gains
    side_ref[:, END] = jnp.exp((position - (BLOCK - 1.0)) * rates).astype(BF16)
    side_ref[:, BEGIN] = decay.astype(BF16)
    side_ref[:, ENTER] = (gains * jnp.exp(-(position + 1.0) * rates)).astype(BF16)
    wide = jnp.minimum(lanes_of((BLOCK, BLOCK + HALO)), BLOCK + 1).astype(F32)
    side_ref[:, LEAVE] = (gains * jnp.exp((wide - float(BLOCK)) * rates)).astype(BF16)
    row = lax.broadcasted_iota(jnp.int32, (BLOCK, BLOCK), 0)
    col = lanes_of((BLOCK, BLOCK))
    for g in range(GROUPS):
        rows = slice(g * ORDER, (g + 1) * ORDER)
        grown, scaled = growth[rows], weighted[rows]
        dims = (((0,), (0,)), ((), ()))
        later = lax.dot_general(grown, scaled, dims, precision=EXACT, preferred_element_type=F32)
        fwd_ref[g] = jnp.where(col >= row, later, 0.0).astype(BF16)


def make_tables(rates, gains, taps):
    stack = jax.ShapeDtypeStruct((GROUPS, BLOCK, BLOCK), BF16)
    side = jax.ShapeDtypeStruct((BLOCK, SIDE), BF16)
    rows = jax.ShapeDtypeStruct((2, BLOCK), F32)
    columns = jax.ShapeDtypeStruct((3 * BLOCK, 3), F32)
    vmem = pl.BlockSpec(memory_space=pltpu.VMEM)
    return pl.pallas_call(
        table_kernel,
        out_shape=(stack, side, rows, columns),
        in_specs=[vmem] * 3,
        out_specs=(vmem,) * 4,
        compiler_params=pltpu.CompilerParams(vmem_limit_bytes=8 << 20),
        cost_estimate=pl.CostEstimate(flops=6 * 64 * 2**20, bytes_accessed=5 << 20, transcendentals=1 << 19),
        name="filter_tables",
    )(rates, gains, taps)


def project_kernel(part, first, ready, ahead, *refs):
    row_ref, weight_ref, refs = refs[0], refs[1], refs[2:]
    sum_ref, refs = (None, refs) if first else (refs[0], refs[1:])
    out_ref, refs = refs[0], refs[1:]

    def fetch(part, target, sem):
        c, x = place_of("core") ^ (part // 2), place_of("x") ^ (part % 2)
        copy = pltpu.make_async_copy(weight_ref.at[:, x, :, c], target, sem)
        copy.start()
        return copy

    copies = []
    held = weight_ref
    if not ready:
        held, sems = refs[-2:]
        copies = [fetch(part, held, sems.at[0])]
        copies += [fetch(later, refs[n], sems.at[n + 1]) for n, later in enumerate(ahead)]
        copies[0].wait()
    total = tuple(
        jnp.zeros((SHARE, BLOCK), F32) if first else sum_ref[:, s * BLOCK : (s + 1) * BLOCK] for s in range(3)
    )

    def add_block(z, total):
        rows = row_ref[z]
        return tuple(total[s] + nn(rows, held[s, z]) for s in range(3))

    total = lax.fori_loop(0, N_Z, add_block, total, unroll=2)
    for s in range(3):
        out_ref[:, s * BLOCK : (s + 1) * BLOCK] = total[s].astype(out_ref.dtype)
    for copy in copies[1:]:
        copy.wait()


def project(part, rows, weight, sums=None, ready=False, ahead=(), last=False):
    vmem = pl.BlockSpec(memory_space=pltpu.VMEM)
    result = jax.ShapeDtypeStruct((SHARE, 3 * BLOCK), BF16 if last else F32)
    block = (3, N_Z, BLOCK, BLOCK)
    scratch = [pltpu.VMEM(block, BF16), pltpu.SemaphoreType.DMA((1 + len(ahead),))]
    earlier = [] if sums is None else [sums]
    return pl.pallas_call(
        functools.partial(project_kernel, part, sums is None, ready, ahead),
        out_shape=(result,) + (jax.ShapeDtypeStruct(block, BF16),) * len(ahead),
        in_specs=[vmem, vmem if ready else pl.BlockSpec(memory_space=pltpu.HBM)] + [vmem] * len(earlier),
        out_specs=(vmem,) * (1 + len(ahead)),
        scratch_shapes=[] if ready else scratch,
        compiler_params=pltpu.CompilerParams(vmem_limit_bytes=(4 if ready else 46) << 20),
        cost_estimate=pl.CostEstimate(
            flops=2 * 64 * 768 * 2048, bytes_accessed=(1 + len(ahead)) * (3 << 20), transcendentals=0
        ),
        name="project",
    )(rows, weight, *earlier)


def back_step(n, held_ref, grad_ref, own_ref, other_ref):
    for core in (1, 0):
        target = other_ref if core else own_ref
        c = place_of("core") ^ core
        for shift in range(2):
            x = place_of("x") ^ shift
            total = nn(held_ref[n, 0, x, c], grad_ref[0:BLOCK])
            total += nn(held_ref[n, 1, x, c], grad_ref[BLOCK : 2 * BLOCK])
            total += nn(held_ref[n, 2, x, c], grad_ref[2 * BLOCK :])
            target[n, shift] = total.astype(BF16)


def source_of(own, n):
    return ((own - 2 * ((0,) + Y_STEPS)[n // 2]) & 6) | ((own & 1) ^ (n % 2))


def mixer_kernel(*refs):
    own = lax.axis_index("ctx")
    table_refs, refs = refs[:N_CTX], refs[N_CTX:]
    sources, refs = refs[:7], refs[7:]
    row_ref, tap_ref, out_ref, grad_proj_ref, own_ref, other_ref, ahead_ref = refs[:7]
    raw_ref, tapped_ref, id_ref, grad_ref, side_ref, fwd_ref, weight_ref, sems = refs[7:]
    copies = []
    for n in range(N_CTX):
        target = grad_ref.at[source_of(own, n)]
        copies.append(pltpu.make_async_copy(sources[n // 2].at[n % 2], target, sems.at[n]))
    copies.append(pltpu.make_async_copy(sources[4], side_ref, sems.at[N_CTX]))
    copies.append(pltpu.make_async_copy(sources[5], fwd_ref, sems.at[N_CTX + 1]))
    for n, step in enumerate(FAR_STEPS + NEAR_STEPS):
        z = (place_of("z") + step) & (N_Z - 1)
        far = n < len(FAR_STEPS)
        target = weight_ref.at[n] if far else ahead_ref.at[n - len(FAR_STEPS)]
        copies.append(pltpu.make_async_copy(sources[6].at[:, :, z], target, sems.at[N_CTX + 2 + n]))
    for copy in copies:
        copy.start()
    table = jnp.concatenate([ref[...].astype(F32) for ref in table_refs], axis=0).T.astype(BF16)
    table = jnp.concatenate([ref[...].astype(F32) for ref in table_refs], axis=0).T
    for tap in range(3):
        tapped_ref[:, tap * VOCAB : (tap + 1) * VOCAB] = (tap_ref[:, tap : tap + 1] * table).astype(BF16)
    table = table.astype(BF16)

    for copy in copies[:N_CTX]:
        copy.wait()
    edge = jnp.full((1, HALO), -1, jnp.int32)
    id_ref[:, :HALO] = edge
    id_ref[:, HALO + WINDOW :] = edge
    for block in range(N_CTX):
        ids = grad_ref[block, BLOCK : BLOCK + EXTRA, :].astype(F32)
        ids = (ids[0:1] * 256.0 + ids[1:2]).astype(jnp.int32)
        id_ref[:, HALO + block * BLOCK : HALO + (block + 1) * BLOCK] = ids
    copies[N_CTX].wait()

    tile_rows = [(lax.broadcasted_iota(jnp.int32, (16, BLOCK), 0) + 16 * n).astype(F32).astype(BF16) for n in range(SHARE // 16)]
    one, none = jnp.ones((16, BLOCK), BF16), jnp.zeros((16, BLOCK), BF16)

    def one_hot(ids):
        share, row = ids >> 6, (ids & (SHARE - 1)).astype(F32)
        tiles = []
        for n in range(N_CTX):
            rows = jnp.where(share == source_of(own, n), row, -1.0)
            rows = jnp.broadcast_to(rows, (16, BLOCK)).astype(BF16)
            tiles += [jnp.where(rows == tile, one, none) for tile in tile_rows]
        return jnp.concatenate(tiles, axis=0)

    def far_lookup(block):
        ids = id_ref[:, pl.ds(pl.multiple_of(block * BLOCK, BLOCK), HALO + BLOCK)]
        return jnp.concatenate([one_hot(ids[:, HALO - tap : HALO - tap + BLOCK]) for tap in range(3)], axis=0)

    def far_features(stream, picks):
        return nn(tapped_ref[stream * BLOCK : (stream + 1) * BLOCK, :], picks)

    for half in range(2):
        begin = pl.multiple_of(own * BLOCK + half * BLOCK, BLOCK)
        raw_ref[:, half * BLOCK : (half + 1) * BLOCK] = nn(table, one_hot(id_ref[:, pl.ds(begin, BLOCK)]))

    def featured(stream):
        rows = slice(stream * BLOCK, (stream + 1) * BLOCK)
        raw = raw_ref[rows, :]
        total = tap_ref[rows, 0:1] * raw[:, HALO:]
        for tap in (1, 2):
            total += tap_ref[rows, tap : tap + 1] * raw[:, HALO - tap : 2 * BLOCK - tap]
        return total

    rate_row = row_ref[0:1]
    gain_row = row_ref[1:2]
    block_decay = jnp.exp(rate_row * -float(BLOCK))
    same_group = (
        lax.broadcasted_iota(jnp.int32, (BLOCK, BLOCK), 0) // GROUP == lanes_of((BLOCK, BLOCK)) // ORDER
    )

    def earlier(block, state):
        picks = far_lookup(block)
        mixed = far_features(1, picks) * far_features(2, picks)
        return block_decay * state + nt(mixed.astype(BF16), side_ref[:, END])

    def later(step, state):
        block = N_CTX - 1 - step
        grad = grad_ref[block, 0:BLOCK, :].astype(F32) * far_features(0, far_lookup(block))
        return block_decay * state + nt(grad.astype(BF16), side_ref[:, BEGIN])

    zero = jnp.zeros((BLOCK, BLOCK), F32)
    before = lax.fori_loop(0, own, earlier, zero)
    after = lax.fori_loop(0, N_CTX - 1 - own, later, zero)

    wide = BLOCK + HALO
    query, key, value = featured(0), featured(1), featured(2)
    mixed = key * value
    following = jnp.minimum(own + 1, N_CTX - 1)
    grad_rows = jnp.concatenate(
        [grad_ref[own, 0:BLOCK, :], grad_ref[following, 0:BLOCK, 0:HALO]], axis=1
    ).astype(F32)
    grad_long = grad_rows * query
    mixed_own = mixed[:, :BLOCK].astype(BF16)
    long_own = grad_long[:, :BLOCK].astype(BF16)

    through = block_decay * before + nt(mixed_own, side_ref[:, END])
    before = jnp.where(same_group, before, 0.0).astype(BF16)
    through = jnp.where(same_group, through, 0.0).astype(BF16)
    after = jnp.where(same_group, after, 0.0).astype(BF16)

    copies[N_CTX + 1].wait()
    conv_rows, mixed_grads = [], []
    for g in range(GROUPS):
        rows = slice(g * GROUP, (g + 1) * GROUP)
        conv_rows.append(nn(mixed_own[rows], fwd_ref[g]))
        mixed_grads.append(nt(long_own[rows], fwd_ref[g]))
    conv = jnp.concatenate(conv_rows, axis=0) + nn(before, side_ref[:, ENTER])
    mixed_grad = jnp.concatenate(mixed_grads, axis=0) + nn(after, side_ref[:, LEAVE.start : LEAVE.start + BLOCK])

    def filter_at(lag):
        terms = jnp.where(same_group, gain_row * jnp.exp(rate_row * -float(lag)), 0.0)
        return jnp.sum(terms, axis=1, keepdims=True)

    second = lanes_of((BLOCK, HALO)) == 1
    conv_next = nn(through, side_ref[:, ENTER.start : ENTER.start + HALO]) + filter_at(0) * mixed[:, BLOCK:]
    conv_next += jnp.where(second, filter_at(1) * mixed[:, BLOCK - 1 : wide - 1], 0.0)
    grad_next = nn(after, side_ref[:, LEAVE.start + BLOCK :])
    grad_next -= jnp.where(second, filter_at(-1) * grad_long[:, BLOCK - 1 : wide - 1], 0.0)

    out_ref[...] = (query[:, :BLOCK] * conv).T.astype(BF16)

    conv = jnp.concatenate([conv, conv_next], axis=1)
    mixed_grad = jnp.concatenate([mixed_grad, grad_next], axis=1)
    lane = lanes_of((BLOCK, wide))
    inside = (lane < BLOCK) | ((lane < BLOCK + 2) & (own < N_CTX - 1))
    streams = (grad_rows * conv, mixed_grad * value, mixed_grad * key)
    for s in range(3):
        rows = slice(s * BLOCK, (s + 1) * BLOCK)
        grads = jnp.where(inside, streams[s], 0.0).astype(BF16).astype(F32)
        total = tap_ref[rows, 0:1] * grads[:, :BLOCK]
        for tap in (1, 2):
            total += tap_ref[rows, tap : tap + 1] * grads[:, tap : tap + BLOCK]
        grad_proj_ref[rows, :] = total.astype(BF16)
    for copy in copies[N_CTX + 2 :]:
        copy.wait()

    def far_step(n, carried):
        back_step(n, weight_ref, grad_proj_ref, own_ref, other_ref)
        return carried

    lax.fori_loop(0, len(FAR_STEPS), far_step, 0)


def mix(pieces, grads, tables, weight):
    fwd, side, row, taps = tables
    vmem = pl.BlockSpec(memory_space=pltpu.VMEM)
    return pl.pallas_call(
        mixer_kernel,
        out_shape=(
            jax.ShapeDtypeStruct((BLOCK, BLOCK), BF16),
            jax.ShapeDtypeStruct((3 * BLOCK, BLOCK), BF16),
            jax.ShapeDtypeStruct((len(FAR_STEPS), 2, BLOCK, BLOCK), BF16),
            jax.ShapeDtypeStruct((len(FAR_STEPS), 2, BLOCK, BLOCK), BF16),
            jax.ShapeDtypeStruct((len(NEAR_STEPS), 3, 2, 2, BLOCK, BLOCK), BF16),
        ),
        in_specs=[vmem] * N_CTX + [pl.BlockSpec(memory_space=pl.ANY)] * 7 + [vmem] * 2,
        out_specs=(vmem,) * 5,
        scratch_shapes=[
            pltpu.VMEM((3 * BLOCK, 2 * BLOCK), F32),
            pltpu.VMEM((3 * BLOCK, 3 * VOCAB), BF16),
            pltpu.VMEM((1, WINDOW + 2 * HALO), jnp.int32),
            pltpu.VMEM((N_CTX, BLOCK + EXTRA, BLOCK), BF16),
            pltpu.VMEM((BLOCK, SIDE), BF16),
            pltpu.VMEM((GROUPS, BLOCK, BLOCK), BF16),
            pltpu.VMEM((len(FAR_STEPS), 3, 2, 2, BLOCK, BLOCK), BF16),
            pltpu.SemaphoreType.DMA((N_CTX + 2 + N_Z,)),
        ],
        compiler_params=pltpu.CompilerParams(vmem_limit_bytes=36 << 20),
        cost_estimate=pl.CostEstimate(flops=3 << 30, bytes_accessed=8 << 20, transcendentals=1 << 16),
        name="mixer",
    )(*pieces, *grads, side, fwd, weight, row, taps)


def back_kernel(grad_ref, held_ref, own_ref, other_ref):
    def one_step(n, carried):
        back_step(n, held_ref, grad_ref, own_ref, other_ref)
        return carried

    lax.fori_loop(0, own_ref.shape[0], one_step, 0)


def back_project(grad_proj, held):
    vmem = pl.BlockSpec(memory_space=pltpu.VMEM)
    count = held.shape[0]
    part = jax.ShapeDtypeStruct((count, 2, BLOCK, BLOCK), BF16)
    return pl.pallas_call(
        back_kernel,
        out_shape=(part, part),
        in_specs=[vmem] * 2,
        out_specs=(vmem,) * 2,
        compiler_params=pltpu.CompilerParams(vmem_limit_bytes=4 << 20),
        cost_estimate=pl.CostEstimate(
            flops=2 * 256 * 768 * 1024 * count, bytes_accessed=count << 21, transcendentals=0
        ),
        name="back_project",
    )(grad_proj, held)


def project_features(rows, weight, pair):
    held = lax.all_to_all(
        jnp.broadcast_to(rows[None], (N_Z,) + rows.shape), "chan", 0, 0, axis_index_groups=Z_GROUPS
    )
    beside = lax.ppermute(held, "chan", X_SWAP)
    across = lax.ppermute(held, "chan", CORE_SWAP)
    held, pair = lax.optimization_barrier((held, pair))
    grads = gather_pairs(pair)
    sums, weight_beside, weight_both = project(0, held, weight, ahead=(1, 3))
    (sums,) = project(2, across, weight, sums)
    beside, sums = lax.optimization_barrier((beside, sums))
    both = lax.ppermute(beside, "chan", CORE_SWAP)
    (sums,) = project(1, beside, weight_beside, sums, ready=True)
    both, sums, grads = lax.optimization_barrier((both, sums, grads))
    (part,) = project(3, both, weight_both, sums, ready=True, last=True)
    return part, grads


def gather_ctx(value):
    across = lax.ppermute(value, "ctx", X_HALF_SWAP)
    found = [value, across]
    for piece in (value, across):
        found += [lax.ppermute(piece, "ctx", y_shift(by)) for by in Y_STEPS]
    return [found[n] for n in (0, 1, 2, 5, 3, 6, 4, 7)]


def pair_ctx(value):
    return jnp.stack([value, lax.ppermute(value, "ctx", X_HALF_SWAP)])


def gather_pairs(pair):
    return [pair] + [lax.ppermute(pair, "ctx", y_shift(by)) for by in Y_STEPS]


def moved(value, by):
    return lax.ppermute(value.astype(BF16), "chan", z_shift(by))


def reduce_chan(own, other, grad_proj, held):
    half = BLOCK // 2
    wide = lambda value: value.astype(F32)
    parts, found = {}, {}

    def add_parts(steps, own, swapped):
        for n, step in enumerate(steps):
            parts[step] = (own[n], swapped[n])

    def lower(step, x):
        return sum(wide(part[x, :half]) for part in parts[step])

    def upper(step, rows=slice(0, half)):
        mine = sum(wide(part[0, half + rows.start : half + rows.stop]) for part in parts[step])
        return mine + wide(found[step][rows])

    def swap_upper(steps):
        sent = [sum(wide(part[1, half:]) for part in parts[step]).astype(BF16) for step in steps]
        return lax.ppermute(jnp.concatenate(sent, axis=0) if len(sent) > 1 else sent[0], "chan", X_SWAP)

    def keep_upper(steps, value):
        for n, step in enumerate(steps):
            found[step] = value[n * half : (n + 1) * half]

    def hop(ahead, behind):
        join = lambda rows: jnp.concatenate([row.astype(BF16) for row in rows], axis=0)
        return moved(join(ahead), 1), moved(join(behind), -1)

    swapped = lax.ppermute(other, "chan", CORE_SWAP)
    near_own, near_other = back_project(grad_proj, held)
    swapped, near_own, near_other = lax.optimization_barrier((swapped, near_own, near_other))
    add_parts(FAR_STEPS, own, swapped)
    near_swapped = lax.ppermute(near_other, "chan", CORE_SWAP)
    first, last = slice(0, half // 2), slice(half // 2, half)
    ahead, behind = hop([lower(4, 0)], [lower(4, 1)])
    keep_upper((4,), swap_upper((4,)))
    swap_far = swap_upper((3, 5))
    ahead, behind = hop(
        [lower(3, 0) + wide(ahead), lower(3, 1), upper(4, first)],
        [lower(5, 0), lower(5, 1) + wide(behind), upper(4, last)],
    )
    swap_far, ahead, behind = lax.optimization_barrier((swap_far, ahead, behind))
    keep_upper((3, 5), swap_far)
    add_parts(NEAR_STEPS, near_own, near_swapped)
    swap_middle = swap_upper((2, 6))
    swap_near = swap_upper((1, 7, 0))
    ahead, behind = hop(
        [
            lower(2, 0) + wide(ahead[:half]),
            lower(2, 1) + wide(ahead[half:BLOCK]),
            upper(3, first) + wide(ahead[BLOCK:]),
            upper(3, last),
        ],
        [
            lower(6, 0) + wide(behind[:half]),
            lower(6, 1) + wide(behind[half:BLOCK]),
            upper(5, first),
            upper(5, last) + wide(behind[BLOCK:]),
        ],
    )
    swap_middle, ahead, behind = lax.optimization_barrier((swap_middle, ahead, behind))
    keep_upper((2, 6), swap_middle)

    def onward(step, rows):
        return [
            lower(step, 0) + wide(rows[:half]),
            lower(step, 1) + wide(rows[half:BLOCK]),
            upper((step + (1 if step < 4 else -1)) % N_Z) + wide(rows[BLOCK:]),
        ]

    ahead, behind = hop(onward(1, ahead), onward(7, behind))
    swap_near, ahead, behind = lax.optimization_barrier((swap_near, ahead, behind))
    keep_upper((1, 7, 0), swap_near)
    final = hop([upper(1) + wide(ahead[BLOCK:])], [upper(7) + wide(behind[BLOCK:])])
    mine, sent = (
        lower(0, x) + wide(ahead[x * half : (x + 1) * half]) + wide(behind[x * half : (x + 1) * half]) for x in range(2)
    )
    mine = mine + wide(lax.ppermute(sent.astype(BF16), "chan", X_SWAP))
    return jnp.concatenate([mine, upper(0) + wide(final[0]) + wide(final[1])], axis=0).astype(BF16)


def body(token_ids, embed_table, in_weight, feat_taps, modal_rates, modal_residues, out_grad):
    weight = in_weight.transpose(1, 0, 2).reshape(3, 2, N_Z, 2, BLOCK, BLOCK)
    own_vocab = lax.dynamic_slice_in_dim(embed_table, lax.axis_index("ctx") * SHARE, SHARE, 0)
    pair = pair_ctx(make_payload(out_grad, token_ids))
    part, grads = project_features(own_vocab, weight, pair)
    modal_rates, part = lax.optimization_barrier((modal_rates, part))
    pieces = gather_ctx(part)
    gains = modal_residues * jnp.sqrt(-jnp.expm1(-2.0 * modal_rates))
    tables = make_tables(modal_rates, gains, feat_taps)
    output, grad_proj, own, other, held = mix(pieces, grads, tables, weight)
    return (output, reduce_chan(own, other, grad_proj, held).T)


def solution(mesh):
    in_specs = (
        P("ctx"),
        P(None, "chan"),
        P(None, None, "chan"),
        P(None, None, "chan"),
        P(None, "chan"),
        P(None, "chan"),
        P("ctx", "chan"),
    )
    out_specs = (P("ctx", "chan"), P("ctx", "chan"))
    return jax.shard_map(body, mesh=mesh, in_specs=in_specs, out_specs=out_specs, check_vma=False)
```

```python
import functools

import jax
import jax.numpy as jnp
from jax import lax
from jax.experimental import pallas as pl
from jax.experimental.pallas import tpu as pltpu
from jax.sharding import PartitionSpec as P

F32 = jnp.float32
BF16 = jnp.bfloat16
EXACT = lax.Precision.HIGHEST
N_CTX = 8
N_CHAN = 32
N_Z = 8
BLOCK = 256
GROUP = 16
ORDER = 16
GROUPS = BLOCK // GROUP
VOCAB = 512
SHARE = VOCAB // N_CTX
HALO = 128
EXTRA = 16
WINDOW = N_CTX * BLOCK

END = slice(0, BLOCK)
BEGIN = slice(BLOCK, 2 * BLOCK)
ENTER = slice(2 * BLOCK, 3 * BLOCK)
LEAVE = slice(3 * BLOCK, 4 * BLOCK + HALO)
SIDE = 4 * BLOCK + HALO

CORE_SWAP = [(i, i ^ 1) for i in range(N_CHAN)]
X_SWAP = [(i, i ^ 16) for i in range(N_CHAN)]
NEAR_STEPS = (3, 5, 2, 6, 1, 7, 0)
X_HALF_SWAP = [(i, i ^ 1) for i in range(N_CTX)]
Y_STEPS = (1, -1, 2)
Z_GROUPS = [[x * 16 + z * 2 + c for z in range(N_Z)] for x in range(2) for c in range(2)]


def z_shift(by):
    return [(i, (i & 16) | ((i + 2 * by) & 15)) for i in range(N_CHAN)]


def y_shift(by):
    return [(i, (i & 1) | ((i + 2 * by) & 7)) for i in range(N_CTX)]


def nn(a, b):
    return lax.dot_general(a, b, (((1,), (0,)), ((), ())), preferred_element_type=F32)


def nt(a, b):
    return lax.dot_general(a, b, (((1,), (1,)), ((), ())), preferred_element_type=F32)


def lanes_of(shape):
    return lax.broadcasted_iota(jnp.int32, shape, 1)


def place_of(axis):
    chan = lax.axis_index("chan")
    return {"x": chan // 16, "z": (chan // 2) & (N_Z - 1), "core": chan & 1}[axis]


def payload_kernel(grad_ref, token_ref, out_ref):
    out_ref[:BLOCK] = grad_ref[...].astype(F32).T.astype(BF16)
    tokens = token_ref[...]
    row = lax.broadcasted_iota(jnp.int32, (EXTRA, BLOCK), 0)
    ids = jnp.where(row == 0, tokens >> 8, jnp.where(row == 1, tokens & 255, 0))
    out_ref[BLOCK:] = ids.astype(F32).astype(BF16)


def make_payload(out_grad, token_ids):
    vmem = pl.BlockSpec(memory_space=pltpu.VMEM)
    return pl.pallas_call(
        payload_kernel,
        out_shape=jax.ShapeDtypeStruct((BLOCK + EXTRA, BLOCK), BF16),
        in_specs=[vmem] * 2,
        out_specs=vmem,
        compiler_params=pltpu.CompilerParams(vmem_limit_bytes=4 << 20),
        cost_estimate=pl.CostEstimate(flops=1 << 16, bytes_accessed=1 << 19, transcendentals=0),
        name="payload",
    )(out_grad, token_ids.reshape(1, BLOCK))


def table_kernel(
    rate_ref, gain_ref, tap_ref,
    fwd_ref, side_ref, row_ref, tap_out_ref,
):
    shape = (BLOCK, ORDER)
    mode = lax.broadcasted_iota(jnp.int32, shape, 0)
    group_pick = jnp.where(mode // ORDER == lanes_of(shape), 1.0, 0.0)
    order_pick = mode % ORDER == lanes_of(shape)
    shape = (ORDER, BLOCK)
    group_row = jnp.where(lanes_of(shape) // ORDER == lax.broadcasted_iota(jnp.int32, shape, 0), 1.0, 0.0)
    order_row = lanes_of(shape) % ORDER == lax.broadcasted_iota(jnp.int32, shape, 0)

    def column(values):
        spread = lax.dot_general(
            group_pick, values, (((1,), (1,)), ((), ())), precision=EXACT, preferred_element_type=F32
        )
        return jnp.sum(jnp.where(order_pick, spread, 0.0), axis=1, keepdims=True)

    def as_row(values):
        spread = lax.dot_general(
            values, group_row, (((1,), (0,)), ((), ())), precision=EXACT, preferred_element_type=F32
        )
        return jnp.sum(jnp.where(order_row, spread, 0.0), axis=0, keepdims=True)

    row_ref[0:1] = as_row(rate_ref[...])
    row_ref[1:2] = as_row(gain_ref[...])
    for s in range(3):
        tap_out_ref[s * BLOCK : (s + 1) * BLOCK, :] = tap_ref[s].T
    rates = column(rate_ref[...])
    gains = column(gain_ref[...])
    position = lanes_of((BLOCK, BLOCK)).astype(F32)
    decay = jnp.exp(-position * rates)
    growth = jnp.exp(position * rates)
    weighted = decay * gains
    side_ref[:, END] = jnp.exp((position - (BLOCK - 1.0)) * rates).astype(BF16)
    side_ref[:, BEGIN] = decay.astype(BF16)
    side_ref[:, ENTER] = (gains * jnp.exp(-(position + 1.0) * rates)).astype(BF16)
    wide = jnp.minimum(lanes_of((BLOCK, BLOCK + HALO)), BLOCK + 1).astype(F32)
    side_ref[:, LEAVE] = (gains * jnp.exp((wide - float(BLOCK)) * rates)).astype(BF16)
    row = lax.broadcasted_iota(jnp.int32, (BLOCK, BLOCK), 0)
    col = lanes_of((BLOCK, BLOCK))
    for g in range(GROUPS):
        rows = slice(g * ORDER, (g + 1) * ORDER)
        grown, scaled = growth[rows], weighted[rows]
        dims = (((0,), (0,)), ((), ()))
        later = lax.dot_general(grown, scaled, dims, precision=EXACT, preferred_element_type=F32)
        fwd_ref[g] = jnp.where(col >= row, later, 0.0).astype(BF16)


def make_tables(rates, gains, taps):
    stack = jax.ShapeDtypeStruct((GROUPS, BLOCK, BLOCK), BF16)
    side = jax.ShapeDtypeStruct((BLOCK, SIDE), BF16)
    rows = jax.ShapeDtypeStruct((2, BLOCK), F32)
    columns = jax.ShapeDtypeStruct((3 * BLOCK, 3), F32)
    vmem = pl.BlockSpec(memory_space=pltpu.VMEM)
    return pl.pallas_call(
        table_kernel,
        out_shape=(stack, side, rows, columns),
        in_specs=[vmem] * 3,
        out_specs=(vmem,) * 4,
        compiler_params=pltpu.CompilerParams(vmem_limit_bytes=8 << 20),
        cost_estimate=pl.CostEstimate(flops=6 * 64 * 2**20, bytes_accessed=5 << 20, transcendentals=1 << 19),
        name="filter_tables",
    )(rates, gains, taps)


def project_kernel(part, first, ready, ahead, *refs):
    row_ref, weight_ref, refs = refs[0], refs[1], refs[2:]
    sum_ref, refs = (None, refs) if first else (refs[0], refs[1:])
    out_ref, refs = refs[0], refs[1:]

    def fetch(part, target, sem):
        c, x = place_of("core") ^ (part // 2), place_of("x") ^ (part % 2)
        copy = pltpu.make_async_copy(weight_ref.at[:, x, :, c], target, sem)
        copy.start()
        return copy

    copies = []
    held = weight_ref
    if not ready:
        held, sems = refs[-2:]
        copies = [fetch(part, held, sems.at[0])]
        copies += [fetch(later, refs[n], sems.at[n + 1]) for n, later in enumerate(ahead)]
        copies[0].wait()
    total = tuple(
        jnp.zeros((SHARE, BLOCK), F32) if first else sum_ref[:, s * BLOCK : (s + 1) * BLOCK] for s in range(3)
    )

    def add_block(z, total):
        rows = row_ref[z]
        return tuple(total[s] + nn(rows, held[s, z]) for s in range(3))

    total = lax.fori_loop(0, N_Z, add_block, total, unroll=2)
    for s in range(3):
        out_ref[:, s * BLOCK : (s + 1) * BLOCK] = total[s].astype(out_ref.dtype)
    for copy in copies[1:]:
        copy.wait()


def project(part, rows, weight, sums=None, ready=False, ahead=(), last=False):
    vmem = pl.BlockSpec(memory_space=pltpu.VMEM)
    result = jax.ShapeDtypeStruct((SHARE, 3 * BLOCK), BF16 if last else F32)
    block = (3, N_Z, BLOCK, BLOCK)
    scratch = [pltpu.VMEM(block, BF16), pltpu.SemaphoreType.DMA((1 + len(ahead),))]
    earlier = [] if sums is None else [sums]
    return pl.pallas_call(
        functools.partial(project_kernel, part, sums is None, ready, ahead),
        out_shape=(result,) + (jax.ShapeDtypeStruct(block, BF16),) * len(ahead),
        in_specs=[vmem, vmem if ready else pl.BlockSpec(memory_space=pltpu.HBM)] + [vmem] * len(earlier),
        out_specs=(vmem,) * (1 + len(ahead)),
        scratch_shapes=[] if ready else scratch,
        compiler_params=pltpu.CompilerParams(vmem_limit_bytes=(4 if ready else 44) << 20),
        cost_estimate=pl.CostEstimate(
            flops=2 * 64 * 768 * 2048, bytes_accessed=(1 + len(ahead)) * (3 << 20), transcendentals=0
        ),
        name="project",
    )(rows, weight, *earlier)


def back_step(n, at, held_ref, grad_ref, own_ref, other_ref):
    for core in (1, 0):
        target = other_ref if core else own_ref
        c = place_of("core") ^ core
        for shift in range(2):
            x = place_of("x") ^ shift
            total = nn(held_ref[at, 0, x, c], grad_ref[0:BLOCK])
            total += nn(held_ref[at, 1, x, c], grad_ref[BLOCK : 2 * BLOCK])
            total += nn(held_ref[at, 2, x, c], grad_ref[2 * BLOCK :])
            target[n, shift] = total.astype(BF16)


def source_of(own, n):
    return ((own - 2 * ((0,) + Y_STEPS)[n // 2]) & 6) | ((own & 1) ^ (n % 2))


def mixer_kernel(*refs):
    own = lax.axis_index("ctx")
    table_refs, refs = refs[:N_CTX], refs[N_CTX:]
    sources, refs = refs[:7], refs[7:]
    row_ref, tap_ref, out_ref, grad_proj_ref, own_ref, other_ref, ahead_ref = refs[:7]
    raw_ref, tapped_ref, id_ref, grad_ref, side_ref, fwd_ref, weight_ref, sems = refs[7:]
    copies = []
    for n in range(N_CTX):
        target = grad_ref.at[source_of(own, n)]
        copies.append(pltpu.make_async_copy(sources[n // 2].at[n % 2], target, sems.at[n]))
    copies.append(pltpu.make_async_copy(sources[4], side_ref, sems.at[N_CTX]))
    copies.append(pltpu.make_async_copy(sources[5], fwd_ref, sems.at[N_CTX + 1]))
    far_z = (place_of("z") + N_Z // 2) & (N_Z - 1)
    copies.append(pltpu.make_async_copy(sources[6].at[:, :, far_z], weight_ref.at[0], sems.at[N_CTX + 2]))
    for n, step in enumerate(NEAR_STEPS):
        z = (place_of("z") + step) & (N_Z - 1)
        copies.append(pltpu.make_async_copy(sources[6].at[:, :, z], ahead_ref.at[n], sems.at[N_CTX + 3 + n]))
    for copy in copies[: N_CTX + 2]:
        copy.start()
    table = jnp.concatenate([ref[...].astype(F32) for ref in table_refs], axis=0).T.astype(BF16)
    table = jnp.concatenate([ref[...].astype(F32) for ref in table_refs], axis=0).T
    for tap in range(3):
        tapped_ref[:, tap * VOCAB : (tap + 1) * VOCAB] = (tap_ref[:, tap : tap + 1] * table).astype(BF16)
    table = table.astype(BF16)

    for copy in copies[:N_CTX]:
        copy.wait()
    edge = jnp.full((1, HALO), -1, jnp.int32)
    id_ref[:, :HALO] = edge
    id_ref[:, HALO + WINDOW :] = edge
    for block in range(N_CTX):
        ids = grad_ref[block, BLOCK : BLOCK + EXTRA, :].astype(F32)
        ids = (ids[0:1] * 256.0 + ids[1:2]).astype(jnp.int32)
        id_ref[:, HALO + block * BLOCK : HALO + (block + 1) * BLOCK] = ids
    for copy in copies[N_CTX + 2 :]:
        copy.start()
    copies[N_CTX].wait()

    tile_rows = [(lax.broadcasted_iota(jnp.int32, (16, BLOCK), 0) + 16 * n).astype(F32).astype(BF16) for n in range(SHARE // 16)]
    one, none = jnp.ones((16, BLOCK), BF16), jnp.zeros((16, BLOCK), BF16)

    def one_hot(ids):
        share, row = ids >> 6, (ids & (SHARE - 1)).astype(F32)
        tiles = []
        for n in range(N_CTX):
            rows = jnp.where(share == source_of(own, n), row, -1.0)
            rows = jnp.broadcast_to(rows, (16, BLOCK)).astype(BF16)
            tiles += [jnp.where(rows == tile, one, none) for tile in tile_rows]
        return jnp.concatenate(tiles, axis=0)

    def far_lookup(block):
        ids = id_ref[:, pl.ds(pl.multiple_of(block * BLOCK, BLOCK), HALO + BLOCK)]
        return jnp.concatenate([one_hot(ids[:, HALO - tap : HALO - tap + BLOCK]) for tap in range(3)], axis=0)

    def far_features(stream, picks):
        return nn(tapped_ref[stream * BLOCK : (stream + 1) * BLOCK, :], picks)

    for half in range(2):
        begin = pl.multiple_of(own * BLOCK + half * BLOCK, BLOCK)
        raw_ref[:, half * BLOCK : (half + 1) * BLOCK] = nn(table, one_hot(id_ref[:, pl.ds(begin, BLOCK)]))

    def featured(stream):
        rows = slice(stream * BLOCK, (stream + 1) * BLOCK)
        raw = raw_ref[rows, :]
        total = tap_ref[rows, 0:1] * raw[:, HALO:]
        for tap in (1, 2):
            total += tap_ref[rows, tap : tap + 1] * raw[:, HALO - tap : 2 * BLOCK - tap]
        return total

    rate_row = row_ref[0:1]
    gain_row = row_ref[1:2]
    block_decay = jnp.exp(rate_row * -float(BLOCK))
    same_group = (
        lax.broadcasted_iota(jnp.int32, (BLOCK, BLOCK), 0) // GROUP == lanes_of((BLOCK, BLOCK)) // ORDER
    )

    def earlier(block, state):
        picks = far_lookup(block)
        mixed = far_features(1, picks) * far_features(2, picks)
        return block_decay * state + nt(mixed.astype(BF16), side_ref[:, END])

    def later(step, state):
        block = N_CTX - 1 - step
        grad = grad_ref[block, 0:BLOCK, :].astype(F32) * far_features(0, far_lookup(block))
        return block_decay * state + nt(grad.astype(BF16), side_ref[:, BEGIN])

    zero = jnp.zeros((BLOCK, BLOCK), F32)
    before = lax.fori_loop(0, own, earlier, zero)
    after = lax.fori_loop(0, N_CTX - 1 - own, later, zero)

    wide = BLOCK + HALO
    query, key, value = featured(0), featured(1), featured(2)
    mixed = key * value
    following = jnp.minimum(own + 1, N_CTX - 1)
    grad_rows = jnp.concatenate(
        [grad_ref[own, 0:BLOCK, :], grad_ref[following, 0:BLOCK, 0:HALO]], axis=1
    ).astype(F32)
    grad_long = grad_rows * query
    mixed_own = mixed[:, :BLOCK].astype(BF16)
    long_own = grad_long[:, :BLOCK].astype(BF16)

    through = block_decay * before + nt(mixed_own, side_ref[:, END])
    before = jnp.where(same_group, before, 0.0).astype(BF16)
    through = jnp.where(same_group, through, 0.0).astype(BF16)
    after = jnp.where(same_group, after, 0.0).astype(BF16)

    copies[N_CTX + 1].wait()
    conv_rows, mixed_grads = [], []
    for g in range(GROUPS):
        rows = slice(g * GROUP, (g + 1) * GROUP)
        conv_rows.append(nn(mixed_own[rows], fwd_ref[g]))
        mixed_grads.append(nt(long_own[rows], fwd_ref[g]))
    conv = jnp.concatenate(conv_rows, axis=0) + nn(before, side_ref[:, ENTER])
    mixed_grad = jnp.concatenate(mixed_grads, axis=0) + nn(after, side_ref[:, LEAVE.start : LEAVE.start + BLOCK])

    def filter_at(lag):
        terms = jnp.where(same_group, gain_row * jnp.exp(rate_row * -float(lag)), 0.0)
        return jnp.sum(terms, axis=1, keepdims=True)

    second = lanes_of((BLOCK, HALO)) == 1
    conv_next = nn(through, side_ref[:, ENTER.start : ENTER.start + HALO]) + filter_at(0) * mixed[:, BLOCK:]
    conv_next += jnp.where(second, filter_at(1) * mixed[:, BLOCK - 1 : wide - 1], 0.0)
    grad_next = nn(after, side_ref[:, LEAVE.start + BLOCK :])
    grad_next -= jnp.where(second, filter_at(-1) * grad_long[:, BLOCK - 1 : wide - 1], 0.0)

    out_ref[...] = (query[:, :BLOCK] * conv).T.astype(BF16)

    conv = jnp.concatenate([conv, conv_next], axis=1)
    mixed_grad = jnp.concatenate([mixed_grad, grad_next], axis=1)
    lane = lanes_of((BLOCK, wide))
    inside = (lane < BLOCK) | ((lane < BLOCK + 2) & (own < N_CTX - 1))
    streams = (grad_rows * conv, mixed_grad * value, mixed_grad * key)
    for s in range(3):
        rows = slice(s * BLOCK, (s + 1) * BLOCK)
        grads = jnp.where(inside, streams[s], 0.0).astype(BF16).astype(F32)
        total = tap_ref[rows, 0:1] * grads[:, :BLOCK]
        for tap in (1, 2):
            total += tap_ref[rows, tap : tap + 1] * grads[:, tap : tap + BLOCK]
        grad_proj_ref[rows, :] = total.astype(BF16)
    for copy in copies[N_CTX + 2 :]:
        copy.wait()
    back_step(0, 0, weight_ref, grad_proj_ref, own_ref, other_ref)


def mix(pieces, grads, tables, weight):
    fwd, side, row, taps = tables
    vmem = pl.BlockSpec(memory_space=pltpu.VMEM)
    return pl.pallas_call(
        mixer_kernel,
        out_shape=(
            jax.ShapeDtypeStruct((BLOCK, BLOCK), BF16),
            jax.ShapeDtypeStruct((3 * BLOCK, BLOCK), BF16),
            jax.ShapeDtypeStruct((1, 2, BLOCK, BLOCK), BF16),
            jax.ShapeDtypeStruct((1, 2, BLOCK, BLOCK), BF16),
            jax.ShapeDtypeStruct((len(NEAR_STEPS), 3, 2, 2, BLOCK, BLOCK), BF16),
        ),
        in_specs=[vmem] * N_CTX + [pl.BlockSpec(memory_space=pl.ANY)] * 7 + [vmem] * 2,
        out_specs=(vmem,) * 5,
        scratch_shapes=[
            pltpu.VMEM((3 * BLOCK, 2 * BLOCK), F32),
            pltpu.VMEM((3 * BLOCK, 3 * VOCAB), BF16),
            pltpu.VMEM((1, WINDOW + 2 * HALO), jnp.int32),
            pltpu.VMEM((N_CTX, BLOCK + EXTRA, BLOCK), BF16),
            pltpu.VMEM((BLOCK, SIDE), BF16),
            pltpu.VMEM((GROUPS, BLOCK, BLOCK), BF16),
            pltpu.VMEM((1, 3, 2, 2, BLOCK, BLOCK), BF16),
            pltpu.SemaphoreType.DMA((N_CTX + 3 + len(NEAR_STEPS),)),
        ],
        compiler_params=pltpu.CompilerParams(vmem_limit_bytes=30 << 20),
        cost_estimate=pl.CostEstimate(flops=3 << 30, bytes_accessed=8 << 20, transcendentals=1 << 16),
        name="mixer",
    )(*pieces, *grads, side, fwd, weight, row, taps)


def back_kernel(begin, grad_ref, held_ref, own_ref, other_ref):
    def one_step(n, carried):
        back_step(n, begin + n, held_ref, grad_ref, own_ref, other_ref)
        return carried

    lax.fori_loop(0, own_ref.shape[0], one_step, 0)


def back_project(grad_proj, held, begin, count):
    vmem = pl.BlockSpec(memory_space=pltpu.VMEM)
    part = jax.ShapeDtypeStruct((count, 2, BLOCK, BLOCK), BF16)
    return pl.pallas_call(
        functools.partial(back_kernel, begin),
        out_shape=(part, part),
        in_specs=[vmem] * 2,
        out_specs=(vmem,) * 2,
        compiler_params=pltpu.CompilerParams(vmem_limit_bytes=4 << 20),
        cost_estimate=pl.CostEstimate(
            flops=2 * 256 * 768 * 1024 * count, bytes_accessed=count << 21, transcendentals=0
        ),
        name="back_project",
    )(grad_proj, held)


def project_features(rows, weight, pair):
    held = lax.all_to_all(
        jnp.broadcast_to(rows[None], (N_Z,) + rows.shape), "chan", 0, 0, axis_index_groups=Z_GROUPS
    )
    beside = lax.ppermute(held, "chan", X_SWAP)
    across = lax.ppermute(held, "chan", CORE_SWAP)
    held, pair = lax.optimization_barrier((held, pair))
    grads = gather_pairs(pair)
    sums, weight_across, weight_beside, weight_both = project(0, held, weight, ahead=(2, 1, 3))
    (sums,) = project(2, across, weight_across, sums, ready=True)
    beside, sums = lax.optimization_barrier((beside, sums))
    both = lax.ppermute(beside, "chan", CORE_SWAP)
    (sums,) = project(1, beside, weight_beside, sums, ready=True)
    both, sums, grads = lax.optimization_barrier((both, sums, grads))
    (part,) = project(3, both, weight_both, sums, ready=True, last=True)
    return part, grads


def gather_ctx(value):
    across = lax.ppermute(value, "ctx", X_HALF_SWAP)
    found = [value, across]
    for piece in (value, across):
        found += [lax.ppermute(piece, "ctx", y_shift(by)) for by in Y_STEPS]
    return [found[n] for n in (0, 1, 2, 5, 3, 6, 4, 7)]


def pair_ctx(value):
    return jnp.stack([value, lax.ppermute(value, "ctx", X_HALF_SWAP)])


def gather_pairs(pair):
    return [pair] + [lax.ppermute(pair, "ctx", y_shift(by)) for by in Y_STEPS]


def moved(value, by):
    return lax.ppermute(value.astype(BF16), "chan", z_shift(by))


def reduce_chan(far_parts, grad_proj, held):
    terms = {}

    def swap(parts):
        return parts[0], lax.ppermute(parts[1], "chan", CORE_SWAP)

    def add_terms(steps, own, swapped):
        for n, step in enumerate(steps):
            for half in range(2):
                terms[step, half] = own[n, half].astype(F32) + swapped[n, half].astype(F32)

    def arrive(values, tied):
        values, tied = lax.optimization_barrier((values, tied))
        return values, tied

    def send(values):
        return {(half, by): moved(value, by) for (half, by), value in values.items()}

    own, swapped = swap(far_parts)
    near = back_project(grad_proj, held, 0, 2)
    (swapped, near) = lax.optimization_barrier((swapped, near))
    add_terms((4,), own, swapped)
    ways = {1: (1, -1), 0: (-1, 1)}
    chain = send({(half, ways[half][0]): terms[4, half] for half in (1, 0)})
    grad_proj, near = lax.optimization_barrier((grad_proj, near))
    near_own, near_swapped = swap(near)
    middle = back_project(grad_proj, held, 2, 2)
    arrived, middle = arrive(chain, middle)
    add_terms((3, 5), near_own, near_swapped)
    middle_own, middle_swapped = swap(middle)
    chain = {}
    for half in (1, 0):
        long, short = ways[half]
        chain[half, long] = terms[(3 * long) % 8, half] + arrived[half, long].astype(F32)
        chain[half, short] = terms[(3 * short) % 8, half]
    chain = send(chain)
    grad_proj, middle_own = lax.optimization_barrier((grad_proj, middle_own))
    last = back_project(grad_proj, held, 4, 3)
    arrived, last = arrive(chain, last)
    add_terms((2, 6), middle_own, middle_swapped)
    last_own, last_swapped = swap(last)
    chain = send({(half, by): value.astype(F32) + terms[(2 * by) % 8, half] for (half, by), value in arrived.items()})
    add_terms((1, 7, 0), last_own, last_swapped)
    chain = send({(half, by): value.astype(F32) + terms[by % 8, half] for (half, by), value in chain.items()})
    far_half, near_half = (
        terms[0, half] + chain[half, 1].astype(F32) + chain[half, -1].astype(F32) for half in (1, 0)
    )
    total = near_half + lax.ppermute(far_half.astype(BF16), "chan", X_SWAP).astype(F32)
    return total.astype(BF16)


def body(token_ids, embed_table, in_weight, feat_taps, modal_rates, modal_residues, out_grad):
    weight = in_weight.transpose(1, 0, 2).reshape(3, 2, N_Z, 2, BLOCK, BLOCK)
    own_vocab = lax.dynamic_slice_in_dim(embed_table, lax.axis_index("ctx") * SHARE, SHARE, 0)
    pair = pair_ctx(make_payload(out_grad, token_ids))
    part, grads = project_features(own_vocab, weight, pair)
    modal_rates, part = lax.optimization_barrier((modal_rates, part))
    pieces = gather_ctx(part)
    gains = modal_residues * jnp.sqrt(-jnp.expm1(-2.0 * modal_rates))
    tables = make_tables(modal_rates, gains, feat_taps)
    output, grad_proj, own, other, held = mix(pieces, grads, tables, weight)
    return (output, reduce_chan((own, other), grad_proj, held).T)


def solution(mesh):
    in_specs = (
        P("ctx"),
        P(None, "chan"),
        P(None, None, "chan"),
        P(None, None, "chan"),
        P(None, "chan"),
        P(None, "chan"),
        P("ctx", "chan"),
    )
    out_specs = (P("ctx", "chan"), P("ctx", "chan"))
    return jax.shard_map(body, mesh=mesh, in_specs=in_specs, out_specs=out_specs, check_vma=False)
```

```python
import functools

import jax
import jax.numpy as jnp
from jax import lax
from jax.experimental import pallas as pl
from jax.experimental.pallas import tpu as pltpu
from jax.sharding import PartitionSpec as P

F32 = jnp.float32
BF16 = jnp.bfloat16
EXACT = lax.Precision.HIGHEST
N_CTX = 8
N_CHAN = 32
N_Z = 8
BLOCK = 256
GROUP = 16
ORDER = 16
GROUPS = BLOCK // GROUP
VOCAB = 512
SHARE = VOCAB // N_CTX
HALO = 128
EXTRA = 16
WINDOW = N_CTX * BLOCK

END = slice(0, BLOCK)
BEGIN = slice(BLOCK, 2 * BLOCK)
ENTER = slice(2 * BLOCK, 3 * BLOCK)
LEAVE = slice(3 * BLOCK, 4 * BLOCK + HALO)
SIDE = 4 * BLOCK + HALO

CORE_SWAP = [(i, i ^ 1) for i in range(N_CHAN)]
X_SWAP = [(i, i ^ 16) for i in range(N_CHAN)]
NEAR_STEPS = (3, 5, 2, 6, 1, 7, 0)
X_HALF_SWAP = [(i, i ^ 1) for i in range(N_CTX)]
Y_STEPS = (1, -1, 2)
Z_GROUPS = [[x * 16 + z * 2 + c for z in range(N_Z)] for x in range(2) for c in range(2)]


def z_shift(by):
    return [(i, (i & 16) | ((i + 2 * by) & 15)) for i in range(N_CHAN)]


def y_shift(by):
    return [(i, (i & 1) | ((i + 2 * by) & 7)) for i in range(N_CTX)]


def nn(a, b):
    return lax.dot_general(a, b, (((1,), (0,)), ((), ())), preferred_element_type=F32)


def nt(a, b):
    return lax.dot_general(a, b, (((1,), (1,)), ((), ())), preferred_element_type=F32)


def lanes_of(shape):
    return lax.broadcasted_iota(jnp.int32, shape, 1)


def place_of(axis):
    chan = lax.axis_index("chan")
    return {"x": chan // 16, "z": (chan // 2) & (N_Z - 1), "core": chan & 1}[axis]


def payload_kernel(grad_ref, token_ref, out_ref):
    out_ref[:BLOCK] = grad_ref[...].astype(F32).T.astype(BF16)
    tokens = token_ref[...]
    row = lax.broadcasted_iota(jnp.int32, (EXTRA, BLOCK), 0)
    ids = jnp.where(row == 0, tokens >> 8, jnp.where(row == 1, tokens & 255, 0))
    out_ref[BLOCK:] = ids.astype(F32).astype(BF16)


def make_payload(out_grad, token_ids):
    vmem = pl.BlockSpec(memory_space=pltpu.VMEM)
    return pl.pallas_call(
        payload_kernel,
        out_shape=jax.ShapeDtypeStruct((BLOCK + EXTRA, BLOCK), BF16),
        in_specs=[vmem] * 2,
        out_specs=vmem,
        compiler_params=pltpu.CompilerParams(vmem_limit_bytes=4 << 20),
        cost_estimate=pl.CostEstimate(flops=1 << 16, bytes_accessed=1 << 19, transcendentals=0),
        name="payload",
    )(out_grad, token_ids.reshape(1, BLOCK))


def table_kernel(
    rate_ref, gain_ref, tap_ref,
    fwd_ref, side_ref, row_ref, tap_out_ref,
):
    shape = (BLOCK, ORDER)
    mode = lax.broadcasted_iota(jnp.int32, shape, 0)
    group_pick = jnp.where(mode // ORDER == lanes_of(shape), 1.0, 0.0)
    order_pick = mode % ORDER == lanes_of(shape)
    shape = (ORDER, BLOCK)
    group_row = jnp.where(lanes_of(shape) // ORDER == lax.broadcasted_iota(jnp.int32, shape, 0), 1.0, 0.0)
    order_row = lanes_of(shape) % ORDER == lax.broadcasted_iota(jnp.int32, shape, 0)

    def column(values):
        spread = lax.dot_general(
            group_pick, values, (((1,), (1,)), ((), ())), precision=EXACT, preferred_element_type=F32
        )
        return jnp.sum(jnp.where(order_pick, spread, 0.0), axis=1, keepdims=True)

    def as_row(values):
        spread = lax.dot_general(
            values, group_row, (((1,), (0,)), ((), ())), precision=EXACT, preferred_element_type=F32
        )
        return jnp.sum(jnp.where(order_row, spread, 0.0), axis=0, keepdims=True)

    row_ref[0:1] = as_row(rate_ref[...])
    row_ref[1:2] = as_row(gain_ref[...])
    for s in range(3):
        tap_out_ref[s * BLOCK : (s + 1) * BLOCK, :] = tap_ref[s].T
    rates = column(rate_ref[...])
    gains = column(gain_ref[...])
    position = lanes_of((BLOCK, BLOCK)).astype(F32)
    decay = jnp.exp(-position * rates)
    growth = jnp.exp(position * rates)
    weighted = decay * gains
    side_ref[:, END] = jnp.exp((position - (BLOCK - 1.0)) * rates).astype(BF16)
    side_ref[:, BEGIN] = decay.astype(BF16)
    side_ref[:, ENTER] = (gains * jnp.exp(-(position + 1.0) * rates)).astype(BF16)
    wide = jnp.minimum(lanes_of((BLOCK, BLOCK + HALO)), BLOCK + 1).astype(F32)
    side_ref[:, LEAVE] = (gains * jnp.exp((wide - float(BLOCK)) * rates)).astype(BF16)
    row = lax.broadcasted_iota(jnp.int32, (BLOCK, BLOCK), 0)
    col = lanes_of((BLOCK, BLOCK))
    for g in range(GROUPS):
        rows = slice(g * ORDER, (g + 1) * ORDER)
        grown, scaled = growth[rows], weighted[rows]
        dims = (((0,), (0,)), ((), ()))
        later = lax.dot_general(grown, scaled, dims, precision=EXACT, preferred_element_type=F32)
        fwd_ref[g] = jnp.where(col >= row, later, 0.0).astype(BF16)


def make_tables(rates, gains, taps):
    stack = jax.ShapeDtypeStruct((GROUPS, BLOCK, BLOCK), BF16)
    side = jax.ShapeDtypeStruct((BLOCK, SIDE), BF16)
    rows = jax.ShapeDtypeStruct((2, BLOCK), F32)
    columns = jax.ShapeDtypeStruct((3 * BLOCK, 3), F32)
    vmem = pl.BlockSpec(memory_space=pltpu.VMEM)
    return pl.pallas_call(
        table_kernel,
        out_shape=(stack, side, rows, columns),
        in_specs=[vmem] * 3,
        out_specs=(vmem,) * 4,
        compiler_params=pltpu.CompilerParams(vmem_limit_bytes=8 << 20),
        cost_estimate=pl.CostEstimate(flops=6 * 64 * 2**20, bytes_accessed=5 << 20, transcendentals=1 << 19),
        name="filter_tables",
    )(rates, gains, taps)


def project_kernel(part, first, ready, ahead, *refs):
    row_ref, weight_ref, refs = refs[0], refs[1], refs[2:]
    sum_ref, refs = (None, refs) if first else (refs[0], refs[1:])
    out_ref, refs = refs[0], refs[1:]

    def fetch(part, target, sem):
        c, x = place_of("core") ^ (part // 2), place_of("x") ^ (part % 2)
        copy = pltpu.make_async_copy(weight_ref.at[:, x, :, c], target, sem)
        copy.start()
        return copy

    copies = []
    held = weight_ref
    if not ready:
        held, sems = refs[-2:]
        copies = [fetch(part, held, sems.at[0])]
        copies += [fetch(later, refs[n], sems.at[n + 1]) for n, later in enumerate(ahead)]
        copies[0].wait()
    total = tuple(
        jnp.zeros((SHARE, BLOCK), F32) if first else sum_ref[:, s * BLOCK : (s + 1) * BLOCK] for s in range(3)
    )

    def add_block(z, total):
        rows = row_ref[z]
        return tuple(total[s] + nn(rows, held[s, z]) for s in range(3))

    total = lax.fori_loop(0, N_Z, add_block, total, unroll=2)
    for s in range(3):
        out_ref[:, s * BLOCK : (s + 1) * BLOCK] = total[s].astype(out_ref.dtype)
    for copy in copies[1:]:
        copy.wait()


def project(part, rows, weight, sums=None, ready=False, ahead=(), last=False):
    vmem = pl.BlockSpec(memory_space=pltpu.VMEM)
    result = jax.ShapeDtypeStruct((SHARE, 3 * BLOCK), BF16 if last else F32)
    block = (3, N_Z, BLOCK, BLOCK)
    scratch = [pltpu.VMEM(block, BF16), pltpu.SemaphoreType.DMA((1 + len(ahead),))]
    earlier = [] if sums is None else [sums]
    return pl.pallas_call(
        functools.partial(project_kernel, part, sums is None, ready, ahead),
        out_shape=(result,) + (jax.ShapeDtypeStruct(block, BF16),) * len(ahead),
        in_specs=[vmem, vmem if ready else pl.BlockSpec(memory_space=pltpu.HBM)] + [vmem] * len(earlier),
        out_specs=(vmem,) * (1 + len(ahead)),
        scratch_shapes=[] if ready else scratch,
        compiler_params=pltpu.CompilerParams(vmem_limit_bytes=(4 if ready else 44) << 20),
        cost_estimate=pl.CostEstimate(
            flops=2 * 64 * 768 * 2048, bytes_accessed=(1 + len(ahead)) * (3 << 20), transcendentals=0
        ),
        name="project",
    )(rows, weight, *earlier)


def back_step(n, at, held_ref, grad_ref, own_ref, other_ref):
    for core in (1, 0):
        target = other_ref if core else own_ref
        c = place_of("core") ^ core
        for shift in range(2):
            x = place_of("x") ^ shift
            total = nn(held_ref[at, 0, x, c], grad_ref[0:BLOCK])
            total += nn(held_ref[at, 1, x, c], grad_ref[BLOCK : 2 * BLOCK])
            total += nn(held_ref[at, 2, x, c], grad_ref[2 * BLOCK :])
            target[n, shift] = total.astype(BF16)


def source_of(own, n):
    return ((own - 2 * ((0,) + Y_STEPS)[n // 2]) & 6) | ((own & 1) ^ (n % 2))


def mixer_kernel(*refs):
    own = lax.axis_index("ctx")
    table_refs, refs = refs[:N_CTX], refs[N_CTX:]
    sources, refs = refs[:7], refs[7:]
    row_ref, tap_ref, out_ref, grad_proj_ref, own_ref, other_ref, ahead_ref = refs[:7]
    raw_ref, tapped_ref, id_ref, grad_ref, side_ref, fwd_ref, weight_ref, sems = refs[7:]
    copies = []
    for n in range(N_CTX):
        target = grad_ref.at[source_of(own, n)]
        copies.append(pltpu.make_async_copy(sources[n // 2].at[n % 2], target, sems.at[n]))
    copies.append(pltpu.make_async_copy(sources[4], side_ref, sems.at[N_CTX]))
    copies.append(pltpu.make_async_copy(sources[5], fwd_ref, sems.at[N_CTX + 1]))
    far_z = (place_of("z") + N_Z // 2) & (N_Z - 1)
    copies.append(pltpu.make_async_copy(sources[6].at[:, :, far_z], weight_ref.at[0], sems.at[N_CTX + 2]))
    for n, step in enumerate(NEAR_STEPS):
        z = (place_of("z") + step) & (N_Z - 1)
        copies.append(pltpu.make_async_copy(sources[6].at[:, :, z], ahead_ref.at[n], sems.at[N_CTX + 3 + n]))
    for copy in copies[: N_CTX + 2]:
        copy.start()
    table = jnp.concatenate([ref[...].astype(F32) for ref in table_refs], axis=0).T.astype(BF16)
    table = jnp.concatenate([ref[...].astype(F32) for ref in table_refs], axis=0).T
    for tap in range(3):
        tapped_ref[:, tap * VOCAB : (tap + 1) * VOCAB] = (tap_ref[:, tap : tap + 1] * table).astype(BF16)
    table = table.astype(BF16)

    for copy in copies[:N_CTX]:
        copy.wait()
    edge = jnp.full((1, HALO), -1, jnp.int32)
    id_ref[:, :HALO] = edge
    id_ref[:, HALO + WINDOW :] = edge
    for block in range(N_CTX):
        ids = grad_ref[block, BLOCK : BLOCK + EXTRA, :].astype(F32)
        ids = (ids[0:1] * 256.0 + ids[1:2]).astype(jnp.int32)
        id_ref[:, HALO + block * BLOCK : HALO + (block + 1) * BLOCK] = ids
    for copy in copies[N_CTX + 2 :]:
        copy.start()
    copies[N_CTX].wait()

    tile_rows = [(lax.broadcasted_iota(jnp.int32, (16, BLOCK), 0) + 16 * n).astype(F32).astype(BF16) for n in range(SHARE // 16)]
    one, none = jnp.ones((16, BLOCK), BF16), jnp.zeros((16, BLOCK), BF16)

    def one_hot(ids):
        share, row = ids >> 6, (ids & (SHARE - 1)).astype(F32)
        tiles = []
        for n in range(N_CTX):
            rows = jnp.where(share == source_of(own, n), row, -1.0)
            rows = jnp.broadcast_to(rows, (16, BLOCK)).astype(BF16)
            tiles += [jnp.where(rows == tile, one, none) for tile in tile_rows]
        return jnp.concatenate(tiles, axis=0)

    def far_lookup(block):
        ids = id_ref[:, pl.ds(pl.multiple_of(block * BLOCK, BLOCK), HALO + BLOCK)]
        return jnp.concatenate([one_hot(ids[:, HALO - tap : HALO - tap + BLOCK]) for tap in range(3)], axis=0)

    def far_features(stream, picks):
        return nn(tapped_ref[stream * BLOCK : (stream + 1) * BLOCK, :], picks)

    for half in range(2):
        begin = pl.multiple_of(own * BLOCK + half * BLOCK, BLOCK)
        raw_ref[:, half * BLOCK : (half + 1) * BLOCK] = nn(table, one_hot(id_ref[:, pl.ds(begin, BLOCK)]))

    def featured(stream):
        rows = slice(stream * BLOCK, (stream + 1) * BLOCK)
        raw = raw_ref[rows, :]
        total = tap_ref[rows, 0:1] * raw[:, HALO:]
        for tap in (1, 2):
            total += tap_ref[rows, tap : tap + 1] * raw[:, HALO - tap : 2 * BLOCK - tap]
        return total

    rate_row = row_ref[0:1]
    gain_row = row_ref[1:2]
    block_decay = jnp.exp(rate_row * -float(BLOCK))
    same_group = (
        lax.broadcasted_iota(jnp.int32, (BLOCK, BLOCK), 0) // GROUP == lanes_of((BLOCK, BLOCK)) // ORDER
    )

    def earlier(block, state):
        picks = far_lookup(block)
        mixed = far_features(1, picks) * far_features(2, picks)
        return block_decay * state + nt(mixed.astype(BF16), side_ref[:, END])

    def later(step, state):
        block = N_CTX - 1 - step
        grad = grad_ref[block, 0:BLOCK, :].astype(F32) * far_features(0, far_lookup(block))
        return block_decay * state + nt(grad.astype(BF16), side_ref[:, BEGIN])

    zero = jnp.zeros((BLOCK, BLOCK), F32)
    before = lax.fori_loop(0, own, earlier, zero)
    after = lax.fori_loop(0, N_CTX - 1 - own, later, zero)

    wide = BLOCK + HALO
    query, key, value = featured(0), featured(1), featured(2)
    mixed = key * value
    following = jnp.minimum(own + 1, N_CTX - 1)
    grad_rows = jnp.concatenate(
        [grad_ref[own, 0:BLOCK, :], grad_ref[following, 0:BLOCK, 0:HALO]], axis=1
    ).astype(F32)
    grad_long = grad_rows * query
    mixed_own = mixed[:, :BLOCK].astype(BF16)
    long_own = grad_long[:, :BLOCK].astype(BF16)

    through = block_decay * before + nt(mixed_own, side_ref[:, END])
    before = jnp.where(same_group, before, 0.0).astype(BF16)
    through = jnp.where(same_group, through, 0.0).astype(BF16)
    after = jnp.where(same_group, after, 0.0).astype(BF16)

    copies[N_CTX + 1].wait()
    conv_rows, mixed_grads = [], []
    for g in range(GROUPS):
        rows = slice(g * GROUP, (g + 1) * GROUP)
        conv_rows.append(nn(mixed_own[rows], fwd_ref[g]))
        mixed_grads.append(nt(long_own[rows], fwd_ref[g]))
    conv = jnp.concatenate(conv_rows, axis=0) + nn(before, side_ref[:, ENTER])
    mixed_grad = jnp.concatenate(mixed_grads, axis=0) + nn(after, side_ref[:, LEAVE.start : LEAVE.start + BLOCK])

    def filter_at(lag):
        terms = jnp.where(same_group, gain_row * jnp.exp(rate_row * -float(lag)), 0.0)
        return jnp.sum(terms, axis=1, keepdims=True)

    second = lanes_of((BLOCK, HALO)) == 1
    conv_next = nn(through, side_ref[:, ENTER.start : ENTER.start + HALO]) + filter_at(0) * mixed[:, BLOCK:]
    conv_next += jnp.where(second, filter_at(1) * mixed[:, BLOCK - 1 : wide - 1], 0.0)
    grad_next = nn(after, side_ref[:, LEAVE.start + BLOCK :])
    grad_next -= jnp.where(second, filter_at(-1) * grad_long[:, BLOCK - 1 : wide - 1], 0.0)

    out_ref[...] = (query[:, :BLOCK] * conv).T.astype(BF16)

    conv = jnp.concatenate([conv, conv_next], axis=1)
    mixed_grad = jnp.concatenate([mixed_grad, grad_next], axis=1)
    lane = lanes_of((BLOCK, wide))
    inside = (lane < BLOCK) | ((lane < BLOCK + 2) & (own < N_CTX - 1))
    streams = (grad_rows * conv, mixed_grad * value, mixed_grad * key)
    for s in range(3):
        rows = slice(s * BLOCK, (s + 1) * BLOCK)
        grads = jnp.where(inside, streams[s], 0.0).astype(BF16).astype(F32)
        total = tap_ref[rows, 0:1] * grads[:, :BLOCK]
        for tap in (1, 2):
            total += tap_ref[rows, tap : tap + 1] * grads[:, tap : tap + BLOCK]
        grad_proj_ref[rows, :] = total.astype(BF16)
    for copy in copies[N_CTX + 2 :]:
        copy.wait()
    back_step(0, 0, weight_ref, grad_proj_ref, own_ref, other_ref)


def mix(pieces, grads, tables, weight):
    fwd, side, row, taps = tables
    vmem = pl.BlockSpec(memory_space=pltpu.VMEM)
    return pl.pallas_call(
        mixer_kernel,
        out_shape=(
            jax.ShapeDtypeStruct((BLOCK, BLOCK), BF16),
            jax.ShapeDtypeStruct((3 * BLOCK, BLOCK), BF16),
            jax.ShapeDtypeStruct((1, 2, BLOCK, BLOCK), BF16),
            jax.ShapeDtypeStruct((1, 2, BLOCK, BLOCK), BF16),
            jax.ShapeDtypeStruct((len(NEAR_STEPS), 3, 2, 2, BLOCK, BLOCK), BF16),
        ),
        in_specs=[vmem] * N_CTX + [pl.BlockSpec(memory_space=pl.ANY)] * 7 + [vmem] * 2,
        out_specs=(vmem,) * 5,
        scratch_shapes=[
            pltpu.VMEM((3 * BLOCK, 2 * BLOCK), F32),
            pltpu.VMEM((3 * BLOCK, 3 * VOCAB), BF16),
            pltpu.VMEM((1, WINDOW + 2 * HALO), jnp.int32),
            pltpu.VMEM((N_CTX, BLOCK + EXTRA, BLOCK), BF16),
            pltpu.VMEM((BLOCK, SIDE), BF16),
            pltpu.VMEM((GROUPS, BLOCK, BLOCK), BF16),
            pltpu.VMEM((1, 3, 2, 2, BLOCK, BLOCK), BF16),
            pltpu.SemaphoreType.DMA((N_CTX + 3 + len(NEAR_STEPS),)),
        ],
        compiler_params=pltpu.CompilerParams(vmem_limit_bytes=30 << 20),
        cost_estimate=pl.CostEstimate(flops=3 << 30, bytes_accessed=8 << 20, transcendentals=1 << 16),
        name="mixer",
    )(*pieces, *grads, side, fwd, weight, row, taps)


def back_kernel(begin, grad_ref, held_ref, own_ref, other_ref):
    def one_step(n, carried):
        back_step(n, begin + n, held_ref, grad_ref, own_ref, other_ref)
        return carried

    lax.fori_loop(0, own_ref.shape[0], one_step, 0)


def back_project(grad_proj, held, begin, count):
    vmem = pl.BlockSpec(memory_space=pltpu.VMEM)
    part = jax.ShapeDtypeStruct((count, 2, BLOCK, BLOCK), BF16)
    return pl.pallas_call(
        functools.partial(back_kernel, begin),
        out_shape=(part, part),
        in_specs=[vmem] * 2,
        out_specs=(vmem,) * 2,
        compiler_params=pltpu.CompilerParams(vmem_limit_bytes=4 << 20),
        cost_estimate=pl.CostEstimate(
            flops=2 * 256 * 768 * 1024 * count, bytes_accessed=count << 21, transcendentals=0
        ),
        name="back_project",
    )(grad_proj, held)


def project_features(rows, weight, pair):
    held = lax.all_to_all(
        jnp.broadcast_to(rows[None], (N_Z,) + rows.shape), "chan", 0, 0, axis_index_groups=Z_GROUPS
    )
    beside = lax.ppermute(held, "chan", X_SWAP)
    across = lax.ppermute(held, "chan", CORE_SWAP)
    held, pair = lax.optimization_barrier((held, pair))
    grads = gather_pairs(pair)
    sums, weight_across, weight_beside, weight_both = project(0, held, weight, ahead=(2, 1, 3))
    (sums,) = project(2, across, weight_across, sums, ready=True)
    beside, sums = lax.optimization_barrier((beside, sums))
    both = lax.ppermute(beside, "chan", CORE_SWAP)
    (sums,) = project(1, beside, weight_beside, sums, ready=True)
    both, sums, grads = lax.optimization_barrier((both, sums, grads))
    (part,) = project(3, both, weight_both, sums, ready=True, last=True)
    return part, grads


def gather_ctx(value):
    shift = lambda piece, by: lax.ppermute(piece, "ctx", y_shift(by))
    across = lax.ppermute(value, "ctx", X_HALF_SWAP)
    above = shift(value, -1)
    return [value, across, shift(value, 1), shift(across, 1), above, shift(across, -1), shift(above, -1), shift(across, 2)]


def pair_ctx(value):
    return jnp.stack([value, lax.ppermute(value, "ctx", X_HALF_SWAP)])


def gather_pairs(pair):
    below, above = (lax.ppermute(pair, "ctx", y_shift(by)) for by in (1, -1))
    far = [lax.ppermute(below[0], "ctx", y_shift(1)), lax.ppermute(above[1], "ctx", y_shift(-1))]
    return [pair, below, above, jnp.stack(far)]


def moved(value, by):
    return lax.ppermute(value.astype(BF16), "chan", z_shift(by))


def reduce_chan(far_parts, grad_proj, held):
    terms = {}

    def swap(parts):
        return parts[0], lax.ppermute(parts[1], "chan", CORE_SWAP)

    def add_terms(steps, own, swapped):
        for n, step in enumerate(steps):
            for half in range(2):
                terms[step, half] = own[n, half].astype(F32) + swapped[n, half].astype(F32)

    def arrive(values, tied):
        values, tied = lax.optimization_barrier((values, tied))
        return values, tied

    def send(values):
        return {(half, by): moved(value, by) for (half, by), value in values.items()}

    own, swapped = swap(far_parts)
    near = back_project(grad_proj, held, 0, 2)
    (swapped, near) = lax.optimization_barrier((swapped, near))
    add_terms((4,), own, swapped)
    ways = {1: (1, -1), 0: (-1, 1)}
    chain = send({(half, ways[half][0]): terms[4, half] for half in (1, 0)})
    grad_proj, near = lax.optimization_barrier((grad_proj, near))
    near_own, near_swapped = swap(near)
    middle = back_project(grad_proj, held, 2, 2)
    arrived, middle = arrive(chain, middle)
    add_terms((3, 5), near_own, near_swapped)
    middle_own, middle_swapped = swap(middle)
    chain = {}
    for half in (1, 0):
        long, short = ways[half]
        chain[half, long] = terms[(3 * long) % 8, half] + arrived[half, long].astype(F32)
        chain[half, short] = terms[(3 * short) % 8, half]
    chain = send(chain)
    grad_proj, middle_own = lax.optimization_barrier((grad_proj, middle_own))
    last = back_project(grad_proj, held, 4, 3)
    arrived, last = arrive(chain, last)
    add_terms((2, 6), middle_own, middle_swapped)
    last_own, last_swapped = swap(last)
    chain = send({(half, by): value.astype(F32) + terms[(2 * by) % 8, half] for (half, by), value in arrived.items()})
    add_terms((1, 7, 0), last_own, last_swapped)
    chain = send({(half, by): value.astype(F32) + terms[by % 8, half] for (half, by), value in chain.items()})
    far_half, near_half = (
        terms[0, half] + chain[half, 1].astype(F32) + chain[half, -1].astype(F32) for half in (1, 0)
    )
    total = near_half + lax.ppermute(far_half.astype(BF16), "chan", X_SWAP).astype(F32)
    return total.astype(BF16)


def body(token_ids, embed_table, in_weight, feat_taps, modal_rates, modal_residues, out_grad):
    weight = in_weight.transpose(1, 0, 2).reshape(3, 2, N_Z, 2, BLOCK, BLOCK)
    own_vocab = lax.dynamic_slice_in_dim(embed_table, lax.axis_index("ctx") * SHARE, SHARE, 0)
    pair = pair_ctx(make_payload(out_grad, token_ids))
    part, grads = project_features(own_vocab, weight, pair)
    modal_rates, part = lax.optimization_barrier((modal_rates, part))
    pieces = gather_ctx(part)
    gains = modal_residues * jnp.sqrt(-jnp.expm1(-2.0 * modal_rates))
    tables = make_tables(modal_rates, gains, feat_taps)
    output, grad_proj, own, other, held = mix(pieces, grads, tables, weight)
    return (output, reduce_chan((own, other), grad_proj, held).T)


def solution(mesh):
    in_specs = (
        P("ctx"),
        P(None, "chan"),
        P(None, None, "chan"),
        P(None, None, "chan"),
        P(None, "chan"),
        P(None, "chan"),
        P("ctx", "chan"),
    )
    out_specs = (P("ctx", "chan"), P("ctx", "chan"))
    return jax.shard_map(body, mesh=mesh, in_specs=in_specs, out_specs=out_specs, check_vma=False)
```
